128 devices in a mesh: seq: 4 (over z), expert: 32 (over y, x, core).
Axes of the slice: x: 4, y: 4, z: 4, core: 2. Of those that a mesh axis runs over, the one named last changes fastest.
Arguments:
- tokens: bfloat16 [2, 4096, 1280], P(None, 'seq'), may hold values from -46.205783 to 46.205783
- slot_embed: bfloat16 [1280, 1024], P(None, 'expert'), may hold values from -0.14115179 to 0.14115179
- combine: bfloat16 [2, 4096, 1024], P(None, 'seq', 'expert'), may hold values from 0.00024414062 to 0.00390625
- w_in: bfloat16 [32, 1280, 5120], P('expert', None, 'seq'), may hold values from -0.15625 to 0.15625
- w_out: bfloat16 [32, 5120, 1280], P('expert', 'seq'), may hold values from -0.078125 to 0.078125
- grad_out: bfloat16 [2, 4096, 1280], P(None, 'seq'), may hold values from -6 to 6
Outputs:
- grad_tokens: bfloat16 [2, 4096, 1280], P(None, ('seq', 'expert'))
- grad_embed: bfloat16 [1280, 1024], P('seq', 'expert')
- grad_w_in: bfloat16 [32, 1280, 5120], P('expert', None, 'seq')
- grad_w_out: bfloat16 [32, 5120, 1280], P('expert', 'seq')
The draws below stay inside these ranges and needn't reach their ends.
All inputs are finite; a program needn't handle non-finite values.
Results may differ from the reference program's by a relative error of at most 0.028.
Values may be sent and summed in bfloat16 or wider, within the bound.
No kernel may reach another device: no remote copies, remote signals or barrier semaphores. Data moves between devices by JAX's collectives and lax.ppermute only.
A program may use at most 128 MiB of HBM per device.

```python
import math
import jax
import jax.numpy as jnp
from jax import lax

D = 1280
HID = 5120
SLOTS = 32
IMAGES = 2
LEN = 4096
EXPERTS = 32


def shared_embed(key):
    normal_part = jax.random.normal(jax.random.fold_in(key, 11), (D, EXPERTS * SLOTS), jnp.float32)
    return jnp.clip(normal_part, -5.0, 5.0) * D ** (-0.5)


def draw_slot_embed(key, part):
    return shared_embed(key).astype(jnp.bfloat16)


def position_ramp(start, ratio):
    position = jnp.arange(LEN, dtype=jnp.float32) / float(max(LEN - 1, 1))
    return (start * jnp.exp(math.log(ratio) * position))[None, :, None]


def draw_tokens(key, part):
    noise_key = jax.random.fold_in(key, 12)
    background = jax.random.normal(noise_key, (IMAGES, LEN, D), jnp.float32)
    background = jnp.clip(background, -6.0, 6.0) * position_ramp(0.8, 2.25)
    return background.astype(jnp.bfloat16)


def block_scale(stream_key, shape, cuts, low, largest):
    gain, own = 1.0, jax.random.fold_in(stream_key, 6)
    for dim, blocks in cuts:
        steps = jnp.exp(jax.random.uniform(jax.random.fold_in(own, dim), (blocks,), jnp.float32, low / len(cuts), largest / len(cuts)))
        gain = gain * jnp.repeat(steps, shape[dim] // blocks).reshape([-1 if axis == dim else 1 for axis in range(len(shape))])
    return gain


def noise(rng, extent, spread, most, split=(), kind=jnp.bfloat16):
    result = spread * jax.random.normal(rng, extent, jnp.float32)
    if split:
        result = result * block_scale(rng, extent, split, -0.22, 0.18)
    return jnp.clip(result, -most, most).astype(kind)


def setup_inputs(seed: int = 0) -> dict:
    key_of = jax.random.split(jax.random.key(seed), 7)
    tokens = draw_tokens(jax.random.fold_in(key_of[6], 71), 0)
    slot_embed = draw_slot_embed(jax.random.fold_in(key_of[6], 71), 0)
    combine = jnp.clip(jnp.exp(math.log(0.00390625) - 2.7725887 * jax.random.uniform(key_of[2], (IMAGES, LEN, EXPERTS * SLOTS), jnp.float32) ** block_scale(key_of[2], (IMAGES, LEN, EXPERTS * SLOTS), ((1, 4), (2, 32)), -0.2, 0.2)), 0.00024414062, 0.00390625).astype(jnp.bfloat16)
    w_in = noise(key_of[3], (EXPERTS, D, HID), D ** -0.5, 0.15625, ((0, 32), (2, 4)))
    w_out = noise(key_of[4], (EXPERTS, HID, D), HID ** -0.5, 0.078125, ((0, 32), (1, 4)))
    grad_out = noise(key_of[5], (IMAGES, LEN, D), 1.0, 6.0, ((1, 4),))
    return {"tokens": tokens, "slot_embed": slot_embed, "combine": combine, "w_in": w_in, "w_out": w_out, "grad_out": grad_out}


def gelu_exact(values):
    return 0.5 * values * (1.0 + jax.scipy.special.erf(values / math.sqrt(2.0)))

def gelu_slope(values):
    return 0.5 * (1.0 + jax.scipy.special.erf(values / math.sqrt(2.0))) + values * jnp.exp(-0.5 * values * values) / math.sqrt(2.0 * math.pi)

def reference(tokens, slot_embed, combine, w_in, w_out, grad_out):
    tokens_full = tokens.astype(jnp.float32)
    embed_full = slot_embed.astype(jnp.float32)
    combine_full = combine.astype(jnp.float32)
    grad_full = grad_out.astype(jnp.float32)
    w_in_full = w_in.astype(jnp.float32)
    w_out_full = w_out.astype(jnp.float32)
    logits = jnp.einsum('itd,dj->itj', tokens_full, embed_full)
    col_peak = lax.optimization_barrier(jnp.max(logits, axis=1, keepdims=True))
    exponent = jnp.exp(logits - col_peak)
    dispatch = (exponent / lax.optimization_barrier(jnp.sum(exponent, axis=1, keepdims=True))).astype(jnp.bfloat16)
    dispatch_full = dispatch.astype(jnp.float32)
    slot_in = jnp.einsum('itj,itd->ijd', dispatch_full, tokens_full).astype(jnp.bfloat16)
    slot_in = slot_in.reshape(IMAGES, EXPERTS, SLOTS, D).astype(jnp.float32)
    pre_act = jnp.einsum('iesd,edh->iesh', slot_in, w_in_full)
    act_value = gelu_exact(pre_act).astype(jnp.bfloat16).astype(jnp.float32)
    slot_out = jnp.einsum('iesh,ehd->iesd', act_value, w_out_full).astype(jnp.bfloat16)
    slot_out = slot_out.reshape(IMAGES, EXPERTS * SLOTS, D).astype(jnp.float32)
    grad_combine = jnp.einsum('itd,ijd->itj', grad_full, slot_out)
    row_dot = lax.optimization_barrier(jnp.sum(combine_full * grad_combine, axis=2, keepdims=True))
    grad_slot_out = jnp.einsum('itj,itd->ijd', combine_full, grad_full).astype(jnp.bfloat16)
    grad_slot_out = grad_slot_out.reshape(IMAGES, EXPERTS, SLOTS, D).astype(jnp.float32)
    grad_act = jnp.einsum('iesd,ehd->iesh', grad_slot_out, w_out_full)
    grad_pre = (grad_act * gelu_slope(pre_act)).astype(jnp.bfloat16).astype(jnp.float32)
    grad_w_out = jnp.einsum('iesh,iesd->ehd', act_value, grad_slot_out).astype(jnp.bfloat16)
    grad_w_in = jnp.einsum('iesd,iesh->edh', slot_in, grad_pre).astype(jnp.bfloat16)
    grad_slot_in = jnp.einsum('iesh,edh->iesd', grad_pre, w_in_full).astype(jnp.bfloat16)
    grad_slot_in = grad_slot_in.reshape(IMAGES, EXPERTS * SLOTS, D).astype(jnp.float32)
    grad_dispatch = jnp.einsum('itd,ijd->itj', tokens_full, grad_slot_in)
    col_dot = lax.optimization_barrier(jnp.sum(dispatch_full * grad_dispatch, axis=1, keepdims=True))
    grad_logits = (dispatch_full * (grad_dispatch - col_dot) + combine_full * (grad_combine - row_dot)).astype(jnp.bfloat16)
    logits_full = grad_logits.astype(jnp.float32)
    grad_embed = jnp.einsum('itd,itj->dj', tokens_full, logits_full).astype(jnp.bfloat16)
    grad_tokens = jnp.einsum('itj,ijd->itd', dispatch_full, grad_slot_in) + jnp.einsum('itj,dj->itd', logits_full, embed_full)
    return (grad_tokens.astype(jnp.bfloat16), grad_embed, grad_w_in, grad_w_out)
```

```python
import math

import jax
import jax.numpy as jnp
from jax import lax
from jax.sharding import Mesh, PartitionSpec as P

F32 = jnp.float32
BF16 = jnp.bfloat16


def gelu_parts(values):
    cdf = 0.5 * (1.0 + jax.scipy.special.erf(values / math.sqrt(2.0)))
    slope = cdf + values * jnp.exp(-0.5 * values * values) / math.sqrt(2.0 * math.pi)
    return values * cdf, slope


def shift(value, axis, by):
    return lax.ppermute(value, axis, [(i, (i + by) % 4) for i in range(4)])


def swap_cores(value):
    return lax.ppermute(value, "core", [(0, 1), (1, 0)])


def rolled(value, index, size, dim):
    twice = jnp.concatenate([value, value], axis=dim)
    return lax.dynamic_slice_in_dim(twice, index * size, value.shape[dim], axis=dim)


def scatter_terms(blocks, axis):
    return [blocks[0]] + [shift(blocks[k], axis, k) for k in (1, 2, 3)]


def gather_blocks(block, axis):
    return [block] + [shift(block, axis, -k) for k in (1, 2, 3)]


def local(tokens, slot_embed, combine, w_in, w_out, grad_out):
    z = lax.axis_index("seq")
    w_in, w_out = w_in[0], w_out[0]
    embed = rolled(slot_embed.T, z, 8, 0)
    comb = rolled(jnp.transpose(combine, (0, 2, 1)), z, 8, 1)

    logits = jnp.einsum("jd,itd->ijt", embed, tokens, preferred_element_type=F32)
    peak = jnp.max(logits, axis=2, keepdims=True)
    weight = jnp.exp(logits - peak)
    total = jnp.sum(weight, axis=2, keepdims=True)
    lse = peak + jnp.log(total)
    slot_part = jnp.einsum("ijt,itd->ijd", weight.astype(BF16), tokens, preferred_element_type=F32)
    slot_part = (slot_part / total).astype(BF16).reshape(2, 4, 8, 1280)
    out_part = jnp.einsum("ijt,itd->ijd", comb, grad_out, preferred_element_type=F32)
    out_part = out_part.astype(BF16).reshape(2, 4, 8, 1280)
    lses = [lse] + [
        jnp.roll(shift(lse, "seq", k), -8 * k, axis=1) for k in (1, 2, 3)
    ]
    top = jnp.maximum(jnp.maximum(lses[0], lses[1]), jnp.maximum(lses[2], lses[3]))
    lse_all = top + jnp.log(sum(jnp.exp(one - top) for one in lses))
    terms = scatter_terms(
        [jnp.stack([slot_part[:, k], out_part[:, k]]) for k in range(4)], "seq"
    )
    slot_own = sum(
        jnp.exp(lses[k] - lse_all)[:, :8] * terms[k][0].astype(F32) for k in range(4)
    )
    out_own = sum(terms[k][1].astype(F32) for k in range(4))
    both = gather_blocks(jnp.stack([slot_own, out_own]).astype(BF16), "seq")
    both = jnp.stack(both)
    slot_in = both[:, 0].reshape(64, 1280)
    grad_slot_out = both[:, 1].reshape(64, 1280)

    pre_act = jnp.dot(slot_in, w_in, preferred_element_type=F32)
    act, slope = gelu_parts(pre_act)
    act = act.astype(BF16)
    out_sum = jnp.dot(act, w_out, preferred_element_type=F32).astype(BF16)
    grad_act = jnp.einsum("sd,hd->sh", grad_slot_out, w_out, preferred_element_type=F32)
    grad_pre = (grad_act * slope).astype(BF16)
    in_sum = jnp.einsum("sh,dh->sd", grad_pre, w_in, preferred_element_type=F32).astype(BF16)
    pair = jnp.stack([out_sum.reshape(4, 16, 1280), in_sum.reshape(4, 16, 1280)], axis=1)
    terms = scatter_terms([pair[k] for k in range(4)], "seq")
    own = sum(term.astype(F32) for term in terms).astype(BF16)
    pair = jnp.stack(gather_blocks(own, "seq"))
    pair = pair.reshape(4, 2, 2, 8, 1280).transpose(1, 2, 0, 3, 4).reshape(2, 2, 32, 1280)
    slot_out, grad_slot_in = pair[0], pair[1]
    slot_in_f = slot_in.reshape(4, 2, 8, 1280).transpose(1, 0, 2, 3).reshape(2, 32, 1280)

    grad_w_out = jnp.einsum("sh,sd->hd", act, grad_slot_out, preferred_element_type=F32)
    grad_w_in = jnp.einsum("sd,sh->dh", slot_in, grad_pre, preferred_element_type=F32)

    grad_combine = jnp.einsum("ijd,itd->ijt", slot_out, grad_out, preferred_element_type=F32)
    comb_f = comb.astype(F32)
    row_dot = jnp.sum(comb_f * grad_combine, axis=1)
    row_dot = row_dot + swap_cores(row_dot)
    for axis in ("x", "y"):
        row_dot = sum(scatter_terms([row_dot] * 4, axis))
    grad_dispatch = jnp.einsum("ijd,itd->ijt", grad_slot_in, tokens, preferred_element_type=F32)
    col_dot = jnp.sum(
        slot_in_f.astype(F32) * grad_slot_in.astype(F32), axis=2, keepdims=True
    )
    dispatch = jnp.exp(logits - lse_all)
    grad_logits = (
        dispatch * (grad_dispatch - col_dot) + comb_f * (grad_combine - row_dot[:, None, :])
    ).astype(BF16)
    dispatch = dispatch.astype(BF16)

    embed_part = jnp.einsum("ijt,itd->jd", grad_logits, tokens, preferred_element_type=F32)
    embed_part = rolled(embed_part.astype(BF16), (4 - z) % 4, 8, 0)
    embed_part = rolled(embed_part.reshape(32, 4, 320).transpose(1, 0, 2), z, 1, 0)
    terms = scatter_terms([embed_part[k] for k in range(4)], "seq")
    grad_embed = sum(term.astype(F32) for term in terms).astype(BF16).T

    y, x, core = lax.axis_index("y"), lax.axis_index("x"), lax.axis_index("core")
    rows = jnp.concatenate([grad_slot_in.reshape(64, 1280), embed])
    rows = jnp.stack(gather_blocks(rows, "y"))
    weights = jnp.stack([dispatch, grad_logits], axis=1).reshape(2, 2, 32, 4, 256)
    weights = rolled(weights.transpose(3, 0, 1, 2, 4), y, 1, 0)
    weights = scatter_terms([weights[k] for k in range(4)], "y")
    weights = jnp.stack([weights[0], weights[3], weights[2], weights[1]])
    slots = jnp.stack(
        [
            jnp.stack([rows[:, 32 * i : 32 * i + 32], rows[:, 64:96]], axis=1)
            for i in range(2)
        ],
        axis=1,
    )
    part = jnp.einsum("kicjt,kicjd->itd", weights, slots, preferred_element_type=F32)
    part = part.astype(BF16).reshape(2, 4, 2, 32, 1280)
    part = part.transpose(2, 1, 0, 3, 4)
    mine = lax.dynamic_index_in_dim(part, core, 0, keepdims=False)
    other = lax.dynamic_index_in_dim(part, 1 - core, 0, keepdims=False)
    part = (mine.astype(F32) + swap_cores(other).astype(F32)).astype(BF16)
    part = rolled(part, x, 1, 0)
    terms = scatter_terms([part[k] for k in range(4)], "x")
    grad_tokens = sum(term.astype(F32) for term in terms).astype(BF16)
    return (
        grad_tokens,
        grad_embed,
        grad_w_in.astype(BF16)[None],
        grad_w_out.astype(BF16)[None],
    )


def solution(mesh):
    fine = Mesh(mesh.devices.reshape(4, 4, 4, 2), ("seq", "y", "x", "core"))
    expert = ("y", "x", "core")
    return jax.shard_map(
        local,
        mesh=fine,
        in_specs=(
            P(None, "seq", None),
            P(None, expert),
            P(None, "seq", expert),
            P(expert, None, "seq"),
            P(expert, "seq", None),
            P(None, "seq", None),
        ),
        out_specs=(
            P(None, ("seq", *expert), None),
            P("seq", expert),
            P(expert, None, "seq"),
            P(expert, "seq", None),
        ),
        check_vma=False,
    )
```

```python
import math

import jax
import jax.numpy as jnp
from jax import lax
from jax.experimental import pallas as pl
from jax.experimental.pallas import tpu as pltpu
from jax.sharding import Mesh, PartitionSpec as P

F32 = jnp.float32
BF16 = jnp.bfloat16
NT = (((1,), (1,)), ((), ()))
TN = (((0,), (0,)), ((), ()))
PARAMS = pltpu.CompilerParams(vmem_limit_bytes=24 * 1024 * 1024)


def shape(dims, dtype):
    return jax.ShapeDtypeStruct(dims, dtype)


def gelu_parts(values):
    cdf = 0.5 * (1.0 + jax.scipy.special.erf(values / math.sqrt(2.0)))
    slope = cdf + values * jnp.exp(-0.5 * values * values) / math.sqrt(2.0 * math.pi)
    return values * cdf, slope


def shift(value, axis, by):
    return lax.ppermute(value, axis, [(i, (i + by) % 4) for i in range(4)])


def swap_cores(value):
    return lax.ppermute(value, "core", [(0, 1), (1, 0)])


def near(value):
    return lax.ppermute(value, "seq", [(0, 1), (1, 0), (2, 3), (3, 2)])


def far(value):
    return lax.ppermute(value, "seq", [(0, 3), (3, 0), (1, 2), (2, 1)])


def add(one, two):
    return (one.astype(F32) + two.astype(F32)).astype(BF16)


def merge(part_a, lse_a, part_b, lse_b):
    top = jnp.maximum(lse_a, lse_b)
    weight_a, weight_b = jnp.exp(lse_a - top), jnp.exp(lse_b - top)
    total = weight_a + weight_b
    share_a, share_b = (weight_a / total)[:, :1], (weight_b / total)[:, :1]
    part = share_a * part_a.astype(F32) + share_b * part_b.astype(F32)
    return part.astype(BF16), top + jnp.log(total)


def scatter_terms(blocks, axis):
    return [blocks[0]] + [shift(blocks[k], axis, k) for k in (1, 2, 3)]


def gather_blocks(block, axis):
    return [block] + [shift(block, axis, -k) for k in (1, 2, 3)]


def chunk(axis, k, size):
    return pl.multiple_of(((lax.axis_index(axis) + k) & 3) * size, size)


def softmax_kernel(tok, embed, logits, part, lse):
    patches = tok[0]
    scores = lax.dot_general(patches, embed[...], NT, preferred_element_type=F32).T
    peak = jnp.max(scores, axis=1, keepdims=True)
    weight = jnp.exp(scores - peak)
    total = jnp.sum(weight, axis=1, keepdims=True)
    sums = jnp.dot(weight.astype(BF16), patches, preferred_element_type=F32)
    logits[...] = scores
    part[...] = (sums / total).astype(BF16)
    lse[...] = jnp.broadcast_to(peak + jnp.log(total), lse.shape)


def local_softmax(tokens, embed):
    return pl.pallas_call(
        softmax_kernel,
        grid=(2,),
        in_specs=[
            pl.BlockSpec((1, 1024, 1280), lambda i: (i, 0, 0)),
            pl.BlockSpec((32, 1280), lambda i: (0, 0)),
        ],
        out_specs=[
            pl.BlockSpec((32, 1024), lambda i: (i, 0)),
            pl.BlockSpec((32, 1280), lambda i: (i, 0)),
            pl.BlockSpec((32, 128), lambda i: (i, 0)),
        ],
        out_shape=[shape((64, 1024), F32), shape((64, 1280), BF16), shape((64, 128), F32)],
        cost_estimate=pl.CostEstimate(flops=700_000_000, bytes_accessed=6_000_000, transcendentals=65536),
        compiler_params=PARAMS,
        name="local_softmax",
    )(tokens, embed)


def combine_grad_kernel(gout, sum_a, sum_b, comb, grad, row):
    slot_out = add(sum_a[...], sum_b[...])
    value = lax.dot_general(gout[0], slot_out, NT, preferred_element_type=F32).T
    grad[...] = value
    row[0] = jnp.sum(comb[...].astype(F32) * value, axis=0, keepdims=True)


def combine_grad(grad_out, sum_a, sum_b, comb):
    return pl.pallas_call(
        combine_grad_kernel,
        grid=(2,),
        in_specs=[
            pl.BlockSpec((1, 1024, 1280), lambda i: (i, 0, 0)),
            pl.BlockSpec((32, 1280), lambda i: (i, 0)),
            pl.BlockSpec((32, 1280), lambda i: (i, 0)),
            pl.BlockSpec((32, 1024), lambda i: (i, 0)),
        ],
        out_specs=[
            pl.BlockSpec((32, 1024), lambda i: (i, 0)),
            pl.BlockSpec((1, 1, 1024), lambda i: (i, 0, 0)),
        ],
        out_shape=[shape((64, 1024), F32), shape((2, 1, 1024), F32)],
        cost_estimate=pl.CostEstimate(flops=350_000_000, bytes_accessed=6_000_000, transcendentals=0),
        compiler_params=PARAMS,
        name="combine_grad",
    )(grad_out, sum_a, sum_b, comb)


def dispatch_grad_kernel(tok, gslot, slot_in, logits, lse, comb, gcomb, full, c0, c1, c2, c3):
    rows = gslot[...]
    col_dot = jnp.sum(slot_in[...].astype(F32) * rows.astype(F32), axis=1, keepdims=True)
    grad = lax.dot_general(tok[0], rows, NT, preferred_element_type=F32).T
    weight = jnp.exp(logits[...] - lse[:, :1])
    full[...] = weight * (grad - col_dot) + comb[...].astype(F32) * gcomb[...]
    for k, out in enumerate((c0, c1, c2, c3)):
        out[...] = full[:, pl.ds(chunk("y", k, 256), 256)].astype(BF16)


def dispatch_grad(tokens, gslot, slot_in, logits, lse, comb, gcomb):
    rows = pl.BlockSpec((32, 1280), lambda i: (i, 0))
    wide = pl.BlockSpec((32, 1024), lambda i: (i, 0))
    part = pl.BlockSpec((32, 256), lambda i: (i, 0))
    return pl.pallas_call(
        dispatch_grad_kernel,
        grid=(2,),
        in_specs=[
            pl.BlockSpec((1, 1024, 1280), lambda i: (i, 0, 0)),
            rows,
            rows,
            wide,
            pl.BlockSpec((32, 128), lambda i: (i, 0)),
            wide,
            wide,
        ],
        out_specs=[wide] + [part] * 4,
        out_shape=[shape((64, 1024), F32)] + [shape((64, 256), BF16)] * 4,
        cost_estimate=pl.CostEstimate(flops=350_000_000, bytes_accessed=7_000_000, transcendentals=65536),
        compiler_params=PARAMS,
        name="dispatch_grad",
    )(tokens, gslot, slot_in, logits, lse, comb, gcomb)


def weights_kernel(logits, lse, o0, o1, o2, o3):
    for k, out in enumerate((o0, o1, o2, o3)):
        piece = logits[:, pl.ds(chunk("y", k, 256), 256)]
        out[...] = jnp.exp(piece - lse[:, :1]).astype(BF16)


def dispatch_chunks(logits, lse):
    return pl.pallas_call(
        weights_kernel,
        out_shape=[shape((64, 256), BF16)] * 4,
        cost_estimate=pl.CostEstimate(flops=65536, bytes_accessed=400_000, transcendentals=65536),
        compiler_params=PARAMS,
        name="dispatch_chunks",
    )(logits, lse)


def split_kernel(value, o0, o1, o2, o3):
    for k, out in enumerate((o0, o1, o2, o3)):
        out[...] = value[:, pl.ds(chunk("y", k, 256), 256)]


def y_chunks(value):
    return pl.pallas_call(
        split_kernel,
        out_shape=[shape((64, 256), BF16)] * 4,
        cost_estimate=pl.CostEstimate(flops=0, bytes_accessed=262_144, transcendentals=0),
        compiler_params=PARAMS,
        name="y_chunks",
    )(value)


def rows_kernel(kinds, *refs):
    ins, (m0, m1, m2, m3, other, scratch) = refs[:-6], refs[-6:]
    for i in range(2):
        weights, rows = [], []
        for kind in range(kinds):
            for k in range(4):
                weight, row = ins[8 * kind + k], ins[8 * kind + 4 + k]
                weights.append(weight[32 * i : 32 * i + 32, :])
                rows.append(row[32 * i : 32 * i + 32, :] if row.shape[0] == 64 else row[...])
        scratch[i] = lax.dot_general(
            jnp.concatenate(weights), jnp.concatenate(rows), TN, preferred_element_type=F32
        )
        core = lax.axis_index("core")
        for k, mine in enumerate((m0, m1, m2, m3)):
            base = ((lax.axis_index("x") + k) & 3) * 64
            here = pl.multiple_of(base + core * 32, 32)
            there = pl.multiple_of(base + (1 - core) * 32, 32)
            mine[i] = scratch[i, pl.ds(here, 32), :].astype(BF16)
            other[k, i] = scratch[i, pl.ds(there, 32), :].astype(BF16)


def patch_rows(kinds):
    refs = [one for weights, rows in kinds for one in (*weights, *rows)]
    block = shape((2, 32, 1280), BF16)
    *mine, other = pl.pallas_call(
        lambda *refs: rows_kernel(len(kinds), *refs),
        out_shape=[block] * 4 + [shape((4, 2, 32, 1280), BF16)],
        scratch_shapes=[pltpu.VMEM((2, 256, 1280), F32)],
        cost_estimate=pl.CostEstimate(flops=170_000_000 * len(kinds), bytes_accessed=3_000_000, transcendentals=0),
        compiler_params=PARAMS,
        name="patch_rows",
    )(*refs)
    return mine, other


def add_kernel(m0, m1, m2, m3, other, o0, o1, o2, o3):
    for k, (mine, out) in enumerate(((m0, o0), (m1, o1), (m2, o2), (m3, o3))):
        out[...] = add(mine[...], other[k])


def add_cores(mine, other):
    return pl.pallas_call(
        add_kernel,
        out_shape=[shape((2, 32, 1280), BF16)] * 4,
        cost_estimate=pl.CostEstimate(flops=327_680, bytes_accessed=2_000_000, transcendentals=0),
        compiler_params=PARAMS,
        name="add_cores",
    )(*mine, other)


def reduce_rows(kinds):
    mine, other = patch_rows(kinds)
    return scatter_terms(add_cores(mine, swap_cores(other)), "x")


def sources(terms):
    return [terms[0], terms[3], terms[2], terms[1]]


def local(tokens, slot_embed, combine, w_in, w_out, grad_out):
    w_in, w_out = w_in[0], w_out[0]
    embed = slot_embed.T
    comb = jnp.transpose(combine, (0, 2, 1)).reshape(64, 1024)
    comb_f = comb.astype(F32)

    out_part = jnp.einsum(
        "ijt,itd->ijd", comb.reshape(2, 32, 1024), grad_out, preferred_element_type=F32
    )
    out_part = out_part.astype(BF16).reshape(64, 1280)
    out_part = add(out_part, far(out_part))
    grad_slot_out = add(out_part, near(out_part))

    logits, part, lse = local_softmax(tokens, embed)
    part, lse = merge(part, lse, near(part), near(lse))
    slot_in, lse = merge(part, lse, far(part), far(lse))

    embeds = gather_blocks(embed, "y")
    combs = sources(scatter_terms(y_chunks(comb), "y"))
    v_terms = reduce_rows([(combs, embeds)])

    pre_act = jnp.dot(slot_in, w_in, preferred_element_type=F32)
    act, slope = gelu_parts(pre_act)
    act = act.astype(BF16)
    out_sum = jnp.dot(act, w_out, preferred_element_type=F32).astype(BF16)
    out_sum = add(out_sum, near(out_sum))
    out_other = far(out_sum)
    grad_act = jnp.einsum("sd,hd->sh", grad_slot_out, w_out, preferred_element_type=F32)
    grad_pre = (grad_act * slope).astype(BF16)
    in_sum = jnp.einsum("sh,dh->sd", grad_pre, w_in, preferred_element_type=F32).astype(BF16)
    in_sum = add(in_sum, far(in_sum))
    grad_slot_in = add(in_sum, near(in_sum))
    grad_w_out = jnp.einsum("sh,sd->hd", act, grad_slot_out, preferred_element_type=F32)
    grad_w_in = jnp.einsum("sd,sh->dh", slot_in, grad_pre, preferred_element_type=F32)

    grad_combine, row_dot = combine_grad(grad_out, out_sum, out_other, comb)
    row_dot = row_dot + swap_cores(row_dot)
    for axis in ("x", "y"):
        row_dot = sum(scatter_terms([row_dot] * 4, axis))

    dispatch = sources(scatter_terms(dispatch_chunks(logits, lse), "y"))
    rows = gather_blocks(grad_slot_in, "y")
    partial_logits, *chunks = dispatch_grad(
        tokens, grad_slot_in, slot_in, logits, lse, comb, grad_combine
    )
    chunks = sources(scatter_terms(chunks, "y"))
    u_terms = reduce_rows([(dispatch, rows), (chunks, embeds)])

    grad_logits = partial_logits - comb_f * jnp.repeat(row_dot, 32, axis=1).reshape(64, 1024)
    grad_logits = grad_logits.astype(BF16).reshape(2, 32, 1024)
    embed_part = jnp.einsum("ijt,itd->jd", grad_logits, tokens, preferred_element_type=F32)
    embed_part = embed_part.astype(BF16)
    embed_part = add(embed_part, near(embed_part))
    embed_sum = add(embed_part, far(embed_part))
    z = lax.axis_index("seq")
    grad_embed = lax.dynamic_slice_in_dim(embed_sum, z * 320, 320, axis=1).T

    place = (lax.axis_index("y") * 4 + lax.axis_index("x")) * 2 + lax.axis_index("core")
    own = lax.dynamic_slice_in_dim(row_dot, place * 32, 32, axis=2).reshape(2, 32, 1)
    grad_tokens = sum(term.astype(F32) for term in u_terms) - own * sum(
        term.astype(F32) for term in v_terms
    )
    return (
        grad_tokens.astype(BF16),
        grad_embed,
        grad_w_in.astype(BF16)[None],
        grad_w_out.astype(BF16)[None],
    )


def solution(mesh):
    fine = Mesh(mesh.devices.reshape(4, 4, 4, 2), ("seq", "y", "x", "core"))
    expert = ("y", "x", "core")
    return jax.shard_map(
        local,
        mesh=fine,
        in_specs=(
            P(None, "seq", None),
            P(None, expert),
            P(None, "seq", expert),
            P(expert, None, "seq"),
            P(expert, "seq", None),
            P(None, "seq", None),
        ),
        out_specs=(
            P(None, ("seq", *expert), None),
            P("seq", expert),
            P(expert, None, "seq"),
            P(expert, "seq", None),
        ),
        check_vma=False,
    )
```

```python
import math

import jax
import jax.numpy as jnp
from jax import lax
from jax.experimental import pallas as pl
from jax.experimental.pallas import tpu as pltpu
from jax.sharding import Mesh, PartitionSpec as P

F32 = jnp.float32
BF16 = jnp.bfloat16
NT = (((1,), (1,)), ((), ()))
TN = (((0,), (0,)), ((), ()))
PARAMS = pltpu.CompilerParams(vmem_limit_bytes=24 * 1024 * 1024)


def shape(dims, dtype):
    return jax.ShapeDtypeStruct(dims, dtype)


def gelu_parts(values):
    cdf = 0.5 * (1.0 + jax.scipy.special.erf(values / math.sqrt(2.0)))
    slope = cdf + values * jnp.exp(-0.5 * values * values) / math.sqrt(2.0 * math.pi)
    return values * cdf, slope


def shift(value, axis, by):
    return lax.ppermute(value, axis, [(i, (i + by) % 4) for i in range(4)])


def swap_cores(value):
    return lax.ppermute(value, "core", [(0, 1), (1, 0)])


def near(value):
    return lax.ppermute(value, "seq", [(0, 1), (1, 0), (2, 3), (3, 2)])


def far(value):
    return lax.ppermute(value, "seq", [(0, 3), (3, 0), (1, 2), (2, 1)])


def add(one, two):
    return (one.astype(F32) + two.astype(F32)).astype(BF16)


def scatter_terms(blocks, axis):
    return [blocks[0]] + [shift(blocks[k], axis, k) for k in (1, 2, 3)]


def gather_blocks(block, axis):
    return [block] + [shift(block, axis, -k) for k in (1, 2, 3)]


def chunk(axis, k, size):
    return pl.multiple_of(((lax.axis_index(axis) + k) & 3) * size, size)


def lse_lanes(lse):
    high = lse.astype(BF16).astype(F32)
    middle = (lse - high).astype(BF16).astype(F32)
    low = lse - high - middle
    lane = lax.broadcasted_iota(jnp.int32, (lse.shape[0], 128), 1)
    lanes = jnp.where(lane == 0, high, jnp.where(lane == 1, middle, low))
    return jnp.where(lane < 3, lanes, 0.0).astype(BF16)


def lse_column(lanes):
    lanes = lanes.astype(F32)
    return lanes[:, 0:1] + lanes[:, 1:2] + lanes[:, 2:3]


def softmax_kernel(tok, embed, logits, part, peak, total, sums):
    step = pl.program_id(1)
    patches = tok[0]
    scores = lax.dot_general(patches, embed[...], NT, preferred_element_type=F32).T
    logits[...] = scores

    @pl.when(step == 0)
    def _():
        peak[...] = jnp.full_like(peak, -jnp.inf)
        total[...] = jnp.zeros_like(total)
        sums[...] = jnp.zeros_like(sums)

    top = jnp.maximum(peak[:, :1], jnp.max(scores, axis=1, keepdims=True))
    scale = jnp.exp(peak[:, :1] - top)
    weight = jnp.exp(scores - top)
    new_total = total[:, :1] * scale + jnp.sum(weight, axis=1, keepdims=True)
    new_sums = sums[...] * scale + jnp.dot(
        weight.astype(BF16), patches, preferred_element_type=F32
    )
    peak[...] = jnp.broadcast_to(top, peak.shape)
    total[...] = jnp.broadcast_to(new_total, total.shape)
    sums[...] = new_sums

    @pl.when(step == pl.num_programs(1) - 1)
    def _():
        part[:, :1280] = (new_sums / new_total).astype(BF16)
        part[:, 1280:] = lse_lanes(top + jnp.log(new_total))


def in_hbm(value):
    return pltpu.with_memory_space_constraint(value, pltpu.HBM)


def local_softmax(tokens, embed):
    return pl.pallas_call(
        softmax_kernel,
        grid=(2, 2),
        in_specs=[
            pl.BlockSpec((1, 512, 1280), lambda i, t: (i, t, 0)),
            pl.BlockSpec((32, 1280), lambda i, t: (0, 0)),
        ],
        out_specs=[
            pl.BlockSpec((32, 512), lambda i, t: (i, t)),
            pl.BlockSpec((32, 1408), lambda i, t: (i, 0)),
        ],
        out_shape=[shape((64, 1024), F32), shape((64, 1408), BF16)],
        scratch_shapes=[
            pltpu.VMEM((32, 128), F32),
            pltpu.VMEM((32, 128), F32),
            pltpu.VMEM((32, 1280), F32),
        ],
        cost_estimate=pl.CostEstimate(flops=700_000_000, bytes_accessed=6_000_000, transcendentals=65536),
        compiler_params=PARAMS,
        name="local_softmax",
    )(in_hbm(tokens), embed)


def merge_kernel(one, two, sums, lse):
    lse_a, lse_b = lse_column(one[:, 1280:]), lse_column(two[:, 1280:])
    top = jnp.maximum(lse_a, lse_b)
    weight_a, weight_b = jnp.exp(lse_a - top), jnp.exp(lse_b - top)
    total = weight_a + weight_b
    part = (weight_a / total) * one[:, :1280].astype(F32)
    part = part + (weight_b / total) * two[:, :1280].astype(F32)
    lse_all = top + jnp.log(total)
    sums[:, :1280] = part.astype(BF16)
    if lse is None:
        sums[:, 1280:] = lse_lanes(lse_all)
    else:
        lse[...] = jnp.broadcast_to(lse_all, lse.shape)


def merge_pair(one, two):
    return pl.pallas_call(
        lambda a, b, out: merge_kernel(a, b, out, None),
        out_shape=shape((64, 1408), BF16),
        cost_estimate=pl.CostEstimate(flops=300_000, bytes_accessed=540_000, transcendentals=256),
        compiler_params=PARAMS,
        name="merge_pair",
    )(one, two)


def merge_last(one, two):
    return pl.pallas_call(
        merge_kernel,
        out_shape=[shape((64, 1280), BF16), shape((64, 128), F32)],
        cost_estimate=pl.CostEstimate(flops=300_000, bytes_accessed=540_000, transcendentals=256),
        compiler_params=PARAMS,
        name="merge_last",
    )(one, two)


def combine_grad_kernel(gout, sum_a, sum_b, comb, grad, row):
    slot_out = add(sum_a[...], sum_b[...])
    value = lax.dot_general(gout[0], slot_out, NT, preferred_element_type=F32).T
    grad[...] = value
    row[0] = jnp.sum(comb[...].astype(F32) * value, axis=0, keepdims=True)


def combine_grad(grad_out, sum_a, sum_b, comb):
    return pl.pallas_call(
        combine_grad_kernel,
        grid=(2, 2),
        in_specs=[
            pl.BlockSpec((1, 512, 1280), lambda i, t: (i, t, 0)),
            pl.BlockSpec((32, 1280), lambda i, t: (i, 0)),
            pl.BlockSpec((32, 1280), lambda i, t: (i, 0)),
            pl.BlockSpec((32, 512), lambda i, t: (i, t)),
        ],
        out_specs=[
            pl.BlockSpec((32, 512), lambda i, t: (i, t)),
            pl.BlockSpec((1, 1, 512), lambda i, t: (i, 0, t)),
        ],
        out_shape=[shape((64, 1024), F32), shape((2, 1, 1024), F32)],
        cost_estimate=pl.CostEstimate(flops=350_000_000, bytes_accessed=6_000_000, transcendentals=0),
        compiler_params=PARAMS,
        name="combine_grad",
    )(in_hbm(grad_out), sum_a, sum_b, comb)


def dispatch_grad_kernel(tok, gslot, slot_in, logits, lse, comb, gcomb, full, c0, c1, c2, c3, all_grad, all_weight):
    step = pl.program_id(1)
    rows = gslot[...]
    col_dot = jnp.sum(slot_in[...].astype(F32) * rows.astype(F32), axis=1, keepdims=True)
    grad = lax.dot_general(tok[0], rows, NT, preferred_element_type=F32).T
    weight = jnp.exp(logits[...] - lse[:, :1])
    value = weight * (grad - col_dot) + comb[...].astype(F32) * gcomb[...]
    full[...] = value
    span = pl.ds(pl.multiple_of(step * 512, 512), 512)
    all_grad[:, span] = value
    all_weight[:, span] = weight

    @pl.when(step == pl.num_programs(1) - 1)
    def _():
        for k, out in enumerate((c0, c1, c2, c3)):
            piece = pl.ds(chunk("y", k, 256), 256)
            out[:, :256] = all_grad[:, piece].astype(BF16)
            out[:, 256:] = all_weight[:, piece].astype(BF16)


def dispatch_grad(tokens, gslot, slot_in, logits, lse, comb, gcomb):
    rows = pl.BlockSpec((32, 1280), lambda i, t: (i, 0))
    wide = pl.BlockSpec((32, 512), lambda i, t: (i, t))
    part = pl.BlockSpec((32, 512), lambda i, t: (i, 0))
    return pl.pallas_call(
        dispatch_grad_kernel,
        grid=(2, 2),
        in_specs=[
            pl.BlockSpec((1, 512, 1280), lambda i, t: (i, t, 0)),
            rows,
            rows,
            wide,
            pl.BlockSpec((32, 128), lambda i, t: (i, 0)),
            wide,
            wide,
        ],
        out_specs=[wide] + [part] * 4,
        out_shape=[shape((64, 1024), F32)] + [shape((64, 512), BF16)] * 4,
        scratch_shapes=[pltpu.VMEM((32, 1024), F32), pltpu.VMEM((32, 1024), F32)],
        cost_estimate=pl.CostEstimate(flops=350_000_000, bytes_accessed=7_000_000, transcendentals=65536),
        compiler_params=PARAMS,
        name="dispatch_grad",
    )(in_hbm(tokens), gslot, slot_in, logits, lse, comb, gcomb)


def inputs_kernel(comb, embed, o0, o1, o2, o3):
    for k, out in enumerate((o0, o1, o2, o3)):
        out[:64, :] = comb[:, pl.ds(chunk("y", k, 256), 256)]
        for n in range(5):
            out[64 + 32 * n : 96 + 32 * n, :] = embed[:, 256 * n : 256 * n + 256]


def input_blocks(comb, embed):
    return pl.pallas_call(
        inputs_kernel,
        out_shape=[shape((224, 256), BF16)] * 4,
        cost_estimate=pl.CostEstimate(flops=0, bytes_accessed=700_000, transcendentals=0),
        compiler_params=PARAMS,
        name="input_blocks",
    )(comb, embed)


def rows_kernel(*refs):
    slots, parts, inputs = (refs[4 * n : 4 * n + 4] for n in range(3))
    row_dot, m0, m1, m2, m3, other, scratch = refs[12:]
    core = lax.axis_index("core")
    embeds = [
        jnp.concatenate([one[64 + 32 * n : 96 + 32 * n, :] for n in range(5)], axis=1)
        for one in inputs
    ]
    for i in range(2):
        half = slice(32 * i, 32 * i + 32)
        dots = row_dot[i, :, pl.ds(chunk("y", 0, 256), 256)]
        weights = [one[half, 256:] for one in parts] + [
            (p[half, :256].astype(F32) - c[half, :].astype(F32) * dots).astype(BF16)
            for p, c in zip(parts, inputs)
        ]
        rows = [one[half, :] for one in slots] + embeds
        scratch[i] = lax.dot_general(
            jnp.concatenate(weights), jnp.concatenate(rows), TN, preferred_element_type=F32
        )
        for k, mine in enumerate((m0, m1, m2, m3)):
            base = ((lax.axis_index("x") + k) & 3) * 64
            here = pl.multiple_of(base + core * 32, 32)
            there = pl.multiple_of(base + (1 - core) * 32, 32)
            mine[i] = scratch[i, pl.ds(here, 32), :].astype(BF16)
            other[k, i] = scratch[i, pl.ds(there, 32), :].astype(BF16)


def patch_rows(slots, parts, inputs, row_dot):
    block = shape((2, 32, 1280), BF16)
    *mine, other = pl.pallas_call(
        rows_kernel,
        out_shape=[block] * 4 + [shape((4, 2, 32, 1280), BF16)],
        scratch_shapes=[pltpu.VMEM((2, 256, 1280), F32)],
        cost_estimate=pl.CostEstimate(flops=335_000_000, bytes_accessed=3_000_000, transcendentals=0),
        compiler_params=PARAMS,
        name="patch_rows",
    )(*slots, *parts, *inputs, row_dot)
    return mine, other


def add_kernel(m0, m1, m2, m3, other, o0, o1, o2, o3):
    for k, (mine, out) in enumerate(((m0, o0), (m1, o1), (m2, o2), (m3, o3))):
        out[...] = add(mine[...], other[k])


def add_cores(mine, other):
    return pl.pallas_call(
        add_kernel,
        out_shape=[shape((2, 32, 1280), BF16)] * 4,
        cost_estimate=pl.CostEstimate(flops=327_680, bytes_accessed=2_000_000, transcendentals=0),
        compiler_params=PARAMS,
        name="add_cores",
    )(*mine, other)


def after(value, *others):
    return lax.optimization_barrier((value, *others))[0]


def sources(terms):
    return [terms[0], terms[3], terms[2], terms[1]]


def local(tokens, slot_embed, combine, w_in, w_out, grad_out):
    w_in, w_out = w_in[0], w_out[0]
    embed = slot_embed.T
    comb = jnp.transpose(combine, (0, 2, 1)).reshape(64, 1024)
    comb_f = comb.astype(F32)
    inputs = sources(scatter_terms(input_blocks(comb, embed), "y"))

    logits, part = local_softmax(tokens, embed)
    part = merge_pair(part, near(part))

    out_part = jnp.einsum(
        "ijt,itd->ijd", comb.reshape(2, 32, 1024), grad_out, preferred_element_type=F32
    )
    out_part = out_part.astype(BF16).reshape(64, 1280)
    out_part = add(out_part, far(out_part))
    grad_slot_out = add(out_part, near(out_part))
    slot_in, lse = merge_last(part, far(part))
    slot_in = after(slot_in, *inputs)

    pre_act = jnp.dot(slot_in, w_in, preferred_element_type=F32)
    act, slope = gelu_parts(pre_act)
    act = act.astype(BF16)
    out_sum = jnp.dot(act, w_out, preferred_element_type=F32).astype(BF16)
    out_sum = add(out_sum, near(out_sum))
    out_other = far(out_sum)
    grad_act = jnp.einsum("sd,hd->sh", grad_slot_out, w_out, preferred_element_type=F32)
    grad_pre = (grad_act * slope).astype(BF16)
    in_sum = jnp.einsum("sh,dh->sd", grad_pre, w_in, preferred_element_type=F32).astype(BF16)
    in_sum = add(in_sum, far(in_sum))
    grad_slot_in = add(in_sum, near(in_sum))

    grad_combine, row_dot = combine_grad(grad_out, out_sum, out_other, comb)
    row_dot = row_dot + swap_cores(row_dot)
    for axis in ("x", "y"):
        row_dot = sum(scatter_terms([row_dot] * 4, axis))

    rows = gather_blocks(grad_slot_in, "y")
    partial_logits, *chunks = dispatch_grad(
        tokens, grad_slot_in, slot_in, logits, lse, comb, grad_combine
    )
    chunks = sources(scatter_terms(chunks, "y"))

    mine, other = patch_rows(rows, chunks, inputs, row_dot)
    sums = add_cores(mine, swap_cores(other))
    terms = scatter_terms(sums, "x")
    grad_tokens = sum(term.astype(F32) for term in terms).astype(BF16)

    grad_logits = partial_logits - comb_f * jnp.repeat(row_dot, 32, axis=1).reshape(64, 1024)
    grad_logits = grad_logits.astype(BF16).reshape(2, 32, 1024)
    embed_part = jnp.einsum("ijt,itd->jd", grad_logits, tokens, preferred_element_type=F32)
    embed_part = embed_part.astype(BF16)
    embed_part = add(embed_part, near(embed_part))
    embed_sum = add(embed_part, far(embed_part))
    z = lax.axis_index("seq")
    grad_embed = lax.dynamic_slice_in_dim(embed_sum, z * 320, 320, axis=1).T

    act_late, slot_late = lax.optimization_barrier((act, slot_in, sums[0]))[:2]
    grad_w_out = jnp.einsum("sh,sd->hd", act_late, grad_slot_out, preferred_element_type=F32)
    grad_w_in = jnp.einsum("sd,sh->dh", slot_late, grad_pre, preferred_element_type=F32)
    return (
        grad_tokens,
        grad_embed,
        grad_w_in.astype(BF16)[None],
        grad_w_out.astype(BF16)[None],
    )


def solution(mesh):
    fine = Mesh(mesh.devices.reshape(4, 4, 4, 2), ("seq", "y", "x", "core"))
    expert = ("y", "x", "core")
    return jax.shard_map(
        local,
        mesh=fine,
        in_specs=(
            P(None, "seq", None),
            P(None, expert),
            P(None, "seq", expert),
            P(expert, None, "seq"),
            P(expert, "seq", None),
            P(None, "seq", None),
        ),
        out_specs=(
            P(None, ("seq", *expert), None),
            P("seq", expert),
            P(expert, None, "seq"),
            P(expert, "seq", None),
        ),
        check_vma=False,
    )
```

```python
import math

import jax
import jax.numpy as jnp
from jax import lax
from jax.experimental import pallas as pl
from jax.experimental.pallas import tpu as pltpu
from jax.sharding import Mesh, PartitionSpec as P

F32 = jnp.float32
BF16 = jnp.bfloat16
NT = (((1,), (1,)), ((), ()))
TN = (((0,), (0,)), ((), ()))
LARGE = pltpu.CompilerParams(vmem_limit_bytes=16 * 1024 * 1024)
MEDIUM = pltpu.CompilerParams(vmem_limit_bytes=10 * 1024 * 1024)
SMALL = pltpu.CompilerParams(vmem_limit_bytes=4 * 1024 * 1024)


def shape(dims, dtype):
    return jax.ShapeDtypeStruct(dims, dtype)


def gelu_parts(values):
    cdf = 0.5 * (1.0 + jax.scipy.special.erf(values / math.sqrt(2.0)))
    slope = cdf + values * jnp.exp(-0.5 * values * values) / math.sqrt(2.0 * math.pi)
    return values * cdf, slope


def shift(value, axis, by):
    return lax.ppermute(value, axis, [(i, (i + by) % 4) for i in range(4)])


def swap_cores(value):
    return lax.ppermute(value, "core", [(0, 1), (1, 0)])


def near(value, axis="seq"):
    return lax.ppermute(value, axis, [(0, 1), (1, 0), (2, 3), (3, 2)])


def far(value, axis="seq"):
    return lax.ppermute(value, axis, [(0, 3), (3, 0), (1, 2), (2, 1)])


def add(one, two):
    return (one.astype(F32) + two.astype(F32)).astype(BF16)


def scatter_terms(blocks, axis):
    return [blocks[0]] + [shift(blocks[k], axis, k) for k in (1, 2, 3)]


def gather_blocks(block, axis):
    return [block] + [shift(block, axis, -k) for k in (1, 2, 3)]


def chunk(axis, k, size):
    return pl.multiple_of(((lax.axis_index(axis) + k) & 3) * size, size)


def lse_lanes(lse):
    high = lse.astype(BF16).astype(F32)
    middle = (lse - high).astype(BF16).astype(F32)
    low = lse - high - middle
    lane = lax.broadcasted_iota(jnp.int32, (lse.shape[0], 128), 1)
    lanes = jnp.where(lane == 0, high, jnp.where(lane == 1, middle, low))
    return jnp.where(lane < 3, lanes, 0.0).astype(BF16)


def lse_column(lanes):
    lanes = lanes.astype(F32)
    return lanes[:, 0:1] + lanes[:, 1:2] + lanes[:, 2:3]


def softmax_kernel(tok, embed, logits, part, peak, total, sums):
    step = pl.program_id(0)

    @pl.when(step == 0)
    def _():
        peak[...] = jnp.full_like(peak, -jnp.inf)
        total[...] = jnp.zeros_like(total)
        sums[...] = jnp.zeros_like(sums)

    scores = [
        lax.dot_general(tok[i], embed[...], NT, preferred_element_type=F32).T for i in range(2)
    ]
    for i in range(2):
        half = slice(32 * i, 32 * i + 32)
        logits[half, :] = scores[i]
        before = peak[half, :1]
        top = jnp.maximum(before, jnp.max(scores[i], axis=1, keepdims=True))
        scale = jnp.exp(before - top)
        weight = jnp.exp(scores[i] - top)
        new_total = total[half, :1] * scale + jnp.sum(weight, axis=1, keepdims=True)
        new_sums = sums[half, :] * scale + jnp.dot(
            weight.astype(BF16), tok[i], preferred_element_type=F32
        )
        peak[half, :] = jnp.broadcast_to(top, (32, 128))
        total[half, :] = jnp.broadcast_to(new_total, (32, 128))
        sums[half, :] = new_sums

        @pl.when(step == pl.num_programs(0) - 1)
        def _():
            part[half, :1280] = (new_sums / new_total).astype(BF16)
            part[half, 1280:] = lse_lanes(top + jnp.log(new_total))


def in_hbm(value):
    return pltpu.with_memory_space_constraint(value, pltpu.HBM)


def local_softmax(tokens, embed):
    return pl.pallas_call(
        softmax_kernel,
        grid=(2,),
        in_specs=[
            pl.BlockSpec((2, 512, 1280), lambda t: (0, t, 0)),
            pl.BlockSpec((32, 1280), lambda t: (0, 0)),
        ],
        out_specs=[
            pl.BlockSpec((64, 512), lambda t: (0, t)),
            pl.BlockSpec((64, 1408), lambda t: (0, 0)),
        ],
        out_shape=[shape((64, 1024), F32), shape((64, 1408), BF16)],
        scratch_shapes=[
            pltpu.VMEM((64, 128), F32),
            pltpu.VMEM((64, 128), F32),
            pltpu.VMEM((64, 1280), F32),
        ],
        cost_estimate=pl.CostEstimate(flops=700_000_000, bytes_accessed=6_000_000, transcendentals=65536),
        compiler_params=LARGE,
        name="local_softmax",
    )(in_hbm(tokens), embed)


def merge_kernel(one, two, sums, lse):
    lse_a, lse_b = lse_column(one[:, 1280:]), lse_column(two[:, 1280:])
    top = jnp.maximum(lse_a, lse_b)
    weight_a, weight_b = jnp.exp(lse_a - top), jnp.exp(lse_b - top)
    total = weight_a + weight_b
    part = (weight_a / total) * one[:, :1280].astype(F32)
    part = part + (weight_b / total) * two[:, :1280].astype(F32)
    lse_all = top + jnp.log(total)
    sums[:, :1280] = part.astype(BF16)
    if lse is None:
        sums[:, 1280:] = lse_lanes(lse_all)
    else:
        lse[...] = jnp.broadcast_to(lse_all, lse.shape)


def merge_pair(one, two):
    return pl.pallas_call(
        lambda a, b, out: merge_kernel(a, b, out, None),
        out_shape=shape((64, 1408), BF16),
        cost_estimate=pl.CostEstimate(flops=300_000, bytes_accessed=540_000, transcendentals=256),
        compiler_params=SMALL,
        name="merge_pair",
    )(one, two)


def merge_last(one, two):
    return pl.pallas_call(
        merge_kernel,
        out_shape=[shape((64, 1280), BF16), shape((64, 128), F32)],
        cost_estimate=pl.CostEstimate(flops=300_000, bytes_accessed=540_000, transcendentals=256),
        compiler_params=SMALL,
        name="merge_last",
    )(one, two)


def combine_grad_kernel(gout, sum_a, sum_b, comb, grad, row):
    slot_out = add(sum_a[...], sum_b[...])
    value = lax.dot_general(gout[0], slot_out, NT, preferred_element_type=F32).T
    grad[...] = value
    row[0] = jnp.sum(comb[...].astype(F32) * value, axis=0, keepdims=True)


def combine_grad(grad_out, sum_a, sum_b, comb):
    return pl.pallas_call(
        combine_grad_kernel,
        grid=(2, 2),
        in_specs=[
            pl.BlockSpec((1, 512, 1280), lambda i, t: (i, t, 0)),
            pl.BlockSpec((32, 1280), lambda i, t: (i, 0)),
            pl.BlockSpec((32, 1280), lambda i, t: (i, 0)),
            pl.BlockSpec((32, 512), lambda i, t: (i, t)),
        ],
        out_specs=[
            pl.BlockSpec((32, 512), lambda i, t: (i, t)),
            pl.BlockSpec((1, 1, 512), lambda i, t: (i, 0, t)),
        ],
        out_shape=[shape((64, 1024), F32), shape((2, 1, 1024), F32)],
        cost_estimate=pl.CostEstimate(flops=350_000_000, bytes_accessed=6_000_000, transcendentals=0),
        compiler_params=MEDIUM,
        name="combine_grad",
    )(grad_out, sum_a, sum_b, comb)


def dispatch_grad_kernel(tok, gslot, slot_in, logits, lse, comb, gcomb, full, c0, c1, c2, c3, all_grad, all_weight):
    step = pl.program_id(1)
    rows = gslot[...]
    col_dot = jnp.sum(slot_in[...].astype(F32) * rows.astype(F32), axis=1, keepdims=True)
    grad = lax.dot_general(tok[0], rows, NT, preferred_element_type=F32).T
    weight = jnp.exp(logits[...] - lse[:, :1])
    value = weight * (grad - col_dot) + comb[...].astype(F32) * gcomb[...]
    full[...] = value
    span = pl.ds(pl.multiple_of(step * 512, 512), 512)
    all_grad[:, span] = value
    all_weight[:, span] = weight

    @pl.when(step == pl.num_programs(1) - 1)
    def _():
        for k, out in enumerate((c0, c1, c2, c3)):
            piece = pl.ds(chunk("y", k, 256), 256)
            out[:, :256] = all_grad[:, piece].astype(BF16)
            out[:, 256:] = all_weight[:, piece].astype(BF16)


def dispatch_grad(tokens, gslot, slot_in, logits, lse, comb, gcomb):
    rows = pl.BlockSpec((32, 1280), lambda i, t: (i, 0))
    wide = pl.BlockSpec((32, 512), lambda i, t: (i, t))
    part = pl.BlockSpec((32, 512), lambda i, t: (i, 0))
    return pl.pallas_call(
        dispatch_grad_kernel,
        grid=(2, 2),
        in_specs=[
            pl.BlockSpec((1, 512, 1280), lambda i, t: (i, t, 0)),
            rows,
            rows,
            wide,
            pl.BlockSpec((32, 128), lambda i, t: (i, 0)),
            wide,
            wide,
        ],
        out_specs=[wide] + [part] * 4,
        out_shape=[shape((64, 1024), F32)] + [shape((64, 512), BF16)] * 4,
        scratch_shapes=[pltpu.VMEM((32, 1024), F32), pltpu.VMEM((32, 1024), F32)],
        cost_estimate=pl.CostEstimate(flops=350_000_000, bytes_accessed=7_000_000, transcendentals=65536),
        compiler_params=MEDIUM,
        name="dispatch_grad",
    )(tokens, gslot, slot_in, logits, lse, comb, gcomb)


def rows_kernel(*refs):
    slots, parts = refs[:4], refs[4:8]
    inputs, row_dot, m0, m1, m2, m3, other, scratch = refs[8:]
    core, y = lax.axis_index("core"), lax.axis_index("y")
    mine_span = pl.ds(chunk("y", 0, 256), 256)
    embeds = [
        jnp.concatenate(
            [inputs[(y + k) & 3, 32 * n : 32 * n + 32, 1024:1664] for n in range(2)], axis=1
        )
        for k in range(4)
    ]
    for i in range(2):
        half = slice(32 * i, 32 * i + 32)
        dots = row_dot[i, :, mine_span]
        weights = [one[half, 256:] for one in parts] + [
            (
                part[half, :256].astype(F32)
                - inputs[(y + k) & 3, half, mine_span].astype(F32) * dots
            ).astype(BF16)
            for k, part in enumerate(parts)
        ]
        rows = [one[half, :] for one in slots] + embeds
        scratch[i] = lax.dot_general(
            jnp.concatenate(weights), jnp.concatenate(rows), TN, preferred_element_type=F32
        )
        for k, mine in enumerate((m0, m1, m2, m3)):
            base = ((lax.axis_index("x") + k) & 3) * 64
            here = pl.multiple_of(base + core * 32, 32)
            there = pl.multiple_of(base + (1 - core) * 32, 32)
            mine[i] = scratch[i, pl.ds(here, 32), :].astype(BF16)
            other[k, i] = scratch[i, pl.ds(there, 32), :].astype(BF16)


def patch_rows(slots, parts, inputs, row_dot):
    block = shape((2, 32, 1280), BF16)
    *mine, other = pl.pallas_call(
        rows_kernel,
        out_shape=[block] * 4 + [shape((4, 2, 32, 1280), BF16)],
        scratch_shapes=[pltpu.VMEM((2, 256, 1280), F32)],
        cost_estimate=pl.CostEstimate(flops=335_000_000, bytes_accessed=3_000_000, transcendentals=0),
        compiler_params=MEDIUM,
        name="patch_rows",
    )(*slots, *parts, inputs, row_dot)
    return mine, other


def add_kernel(m0, m1, m2, m3, other, o0, o1, o2, o3):
    for k, (mine, out) in enumerate(((m0, o0), (m1, o1), (m2, o2), (m3, o3))):
        out[...] = add(mine[...], other[k])


def add_cores(mine, other):
    return pl.pallas_call(
        add_kernel,
        out_shape=[shape((2, 32, 1280), BF16)] * 4,
        cost_estimate=pl.CostEstimate(flops=327_680, bytes_accessed=2_000_000, transcendentals=0),
        compiler_params=SMALL,
        name="add_cores",
    )(*mine, other)


def after(value, *others):
    return lax.optimization_barrier((value, *others))[0]


def sources(terms):
    return [terms[0], terms[3], terms[2], terms[1]]


def local(tokens, slot_embed, combine, w_in, w_out, grad_out):
    w_in, w_out = w_in[0], w_out[0]
    embed = slot_embed.T
    comb = jnp.transpose(combine, (0, 2, 1)).reshape(64, 1024)
    comb_f = comb.astype(F32)
    inputs = jnp.concatenate([embed[:, :640], embed[:, 640:]], axis=0)
    inputs = jnp.concatenate([comb, inputs, jnp.zeros((64, 896), BF16)], axis=1)
    inputs = lax.all_gather(inputs, "y")

    logits, part = local_softmax(tokens, embed)
    comb_late = after(comb, part)
    part = merge_pair(part, near(part))

    out_part = jnp.einsum(
        "ijt,itd->ijd", comb_late.reshape(2, 32, 1024), grad_out, preferred_element_type=F32
    )
    out_part = out_part.astype(BF16).reshape(64, 1280)
    out_part = add(out_part, far(out_part))
    grad_slot_out = add(out_part, near(out_part))
    slot_in, lse = merge_last(part, far(part))

    pre_act = jnp.dot(slot_in, w_in, preferred_element_type=F32)
    act, slope = gelu_parts(pre_act)
    act = act.astype(BF16)
    out_sum = jnp.dot(act, w_out, preferred_element_type=F32).astype(BF16)
    grad_slot_out = after(grad_slot_out, out_sum)
    out_sum = add(out_sum, near(out_sum))
    out_other = far(out_sum)
    grad_act = jnp.einsum("sd,hd->sh", grad_slot_out, w_out, preferred_element_type=F32)
    grad_pre = (grad_act * slope).astype(BF16)
    in_sum = jnp.einsum("sh,dh->sd", grad_pre, w_in, preferred_element_type=F32).astype(BF16)
    in_sum = add(in_sum, far(in_sum))
    in_other = near(in_sum)

    grad_combine, row_dot = combine_grad(grad_out, out_sum, out_other, comb)
    grad_slot_in = add(after(in_sum, row_dot), in_other)
    row_dot = row_dot + swap_cores(row_dot)
    row_dot = row_dot + near(row_dot, "x")
    act_late, late, row_dot = lax.optimization_barrier((act, grad_slot_in, row_dot))
    row_dot = row_dot + far(row_dot, "x")
    row_dot = row_dot + near(row_dot, "y")
    row_dot = row_dot + far(row_dot, "y")

    rows = gather_blocks(grad_slot_in, "y")
    partial_logits, *chunks = dispatch_grad(
        tokens, late, slot_in, logits, lse, comb, grad_combine
    )
    chunks = sources(scatter_terms(chunks, "y"))

    mine, other = patch_rows(rows, chunks, inputs, row_dot)
    sums = add_cores(mine, swap_cores(other))
    terms = scatter_terms(sums, "x")
    grad_tokens = sum(term.astype(F32) for term in terms).astype(BF16)

    grad_logits = partial_logits - comb_f * jnp.repeat(row_dot, 32, axis=1).reshape(64, 1024)
    grad_logits = grad_logits.astype(BF16).reshape(2, 32, 1024)
    embed_part = jnp.einsum("ijt,itd->jd", grad_logits, tokens, preferred_element_type=F32)
    embed_part = embed_part.astype(BF16)
    embed_part = add(embed_part, near(embed_part))
    embed_part = after(embed_part, sums[0])
    embed_sum = add(embed_part, far(embed_part))
    z = lax.axis_index("seq")
    grad_embed = lax.dynamic_slice_in_dim(embed_sum, z * 320, 320, axis=1).T

    slot_late = after(slot_in, sums[0])
    grad_w_out = jnp.einsum("sh,sd->hd", act_late, grad_slot_out, preferred_element_type=F32)
    grad_w_in = jnp.einsum("sd,sh->dh", slot_late, grad_pre, preferred_element_type=F32)
    return (
        grad_tokens,
        grad_embed,
        grad_w_in.astype(BF16)[None],
        grad_w_out.astype(BF16)[None],
    )


def solution(mesh):
    fine = Mesh(mesh.devices.reshape(4, 4, 4, 2), ("seq", "y", "x", "core"))
    expert = ("y", "x", "core")
    return jax.shard_map(
        local,
        mesh=fine,
        in_specs=(
            P(None, "seq", None),
            P(None, expert),
            P(None, "seq", expert),
            P(expert, None, "seq"),
            P(expert, "seq", None),
            P(None, "seq", None),
        ),
        out_specs=(
            P(None, ("seq", *expert), None),
            P("seq", expert),
            P(expert, None, "seq"),
            P(expert, "seq", None),
        ),
        check_vma=False,
    )
```

```python
import math

import jax
import jax.numpy as jnp
from jax import lax
from jax.experimental import pallas as pl
from jax.experimental.pallas import tpu as pltpu
from jax.sharding import Mesh, PartitionSpec as P

F32 = jnp.float32
BF16 = jnp.bfloat16
NT = (((1,), (1,)), ((), ()))
TN = (((0,), (0,)), ((), ()))
LARGE = pltpu.CompilerParams(vmem_limit_bytes=16 * 1024 * 1024)
MEDIUM = pltpu.CompilerParams(vmem_limit_bytes=10 * 1024 * 1024)
SMALL = pltpu.CompilerParams(vmem_limit_bytes=4 * 1024 * 1024)


def shape(dims, dtype):
    return jax.ShapeDtypeStruct(dims, dtype)


def gelu_parts(values):
    cdf = 0.5 * (1.0 + jax.scipy.special.erf(values / math.sqrt(2.0)))
    slope = cdf + values * jnp.exp(-0.5 * values * values) / math.sqrt(2.0 * math.pi)
    return values * cdf, slope


def shift(value, axis, by):
    return lax.ppermute(value, axis, [(i, (i + by) % 4) for i in range(4)])


def swap_cores(value):
    return lax.ppermute(value, "core", [(0, 1), (1, 0)])


def near(value, axis="seq"):
    return lax.ppermute(value, axis, [(0, 1), (1, 0), (2, 3), (3, 2)])


def far(value, axis="seq"):
    return lax.ppermute(value, axis, [(0, 3), (3, 0), (1, 2), (2, 1)])


def add(one, two):
    return (one.astype(F32) + two.astype(F32)).astype(BF16)


def scatter_terms(blocks, axis):
    return [blocks[0]] + [shift(blocks[k], axis, k) for k in (1, 2, 3)]


def gather_blocks(block, axis):
    return [block] + [shift(block, axis, -k) for k in (1, 2, 3)]


def chunk(axis, k, size):
    return pl.multiple_of(((lax.axis_index(axis) + k) & 3) * size, size)


def lse_lanes(lse):
    high = lse.astype(BF16).astype(F32)
    middle = (lse - high).astype(BF16).astype(F32)
    low = lse - high - middle
    lane = lax.broadcasted_iota(jnp.int32, (lse.shape[0], 128), 1)
    lanes = jnp.where(lane == 0, high, jnp.where(lane == 1, middle, low))
    return jnp.where(lane < 3, lanes, 0.0).astype(BF16)


def lse_column(lanes):
    lanes = lanes.astype(F32)
    return lanes[:, 0:1] + lanes[:, 1:2] + lanes[:, 2:3]


def softmax_kernel(t00, t01, t10, t11, embed, logits, part, peak, total, sums):
    step = pl.program_id(0)

    @pl.when(step == 0)
    def _():
        peak[...] = jnp.full_like(peak, -jnp.inf)
        total[...] = jnp.zeros_like(total)
        sums[...] = jnp.zeros_like(sums)

    slots = embed[...]
    blocks = [[t00[0], t01[0]], [t10[0], t11[0]]]
    scores = [
        jnp.concatenate(
            [lax.dot_general(one, slots, NT, preferred_element_type=F32).T for one in pair],
            axis=1,
        )
        for pair in blocks
    ]
    for i in range(2):
        half = slice(32 * i, 32 * i + 32)
        logits[half, :] = scores[i]
        before = peak[half, :1]
        top = jnp.maximum(before, jnp.max(scores[i], axis=1, keepdims=True))
        scale = jnp.exp(before - top)
        weight = jnp.exp(scores[i] - top)
        new_total = total[half, :1] * scale + jnp.sum(weight, axis=1, keepdims=True)
        weight = weight.astype(BF16)
        new_sums = sums[half, :] * scale
        for n in range(2):
            new_sums = new_sums + jnp.dot(
                weight[:, 256 * n : 256 * n + 256], blocks[i][n], preferred_element_type=F32
            )
        peak[half, :] = jnp.broadcast_to(top, (32, 128))
        total[half, :] = jnp.broadcast_to(new_total, (32, 128))
        sums[half, :] = new_sums

        @pl.when(step == pl.num_programs(0) - 1)
        def _():
            part[half, :1280] = (new_sums / new_total).astype(BF16)
            part[half, 1280:] = lse_lanes(top + jnp.log(new_total))


def in_hbm(value):
    return pltpu.with_memory_space_constraint(value, pltpu.HBM)


def local_softmax(tokens, embed):
    return pl.pallas_call(
        softmax_kernel,
        grid=(2,),
        in_specs=[
            pl.BlockSpec((1, 256, 1280), lambda t: (0, 2 * t, 0)),
            pl.BlockSpec((1, 256, 1280), lambda t: (0, 2 * t + 1, 0)),
            pl.BlockSpec((1, 256, 1280), lambda t: (1, 2 * t, 0)),
            pl.BlockSpec((1, 256, 1280), lambda t: (1, 2 * t + 1, 0)),
            pl.BlockSpec((32, 1280), lambda t: (0, 0)),
        ],
        out_specs=[
            pl.BlockSpec((64, 512), lambda t: (0, t)),
            pl.BlockSpec((64, 1408), lambda t: (0, 0)),
        ],
        out_shape=[shape((64, 1024), F32), shape((64, 1408), BF16)],
        scratch_shapes=[
            pltpu.VMEM((64, 128), F32),
            pltpu.VMEM((64, 128), F32),
            pltpu.VMEM((64, 1280), F32),
        ],
        cost_estimate=pl.CostEstimate(flops=700_000_000, bytes_accessed=6_000_000, transcendentals=65536),
        compiler_params=LARGE,
        name="local_softmax",
    )(*[in_hbm(tokens)] * 4, embed)


def merge_kernel(one, two, sums, lse):
    lse_a, lse_b = lse_column(one[:, 1280:]), lse_column(two[:, 1280:])
    top = jnp.maximum(lse_a, lse_b)
    weight_a, weight_b = jnp.exp(lse_a - top), jnp.exp(lse_b - top)
    total = weight_a + weight_b
    part = (weight_a / total) * one[:, :1280].astype(F32)
    part = part + (weight_b / total) * two[:, :1280].astype(F32)
    lse_all = top + jnp.log(total)
    sums[:, :1280] = part.astype(BF16)
    if lse is None:
        sums[:, 1280:] = lse_lanes(lse_all)
    else:
        lse[...] = jnp.broadcast_to(lse_all, lse.shape)


def merge_pair(one, two):
    return pl.pallas_call(
        lambda a, b, out: merge_kernel(a, b, out, None),
        out_shape=shape((64, 1408), BF16),
        cost_estimate=pl.CostEstimate(flops=300_000, bytes_accessed=540_000, transcendentals=256),
        compiler_params=SMALL,
        name="merge_pair",
    )(one, two)


def merge_last(one, two):
    return pl.pallas_call(
        merge_kernel,
        out_shape=[shape((64, 1280), BF16), shape((64, 128), F32)],
        cost_estimate=pl.CostEstimate(flops=300_000, bytes_accessed=540_000, transcendentals=256),
        compiler_params=SMALL,
        name="merge_last",
    )(one, two)


def combine_grad_kernel(gout, sum_a, sum_b, comb, grad, row):
    slot_out = add(sum_a[...], sum_b[...])
    value = lax.dot_general(gout[0], slot_out, NT, preferred_element_type=F32).T
    grad[...] = value
    row[0] = jnp.sum(comb[...].astype(F32) * value, axis=0, keepdims=True)


def combine_grad(grad_out, sum_a, sum_b, comb):
    return pl.pallas_call(
        combine_grad_kernel,
        grid=(2, 2),
        in_specs=[
            pl.BlockSpec((1, 512, 1280), lambda i, t: (i, t, 0)),
            pl.BlockSpec((32, 1280), lambda i, t: (i, 0)),
            pl.BlockSpec((32, 1280), lambda i, t: (i, 0)),
            pl.BlockSpec((32, 512), lambda i, t: (i, t)),
        ],
        out_specs=[
            pl.BlockSpec((32, 512), lambda i, t: (i, t)),
            pl.BlockSpec((1, 1, 512), lambda i, t: (i, 0, t)),
        ],
        out_shape=[shape((64, 1024), F32), shape((2, 1, 1024), F32)],
        cost_estimate=pl.CostEstimate(flops=350_000_000, bytes_accessed=6_000_000, transcendentals=0),
        compiler_params=MEDIUM,
        name="combine_grad",
    )(grad_out, sum_a, sum_b, comb)


def dispatch_grad_kernel(tok, gslot, slot_in, logits, lse, comb, gcomb, full, c0, c1, c2, c3, all_weight):
    rows = gslot[...]
    col_dot = jnp.sum(slot_in[...].astype(F32) * rows.astype(F32), axis=1, keepdims=True)
    grad = lax.dot_general(tok[0], rows, NT, preferred_element_type=F32).T
    weight = jnp.exp(logits[...] - lse[:, :1])
    full[...] = weight * (grad - col_dot) + comb[...].astype(F32) * gcomb[...]
    all_weight[...] = weight
    for k, out in enumerate((c0, c1, c2, c3)):
        piece = pl.ds(chunk("y", k, 256), 256)
        out[:, :1280] = rows
        out[:, 1280:1536] = full[:, piece].astype(BF16)
        out[:, 1536:] = all_weight[:, piece].astype(BF16)


def dispatch_grad(tokens, gslot, slot_in, logits, lse, comb, gcomb):
    rows = pl.BlockSpec((32, 1280), lambda i: (i, 0))
    wide = pl.BlockSpec((32, 1024), lambda i: (i, 0))
    part = pl.BlockSpec((32, 1792), lambda i: (i, 0))
    return pl.pallas_call(
        dispatch_grad_kernel,
        grid=(2,),
        in_specs=[
            pl.BlockSpec((1, 1024, 1280), lambda i: (i, 0, 0)),
            rows,
            rows,
            wide,
            pl.BlockSpec((32, 128), lambda i: (i, 0)),
            wide,
            wide,
        ],
        out_specs=[wide] + [part] * 4,
        out_shape=[shape((64, 1024), F32)] + [shape((64, 1792), BF16)] * 4,
        scratch_shapes=[pltpu.VMEM((32, 1024), F32)],
        cost_estimate=pl.CostEstimate(flops=350_000_000, bytes_accessed=7_000_000, transcendentals=65536),
        compiler_params=MEDIUM,
        name="dispatch_grad",
    )(tokens, gslot, slot_in, logits, lse, comb, gcomb)


def inputs_kernel(comb, embed, o0, o1, o2, o3):
    for k, out in enumerate((o0, o1, o2, o3)):
        out[:64, :] = comb[:, pl.ds(chunk("y", k, 256), 256)]
        for n in range(5):
            out[64 + 32 * n : 96 + 32 * n, :] = embed[:, 256 * n : 256 * n + 256]


def input_blocks(comb, embed):
    return pl.pallas_call(
        inputs_kernel,
        out_shape=[shape((224, 256), BF16)] * 4,
        cost_estimate=pl.CostEstimate(flops=0, bytes_accessed=700_000, transcendentals=0),
        compiler_params=SMALL,
        name="input_blocks",
    )(comb, embed)


def embed_grad_kernel(tok, partial_logits, comb, row_dot, out, sums):
    grad = partial_logits[...] - comb[...].astype(F32) * row_dot[0]
    value = jnp.dot(grad.astype(BF16), tok[0], preferred_element_type=F32)

    @pl.when(pl.program_id(0) == 0)
    def _():
        sums[...] = value

    @pl.when(pl.program_id(0) == 1)
    def _():
        out[...] = (sums[...] + value).astype(BF16)


def embed_grad(tokens, partial_logits, comb, row_dot):
    wide = pl.BlockSpec((32, 1024), lambda i: (i, 0))
    return pl.pallas_call(
        embed_grad_kernel,
        grid=(2,),
        in_specs=[
            pl.BlockSpec((1, 1024, 1280), lambda i: (i, 0, 0)),
            wide,
            wide,
            pl.BlockSpec((1, 1, 1024), lambda i: (i, 0, 0)),
        ],
        out_specs=pl.BlockSpec((32, 1280), lambda i: (0, 0)),
        out_shape=shape((32, 1280), BF16),
        scratch_shapes=[pltpu.VMEM((32, 1280), F32)],
        cost_estimate=pl.CostEstimate(flops=170_000_000, bytes_accessed=6_000_000, transcendentals=0),
        compiler_params=MEDIUM,
        name="embed_grad",
    )(tokens, partial_logits, comb, row_dot)


def rows_kernel(*refs):
    parts, inputs = refs[:4], refs[4:8]
    row_dot, mine, other, scratch = refs[8:]
    core = lax.axis_index("core")
    embeds = [
        jnp.concatenate([one[64 + 32 * n : 96 + 32 * n, :] for n in range(5)], axis=1)
        for one in inputs
    ]
    for i in range(2):
        half = slice(32 * i, 32 * i + 32)
        dots = row_dot[i, :, pl.ds(chunk("y", 0, 256), 256)]
        weights = [one[half, 1536:] for one in parts] + [
            (p[half, 1280:1536].astype(F32) - c[half, :].astype(F32) * dots).astype(BF16)
            for p, c in zip(parts, inputs)
        ]
        rows = [one[half, :1280] for one in parts] + embeds
        scratch[i] = lax.dot_general(
            jnp.concatenate(weights), jnp.concatenate(rows), TN, preferred_element_type=F32
        )
        for k in range(4):
            base = ((lax.axis_index("x") + k) & 3) * 64
            here = pl.multiple_of(base + core * 32, 32)
            there = pl.multiple_of(base + (1 - core) * 32, 32)
            mine[k, i] = scratch[i, pl.ds(here, 32), :].astype(BF16)
            other[k, i] = scratch[i, pl.ds(there, 32), :].astype(BF16)


def patch_rows(parts, inputs, row_dot):
    return pl.pallas_call(
        rows_kernel,
        out_shape=[shape((4, 2, 32, 1280), BF16)] * 2,
        scratch_shapes=[pltpu.VMEM((2, 256, 1280), F32)],
        cost_estimate=pl.CostEstimate(flops=335_000_000, bytes_accessed=3_000_000, transcendentals=0),
        compiler_params=MEDIUM,
        name="patch_rows",
    )(*parts, *inputs, row_dot)


def add_kernel(mine, other, o0, o1, o2, o3):
    for k, out in enumerate((o0, o1, o2, o3)):
        out[...] = add(mine[k], other[k])


def add_cores(mine, other):
    return pl.pallas_call(
        add_kernel,
        out_shape=[shape((2, 32, 1280), BF16)] * 4,
        cost_estimate=pl.CostEstimate(flops=327_680, bytes_accessed=2_000_000, transcendentals=0),
        compiler_params=SMALL,
        name="add_cores",
    )(mine, other)


def after(value, *others):
    return lax.optimization_barrier((value, *others))[0]


def sources(terms):
    return [terms[0], terms[3], terms[2], terms[1]]


def local(tokens, slot_embed, combine, w_in, w_out, grad_out):
    w_in, w_out = w_in[0], w_out[0]
    embed = slot_embed.T
    comb = jnp.transpose(combine, (0, 2, 1)).reshape(64, 1024)

    logits, part = local_softmax(tokens, embed)
    comb_late = after(comb, part)
    out_part = jnp.einsum(
        "ijt,itd->ijd", comb_late.reshape(2, 32, 1024), grad_out, preferred_element_type=F32
    )
    out_part = out_part.astype(BF16).reshape(64, 1280)
    part = merge_pair(part, near(part))
    out_other = far(out_part)
    comb_late = after(comb_late, part)
    slot_in, lse = merge_last(part, far(part))
    out_part = add(after(out_part, slot_in), out_other)
    inputs = sources(scatter_terms(input_blocks(comb_late, embed), "y"))
    grad_slot_out = add(out_part, near(out_part))

    pre_act = jnp.dot(slot_in, w_in, preferred_element_type=F32)
    act, slope = gelu_parts(pre_act)
    act = act.astype(BF16)
    out_sum = jnp.dot(act, w_out, preferred_element_type=F32).astype(BF16)
    grad_slot_out = after(grad_slot_out, out_sum)
    out_sum = add(out_sum, near(out_sum))
    out_sum = after(out_sum, *inputs)
    sum_other = far(out_sum)
    grad_act = jnp.einsum("sd,hd->sh", grad_slot_out, w_out, preferred_element_type=F32)
    grad_pre = (grad_act * slope).astype(BF16)
    in_sum = jnp.einsum("sh,dh->sd", grad_pre, w_in, preferred_element_type=F32).astype(BF16)
    in_sum = add(in_sum, far(in_sum))
    in_other = near(in_sum)

    grad_combine, row_dot = combine_grad(grad_out, out_sum, sum_other, comb)
    grad_slot_in = add(after(in_sum, row_dot), in_other)
    row_dot = row_dot + swap_cores(row_dot)
    late, row_dot = lax.optimization_barrier((grad_slot_in, row_dot))
    row_dot = row_dot + near(row_dot, "x")
    row_dot = row_dot + far(row_dot, "x")
    row_dot = row_dot + near(row_dot, "y")
    row_dot = row_dot + far(row_dot, "y")

    partial_logits, *parts = dispatch_grad(
        tokens, late, slot_in, logits, lse, comb, grad_combine
    )
    parts = sources(scatter_terms(parts, "y"))

    mine, other = patch_rows(parts, inputs, row_dot)
    other_core = swap_cores(other)

    partial_logits, mine = lax.optimization_barrier((partial_logits, mine))
    embed_part = embed_grad(tokens, partial_logits, comb, row_dot)
    embed_other = near(embed_part)
    sums = add_cores(mine, other_core)
    terms = scatter_terms(sums, "x")
    grad_tokens = sum(term.astype(F32) for term in terms).astype(BF16)
    embed_part = add(after(embed_part, sums[0]), embed_other)
    embed_sum = add(embed_part, far(embed_part))
    z = lax.axis_index("seq")
    grad_embed = lax.dynamic_slice_in_dim(embed_sum, z * 320, 320, axis=1).T

    act_late, slot_late = lax.optimization_barrier((act, slot_in, sums[0]))[:2]
    grad_w_out = jnp.einsum("sh,sd->hd", act_late, grad_slot_out, preferred_element_type=F32)
    grad_w_in = jnp.einsum("sd,sh->dh", slot_late, grad_pre, preferred_element_type=F32)
    return (
        grad_tokens,
        grad_embed,
        grad_w_in.astype(BF16)[None],
        grad_w_out.astype(BF16)[None],
    )


def solution(mesh):
    fine = Mesh(mesh.devices.reshape(4, 4, 4, 2), ("seq", "y", "x", "core"))
    expert = ("y", "x", "core")
    return jax.shard_map(
        local,
        mesh=fine,
        in_specs=(
            P(None, "seq", None),
            P(None, expert),
            P(None, "seq", expert),
            P(expert, None, "seq"),
            P(expert, "seq", None),
            P(None, "seq", None),
        ),
        out_specs=(
            P(None, ("seq", *expert), None),
            P("seq", expert),
            P(expert, None, "seq"),
            P(expert, "seq", None),
        ),
        check_vma=False,
    )
```

```python
import math

import jax
import jax.numpy as jnp
from jax import lax
from jax.experimental import pallas as pl
from jax.experimental.pallas import tpu as pltpu
from jax.sharding import Mesh, PartitionSpec as P

F32 = jnp.float32
BF16 = jnp.bfloat16
NT = (((1,), (1,)), ((), ()))
TN = (((0,), (0,)), ((), ()))
LARGE = pltpu.CompilerParams(vmem_limit_bytes=16 * 1024 * 1024)
MEDIUM = pltpu.CompilerParams(vmem_limit_bytes=10 * 1024 * 1024)
SMALL = pltpu.CompilerParams(vmem_limit_bytes=4 * 1024 * 1024)


def shape(dims, dtype):
    return jax.ShapeDtypeStruct(dims, dtype)


def gelu_parts(values):
    cdf = 0.5 * (1.0 + jax.scipy.special.erf(values / math.sqrt(2.0)))
    slope = cdf + values * jnp.exp(-0.5 * values * values) / math.sqrt(2.0 * math.pi)
    return values * cdf, slope


def shift(value, axis, by):
    return lax.ppermute(value, axis, [(i, (i + by) % 4) for i in range(4)])


def swap_cores(value):
    return lax.ppermute(value, "core", [(0, 1), (1, 0)])


def near(value, axis="seq"):
    return lax.ppermute(value, axis, [(0, 1), (1, 0), (2, 3), (3, 2)])


def far(value, axis="seq"):
    return lax.ppermute(value, axis, [(0, 3), (3, 0), (1, 2), (2, 1)])


def add(one, two):
    return (one.astype(F32) + two.astype(F32)).astype(BF16)


def scatter_terms(blocks, axis):
    return [blocks[0]] + [shift(blocks[k], axis, k) for k in (1, 2, 3)]


def gather_blocks(block, axis):
    return [block] + [shift(block, axis, -k) for k in (1, 2, 3)]


def chunk(axis, k, size):
    return pl.multiple_of(((lax.axis_index(axis) + k) & 3) * size, size)


def lse_lanes(lse):
    high = lse.astype(BF16).astype(F32)
    middle = (lse - high).astype(BF16).astype(F32)
    low = lse - high - middle
    lane = lax.broadcasted_iota(jnp.int32, (lse.shape[0], 128), 1)
    lanes = jnp.where(lane == 0, high, jnp.where(lane == 1, middle, low))
    return jnp.where(lane < 3, lanes, 0.0).astype(BF16)


def lse_column(lanes):
    lanes = lanes.astype(F32)
    return lanes[:, 0:1] + lanes[:, 1:2] + lanes[:, 2:3]


def softmax_kernel(t00, t01, t10, t11, embed, logits, part, peak, total, sums):
    step = pl.program_id(0)

    @pl.when(step == 0)
    def _():
        peak[...] = jnp.full_like(peak, -jnp.inf)
        total[...] = jnp.zeros_like(total)
        sums[...] = jnp.zeros_like(sums)

    slots = embed[...]
    blocks = [[t00[0], t01[0]], [t10[0], t11[0]]]
    scores = [
        jnp.concatenate(
            [lax.dot_general(one, slots, NT, preferred_element_type=F32).T for one in pair],
            axis=1,
        )
        for pair in blocks
    ]
    for i in range(2):
        half = slice(32 * i, 32 * i + 32)
        logits[half, :] = scores[i]
        before = peak[half, :1]
        top = jnp.maximum(before, jnp.max(scores[i], axis=1, keepdims=True))
        scale = jnp.exp(before - top)
        weight = jnp.exp(scores[i] - top)
        new_total = total[half, :1] * scale + jnp.sum(weight, axis=1, keepdims=True)
        weight = weight.astype(BF16)
        new_sums = sums[half, :] * scale
        for n in range(2):
            new_sums = new_sums + jnp.dot(
                weight[:, 256 * n : 256 * n + 256], blocks[i][n], preferred_element_type=F32
            )
        peak[half, :] = jnp.broadcast_to(top, (32, 128))
        total[half, :] = jnp.broadcast_to(new_total, (32, 128))
        sums[half, :] = new_sums

        @pl.when(step == pl.num_programs(0) - 1)
        def _():
            part[half, :1280] = (new_sums / new_total).astype(BF16)
            part[half, 1280:] = lse_lanes(top + jnp.log(new_total))


def in_hbm(value):
    return pltpu.with_memory_space_constraint(value, pltpu.HBM)


def local_softmax(tokens, embed):
    return pl.pallas_call(
        softmax_kernel,
        grid=(2,),
        in_specs=[
            pl.BlockSpec((1, 256, 1280), lambda t: (0, 2 * t, 0)),
            pl.BlockSpec((1, 256, 1280), lambda t: (0, 2 * t + 1, 0)),
            pl.BlockSpec((1, 256, 1280), lambda t: (1, 2 * t, 0)),
            pl.BlockSpec((1, 256, 1280), lambda t: (1, 2 * t + 1, 0)),
            pl.BlockSpec((32, 1280), lambda t: (0, 0)),
        ],
        out_specs=[
            pl.BlockSpec((64, 512), lambda t: (0, t)),
            pl.BlockSpec((64, 1408), lambda t: (0, 0)),
        ],
        out_shape=[shape((64, 1024), F32), shape((64, 1408), BF16)],
        scratch_shapes=[
            pltpu.VMEM((64, 128), F32),
            pltpu.VMEM((64, 128), F32),
            pltpu.VMEM((64, 1280), F32),
        ],
        cost_estimate=pl.CostEstimate(flops=700_000_000, bytes_accessed=6_000_000, transcendentals=65536),
        compiler_params=LARGE,
        name="local_softmax",
    )(*[in_hbm(tokens)] * 4, embed)


def merge_kernel(one, two, sums, lse):
    lse_a, lse_b = lse_column(one[:, 1280:]), lse_column(two[:, 1280:])
    top = jnp.maximum(lse_a, lse_b)
    weight_a, weight_b = jnp.exp(lse_a - top), jnp.exp(lse_b - top)
    total = weight_a + weight_b
    part = (weight_a / total) * one[:, :1280].astype(F32)
    part = part + (weight_b / total) * two[:, :1280].astype(F32)
    lse_all = top + jnp.log(total)
    sums[:, :1280] = part.astype(BF16)
    if lse is None:
        sums[:, 1280:] = lse_lanes(lse_all)
    else:
        lse[...] = jnp.broadcast_to(lse_all, lse.shape)


def merge_pair(one, two):
    return pl.pallas_call(
        lambda a, b, out: merge_kernel(a, b, out, None),
        out_shape=shape((64, 1408), BF16),
        cost_estimate=pl.CostEstimate(flops=300_000, bytes_accessed=540_000, transcendentals=256),
        compiler_params=SMALL,
        name="merge_pair",
    )(one, two)


def merge_last(one, two):
    return pl.pallas_call(
        merge_kernel,
        out_shape=[shape((64, 1280), BF16), shape((64, 128), F32)],
        cost_estimate=pl.CostEstimate(flops=300_000, bytes_accessed=540_000, transcendentals=256),
        compiler_params=SMALL,
        name="merge_last",
    )(one, two)


def combine_grad_kernel(gout, sum_a, sum_b, comb, grad, row):
    slot_out = add(sum_a[...], sum_b[...])
    value = lax.dot_general(gout[0], slot_out, NT, preferred_element_type=F32).T
    grad[...] = value
    row[0] = jnp.sum(comb[...].astype(F32) * value, axis=0, keepdims=True)


def combine_grad(grad_out, sum_a, sum_b, comb):
    return pl.pallas_call(
        combine_grad_kernel,
        grid=(2, 2),
        in_specs=[
            pl.BlockSpec((1, 512, 1280), lambda i, t: (i, t, 0)),
            pl.BlockSpec((32, 1280), lambda i, t: (i, 0)),
            pl.BlockSpec((32, 1280), lambda i, t: (i, 0)),
            pl.BlockSpec((32, 512), lambda i, t: (i, t)),
        ],
        out_specs=[
            pl.BlockSpec((32, 512), lambda i, t: (i, t)),
            pl.BlockSpec((1, 1, 512), lambda i, t: (i, 0, t)),
        ],
        out_shape=[shape((64, 1024), F32), shape((2, 1, 1024), F32)],
        cost_estimate=pl.CostEstimate(flops=350_000_000, bytes_accessed=6_000_000, transcendentals=0),
        compiler_params=MEDIUM,
        name="combine_grad",
    )(grad_out, sum_a, sum_b, comb)


def dispatch_grad_kernel(tok, gslot, slot_in, logits, lse, comb, gcomb, full, c0, c1, c2, c3, all_weight):
    rows = gslot[...]
    col_dot = jnp.sum(slot_in[...].astype(F32) * rows.astype(F32), axis=1, keepdims=True)
    grad = lax.dot_general(tok[0], rows, NT, preferred_element_type=F32).T
    weight = jnp.exp(logits[...] - lse[:, :1])
    full[...] = weight * (grad - col_dot) + comb[...].astype(F32) * gcomb[...]
    all_weight[...] = weight
    for k, out in enumerate((c0, c1, c2, c3)):
        piece = pl.ds(chunk("y", k, 256), 256)
        out[:, :1280] = rows
        out[:, 1280:1536] = full[:, piece].astype(BF16)
        out[:, 1536:] = all_weight[:, piece].astype(BF16)


def dispatch_grad(tokens, gslot, slot_in, logits, lse, comb, gcomb):
    rows = pl.BlockSpec((32, 1280), lambda i: (i, 0))
    wide = pl.BlockSpec((32, 1024), lambda i: (i, 0))
    part = pl.BlockSpec((32, 1792), lambda i: (i, 0))
    return pl.pallas_call(
        dispatch_grad_kernel,
        grid=(2,),
        in_specs=[
            pl.BlockSpec((1, 1024, 1280), lambda i: (i, 0, 0)),
            rows,
            rows,
            wide,
            pl.BlockSpec((32, 128), lambda i: (i, 0)),
            wide,
            wide,
        ],
        out_specs=[wide] + [part] * 4,
        out_shape=[shape((64, 1024), F32)] + [shape((64, 1792), BF16)] * 4,
        scratch_shapes=[pltpu.VMEM((32, 1024), F32)],
        cost_estimate=pl.CostEstimate(flops=350_000_000, bytes_accessed=7_000_000, transcendentals=65536),
        compiler_params=MEDIUM,
        name="dispatch_grad",
    )(tokens, gslot, slot_in, logits, lse, comb, gcomb)


def inputs_kernel(comb, embed, o0, o1, o2, o3):
    for k, out in enumerate((o0, o1, o2, o3)):
        out[:64, :] = comb[:, pl.ds(chunk("y", k, 256), 256)]
        for n in range(5):
            out[64 + 32 * n : 96 + 32 * n, :] = embed[:, 256 * n : 256 * n + 256]


def input_blocks(comb, embed):
    return pl.pallas_call(
        inputs_kernel,
        out_shape=[shape((224, 256), BF16)] * 4,
        cost_estimate=pl.CostEstimate(flops=0, bytes_accessed=700_000, transcendentals=0),
        compiler_params=SMALL,
        name="input_blocks",
    )(comb, embed)


def embed_grad_kernel(tok, partial_logits, comb, row_dot, out, sums):
    grad = partial_logits[...] - comb[...].astype(F32) * row_dot[0]
    value = jnp.dot(grad.astype(BF16), tok[0], preferred_element_type=F32)

    @pl.when(pl.program_id(0) == 0)
    def _():
        sums[...] = value

    @pl.when(pl.program_id(0) == 1)
    def _():
        out[...] = (sums[...] + value).astype(BF16)


def embed_grad(tokens, partial_logits, comb, row_dot):
    wide = pl.BlockSpec((32, 1024), lambda i: (i, 0))
    return pl.pallas_call(
        embed_grad_kernel,
        grid=(2,),
        in_specs=[
            pl.BlockSpec((1, 1024, 1280), lambda i: (i, 0, 0)),
            wide,
            wide,
            pl.BlockSpec((1, 1, 1024), lambda i: (i, 0, 0)),
        ],
        out_specs=pl.BlockSpec((32, 1280), lambda i: (0, 0)),
        out_shape=shape((32, 1280), BF16),
        scratch_shapes=[pltpu.VMEM((32, 1280), F32)],
        cost_estimate=pl.CostEstimate(flops=170_000_000, bytes_accessed=6_000_000, transcendentals=0),
        compiler_params=MEDIUM,
        name="embed_grad",
    )(tokens, partial_logits, comb, row_dot)


def rows_kernel(*refs):
    parts, inputs = refs[:4], refs[4:8]
    row_dot, mine, other, scratch = refs[8:]
    core = lax.axis_index("core")
    embeds = [
        jnp.concatenate([one[64 + 32 * n : 96 + 32 * n, :] for n in range(5)], axis=1)
        for one in inputs
    ]
    for i in range(2):
        half = slice(32 * i, 32 * i + 32)
        dots = row_dot[i, :, pl.ds(chunk("y", 0, 256), 256)]
        weights = [one[half, 1536:] for one in parts] + [
            (p[half, 1280:1536].astype(F32) - c[half, :].astype(F32) * dots).astype(BF16)
            for p, c in zip(parts, inputs)
        ]
        rows = [one[half, :1280] for one in parts] + embeds
        scratch[i] = lax.dot_general(
            jnp.concatenate(weights), jnp.concatenate(rows), TN, preferred_element_type=F32
        )
        for k in range(4):
            base = ((lax.axis_index("x") + k) & 3) * 64
            here = pl.multiple_of(base + core * 32, 32)
            there = pl.multiple_of(base + (1 - core) * 32, 32)
            mine[k, i] = scratch[i, pl.ds(here, 32), :].astype(BF16)
            other[k, i] = scratch[i, pl.ds(there, 32), :].astype(BF16)


def patch_rows(parts, inputs, row_dot):
    return pl.pallas_call(
        rows_kernel,
        out_shape=[shape((4, 2, 32, 1280), BF16)] * 2,
        scratch_shapes=[pltpu.VMEM((2, 256, 1280), F32)],
        cost_estimate=pl.CostEstimate(flops=335_000_000, bytes_accessed=3_000_000, transcendentals=0),
        compiler_params=MEDIUM,
        name="patch_rows",
    )(*parts, *inputs, row_dot)


def add_kernel(mine, other, o0, o1, o2, o3):
    for k, out in enumerate((o0, o1, o2, o3)):
        out[...] = add(mine[k], other[k])


def add_cores(mine, other):
    return pl.pallas_call(
        add_kernel,
        out_shape=[shape((2, 32, 1280), BF16)] * 4,
        cost_estimate=pl.CostEstimate(flops=327_680, bytes_accessed=2_000_000, transcendentals=0),
        compiler_params=SMALL,
        name="add_cores",
    )(mine, other)


def after(value, *others):
    return lax.optimization_barrier((value, *others))[0]


def sources(terms):
    return [terms[0], terms[3], terms[2], terms[1]]


def local(tokens, slot_embed, combine, w_in, w_out, grad_out):
    w_in, w_out = w_in[0], w_out[0]
    embed = slot_embed.T
    comb = jnp.transpose(combine, (0, 2, 1)).reshape(64, 1024)

    logits, part = local_softmax(tokens, embed)
    comb_late = after(comb, part)
    out_part = jnp.einsum(
        "ijt,itd->ijd", comb_late.reshape(2, 32, 1024), grad_out, preferred_element_type=F32
    )
    out_part = out_part.astype(BF16).reshape(64, 1280)
    part_other = near(part)
    part, out_part = lax.optimization_barrier((part, out_part))
    out_other = far(out_part)
    part = merge_pair(part, part_other)
    comb_late = after(comb_late, part)
    slot_in, lse = merge_last(part, far(part))
    inputs = input_blocks(comb_late, embed)
    out_part = add(after(out_part, inputs[0]), out_other)
    inputs = sources(scatter_terms(inputs, "y"))
    grad_slot_out = add(out_part, near(out_part))

    pre_act = jnp.dot(slot_in, w_in, preferred_element_type=F32)
    act, slope = gelu_parts(pre_act)
    act = act.astype(BF16)
    out_sum = jnp.dot(act, w_out, preferred_element_type=F32).astype(BF16)
    grad_slot_out = after(grad_slot_out, out_sum)
    out_sum = add(out_sum, near(out_sum))
    out_sum = after(out_sum, *inputs)
    sum_other = far(out_sum)
    grad_act = jnp.einsum("sd,hd->sh", grad_slot_out, w_out, preferred_element_type=F32)
    grad_pre = (grad_act * slope).astype(BF16)
    in_sum = jnp.einsum("sh,dh->sd", grad_pre, w_in, preferred_element_type=F32).astype(BF16)
    in_sum = after(in_sum, out_sum)
    in_sum = add(in_sum, far(in_sum))
    in_other = near(in_sum)

    grad_combine, row_dot = combine_grad(grad_out, out_sum, sum_other, comb)
    grad_slot_in = add(after(in_sum, row_dot), in_other)
    row_dot = row_dot + swap_cores(row_dot)
    late, row_dot = lax.optimization_barrier((grad_slot_in, row_dot))
    row_dot = row_dot + near(row_dot, "x")
    row_dot = row_dot + far(row_dot, "x")
    row_dot = row_dot + near(row_dot, "y")
    row_dot = row_dot + far(row_dot, "y")

    partial_logits, *parts = dispatch_grad(
        tokens, late, slot_in, logits, lse, comb, grad_combine
    )
    parts = sources(scatter_terms(parts, "y"))

    mine, other = patch_rows(parts, inputs, row_dot)
    other_core = swap_cores(other)

    partial_logits, mine = lax.optimization_barrier((partial_logits, mine))
    embed_part = embed_grad(tokens, partial_logits, comb, row_dot)
    embed_other = near(embed_part)
    sums = add_cores(mine, other_core)
    terms = scatter_terms(sums, "x")
    grad_tokens = sum(term.astype(F32) for term in terms).astype(BF16)
    act_late, slot_late = lax.optimization_barrier((act, slot_in, sums[0]))[:2]
    grad_w_out = jnp.einsum("sh,sd->hd", act_late, grad_slot_out, preferred_element_type=F32)
    grad_w_out = grad_w_out.astype(BF16)
    grad_w_in = jnp.einsum("sd,sh->dh", slot_late, grad_pre, preferred_element_type=F32)

    embed_part = add(after(embed_part, grad_w_out), embed_other)
    embed_sum = add(embed_part, far(embed_part))
    z = lax.axis_index("seq")
    grad_embed = lax.dynamic_slice_in_dim(embed_sum, z * 320, 320, axis=1).T
    return (
        grad_tokens,
        grad_embed,
        grad_w_in.astype(BF16)[None],
        grad_w_out[None],
    )


def solution(mesh):
    fine = Mesh(mesh.devices.reshape(4, 4, 4, 2), ("seq", "y", "x", "core"))
    expert = ("y", "x", "core")
    return jax.shard_map(
        local,
        mesh=fine,
        in_specs=(
            P(None, "seq", None),
            P(None, expert),
            P(None, "seq", expert),
            P(expert, None, "seq"),
            P(expert, "seq", None),
            P(None, "seq", None),
        ),
        out_specs=(
            P(None, ("seq", *expert), None),
            P("seq", expert),
            P(expert, None, "seq"),
            P(expert, "seq", None),
        ),
        check_vma=False,
    )
```

```python
import math

import jax
import jax.numpy as jnp
from jax import lax
from jax.experimental import pallas as pl
from jax.experimental.pallas import tpu as pltpu
from jax.sharding import Mesh, PartitionSpec as P

F32 = jnp.float32
BF16 = jnp.bfloat16
NT = (((1,), (1,)), ((), ()))
TN = (((0,), (0,)), ((), ()))
LARGE = pltpu.CompilerParams(vmem_limit_bytes=16 * 1024 * 1024)
MEDIUM = pltpu.CompilerParams(vmem_limit_bytes=10 * 1024 * 1024)
SMALL = pltpu.CompilerParams(vmem_limit_bytes=4 * 1024 * 1024)


def shape(dims, dtype):
    return jax.ShapeDtypeStruct(dims, dtype)


def gelu_parts(values):
    cdf = 0.5 * (1.0 + jax.scipy.special.erf(values / math.sqrt(2.0)))
    slope = cdf + values * jnp.exp(-0.5 * values * values) / math.sqrt(2.0 * math.pi)
    return values * cdf, slope


def shift(value, axis, by):
    return lax.ppermute(value, axis, [(i, (i + by) % 4) for i in range(4)])


def swap_cores(value):
    return lax.ppermute(value, "core", [(0, 1), (1, 0)])


def near(value, axis="seq"):
    return lax.ppermute(value, axis, [(0, 1), (1, 0), (2, 3), (3, 2)])


def far(value, axis="seq"):
    return lax.ppermute(value, axis, [(0, 3), (3, 0), (1, 2), (2, 1)])


def add(one, two):
    return (one.astype(F32) + two.astype(F32)).astype(BF16)


def scatter_terms(blocks, axis):
    return [blocks[0]] + [shift(blocks[k], axis, k) for k in (1, 2, 3)]


def gather_blocks(block, axis):
    return [block] + [shift(block, axis, -k) for k in (1, 2, 3)]


def chunk(axis, k, size):
    return pl.multiple_of(((lax.axis_index(axis) + k) & 3) * size, size)


def lse_lanes(lse):
    high = lse.astype(BF16).astype(F32)
    middle = (lse - high).astype(BF16).astype(F32)
    low = lse - high - middle
    lane = lax.broadcasted_iota(jnp.int32, (lse.shape[0], 128), 1)
    lanes = jnp.where(lane == 0, high, jnp.where(lane == 1, middle, low))
    return jnp.where(lane < 3, lanes, 0.0).astype(BF16)


def lse_column(lanes):
    lanes = lanes.astype(F32)
    return lanes[:, 0:1] + lanes[:, 1:2] + lanes[:, 2:3]


def softmax_kernel(t00, t01, t10, t11, embed, logits, part, peak, total, sums):
    step = pl.program_id(0)

    @pl.when(step == 0)
    def _():
        peak[...] = jnp.full_like(peak, -jnp.inf)
        total[...] = jnp.zeros_like(total)
        sums[...] = jnp.zeros_like(sums)

    slots = embed[...]
    blocks = [[t00[0], t01[0]], [t10[0], t11[0]]]
    scores = [
        jnp.concatenate(
            [lax.dot_general(one, slots, NT, preferred_element_type=F32).T for one in pair],
            axis=1,
        )
        for pair in blocks
    ]
    for i in range(2):
        half = slice(32 * i, 32 * i + 32)
        logits[half, :] = scores[i]
        before = peak[half, :1]
        top = jnp.maximum(before, jnp.max(scores[i], axis=1, keepdims=True))
        scale = jnp.exp(before - top)
        weight = jnp.exp(scores[i] - top)
        new_total = total[half, :1] * scale + jnp.sum(weight, axis=1, keepdims=True)
        weight = weight.astype(BF16)
        new_sums = sums[half, :] * scale
        for n in range(2):
            new_sums = new_sums + jnp.dot(
                weight[:, 256 * n : 256 * n + 256], blocks[i][n], preferred_element_type=F32
            )
        peak[half, :] = jnp.broadcast_to(top, (32, 128))
        total[half, :] = jnp.broadcast_to(new_total, (32, 128))
        sums[half, :] = new_sums

        @pl.when(step == pl.num_programs(0) - 1)
        def _():
            part[half, :1280] = (new_sums / new_total).astype(BF16)
            part[half, 1280:] = lse_lanes(top + jnp.log(new_total))


def in_hbm(value):
    return pltpu.with_memory_space_constraint(value, pltpu.HBM)


def local_softmax(tokens, embed):
    return pl.pallas_call(
        softmax_kernel,
        grid=(2,),
        in_specs=[
            *patch_streams(),
            pl.BlockSpec((32, 1280), lambda t: (0, 0)),
        ],
        out_specs=[
            pl.BlockSpec((64, 512), lambda t: (0, t)),
            pl.BlockSpec((64, 1408), lambda t: (0, 0)),
        ],
        out_shape=[shape((64, 1024), F32), shape((64, 1408), BF16)],
        scratch_shapes=[
            pltpu.VMEM((64, 128), F32),
            pltpu.VMEM((64, 128), F32),
            pltpu.VMEM((64, 1280), F32),
        ],
        cost_estimate=pl.CostEstimate(flops=700_000_000, bytes_accessed=6_000_000, transcendentals=65536),
        compiler_params=LARGE,
        name="local_softmax",
    )(*[in_hbm(tokens)] * 4, in_hbm(embed))


def merge_kernel(one, two, sums, lse):
    lse_a, lse_b = lse_column(one[:, 1280:]), lse_column(two[:, 1280:])
    top = jnp.maximum(lse_a, lse_b)
    weight_a, weight_b = jnp.exp(lse_a - top), jnp.exp(lse_b - top)
    total = weight_a + weight_b
    part = (weight_a / total) * one[:, :1280].astype(F32)
    part = part + (weight_b / total) * two[:, :1280].astype(F32)
    lse_all = top + jnp.log(total)
    sums[:, :1280] = part.astype(BF16)
    if lse is None:
        sums[:, 1280:] = lse_lanes(lse_all)
    else:
        lse[...] = jnp.broadcast_to(lse_all, lse.shape)


def merge_pair(one, two):
    return pl.pallas_call(
        lambda a, b, out: merge_kernel(a, b, out, None),
        out_shape=shape((64, 1408), BF16),
        cost_estimate=pl.CostEstimate(flops=300_000, bytes_accessed=540_000, transcendentals=256),
        compiler_params=SMALL,
        name="merge_pair",
    )(one, two)


def merge_last(one, two):
    return pl.pallas_call(
        merge_kernel,
        out_shape=[shape((64, 1280), BF16), shape((64, 128), F32)],
        cost_estimate=pl.CostEstimate(flops=300_000, bytes_accessed=540_000, transcendentals=256),
        compiler_params=SMALL,
        name="merge_last",
    )(one, two)


def combine_grad_kernel(gout, sum_a, sum_b, comb, grad, row):
    slot_out = add(sum_a[...], sum_b[...])
    value = lax.dot_general(gout[0], slot_out, NT, preferred_element_type=F32).T
    grad[...] = value
    row[0] = jnp.sum(comb[...].astype(F32) * value, axis=0, keepdims=True)


def combine_grad(grad_out, sum_a, sum_b, comb):
    return pl.pallas_call(
        combine_grad_kernel,
        grid=(2, 2),
        in_specs=[
            pl.BlockSpec((1, 512, 1280), lambda i, t: (i, t, 0)),
            pl.BlockSpec((32, 1280), lambda i, t: (i, 0)),
            pl.BlockSpec((32, 1280), lambda i, t: (i, 0)),
            pl.BlockSpec((32, 512), lambda i, t: (i, t)),
        ],
        out_specs=[
            pl.BlockSpec((32, 512), lambda i, t: (i, t)),
            pl.BlockSpec((1, 1, 512), lambda i, t: (i, 0, t)),
        ],
        out_shape=[shape((64, 1024), F32), shape((2, 1, 1024), F32)],
        cost_estimate=pl.CostEstimate(flops=350_000_000, bytes_accessed=6_000_000, transcendentals=0),
        compiler_params=MEDIUM,
        name="combine_grad",
    )(grad_out, sum_a, sum_b, comb)


def dispatch_grad_kernel(tok, gslot, slot_in, logits, lse, comb, gcomb, full, c0, c1, c2, c3, all_weight):
    rows = gslot[...]
    col_dot = jnp.sum(slot_in[...].astype(F32) * rows.astype(F32), axis=1, keepdims=True)
    grad = lax.dot_general(tok[0], rows, NT, preferred_element_type=F32).T
    weight = jnp.exp(logits[...] - lse[:, :1])
    full[...] = weight * (grad - col_dot) + comb[...].astype(F32) * gcomb[...]
    all_weight[...] = weight
    for k, out in enumerate((c0, c1, c2, c3)):
        piece = pl.ds(chunk("y", k, 256), 256)
        out[:, :1280] = rows
        out[:, 1280:1536] = full[:, piece].astype(BF16)
        out[:, 1536:] = all_weight[:, piece].astype(BF16)


def dispatch_grad(tokens, gslot, slot_in, logits, lse, comb, gcomb):
    rows = pl.BlockSpec((32, 1280), lambda i: (i, 0))
    wide = pl.BlockSpec((32, 1024), lambda i: (i, 0))
    part = pl.BlockSpec((32, 1792), lambda i: (i, 0))
    return pl.pallas_call(
        dispatch_grad_kernel,
        grid=(2,),
        in_specs=[
            pl.BlockSpec((1, 1024, 1280), lambda i: (i, 0, 0)),
            rows,
            rows,
            wide,
            pl.BlockSpec((32, 128), lambda i: (i, 0)),
            wide,
            wide,
        ],
        out_specs=[wide] + [part] * 4,
        out_shape=[shape((64, 1024), F32)] + [shape((64, 1792), BF16)] * 4,
        scratch_shapes=[pltpu.VMEM((32, 1024), F32)],
        cost_estimate=pl.CostEstimate(flops=350_000_000, bytes_accessed=7_000_000, transcendentals=65536),
        compiler_params=MEDIUM,
        name="dispatch_grad",
    )(tokens, gslot, slot_in, logits, lse, comb, gcomb)


def inputs_kernel(comb, embed, o0, o1, o2, o3):
    for k, out in enumerate((o0, o1, o2, o3)):
        out[:64, :] = comb[:, pl.ds(chunk("y", k, 256), 256)]
        for n in range(5):
            out[64 + 32 * n : 96 + 32 * n, :] = embed[:, 256 * n : 256 * n + 256]


def input_blocks(comb, embed):
    return pl.pallas_call(
        inputs_kernel,
        out_shape=[shape((224, 256), BF16)] * 4,
        cost_estimate=pl.CostEstimate(flops=0, bytes_accessed=700_000, transcendentals=0),
        compiler_params=SMALL,
        name="input_blocks",
    )(comb, embed)


def embed_grad_kernel(t00, t01, t10, t11, partial_logits, comb, row_dot, out, sums):
    value = 0.0
    for i, pair in enumerate(((t00, t01), (t10, t11))):
        half = slice(32 * i, 32 * i + 32)
        grad = partial_logits[half, :] - comb[half, :].astype(F32) * row_dot[i]
        grad = grad.astype(BF16)
        for n in range(2):
            value = value + jnp.dot(
                grad[:, 256 * n : 256 * n + 256], pair[n][0], preferred_element_type=F32
            )

    @pl.when(pl.program_id(0) == 0)
    def _():
        sums[...] = value

    @pl.when(pl.program_id(0) == 1)
    def _():
        out[...] = (sums[...] + value).astype(BF16)


def patch_streams():
    return [
        pl.BlockSpec((1, 256, 1280), lambda t, i=i, n=n: (i, 2 * t + n, 0))
        for i in range(2)
        for n in range(2)
    ]


def embed_grad(tokens, partial_logits, comb, row_dot):
    wide = pl.BlockSpec((64, 512), lambda t: (0, t))
    return pl.pallas_call(
        embed_grad_kernel,
        grid=(2,),
        in_specs=[*patch_streams(), wide, wide, pl.BlockSpec((2, 1, 512), lambda t: (0, 0, t))],
        out_specs=pl.BlockSpec((32, 1280), lambda t: (0, 0)),
        out_shape=shape((32, 1280), BF16),
        scratch_shapes=[pltpu.VMEM((32, 1280), F32)],
        cost_estimate=pl.CostEstimate(flops=170_000_000, bytes_accessed=6_000_000, transcendentals=0),
        compiler_params=MEDIUM,
        name="embed_grad",
    )(*[in_hbm(tokens)] * 4, partial_logits, comb, row_dot)


def rows_kernel(*refs):
    parts, inputs = refs[:4], refs[4:8]
    row_dot, mine, other, scratch = refs[8:]
    core = lax.axis_index("core")
    embeds = [
        jnp.concatenate([one[64 + 32 * n : 96 + 32 * n, :] for n in range(5)], axis=1)
        for one in inputs
    ]
    for i in range(2):
        half = slice(32 * i, 32 * i + 32)
        dots = row_dot[i, :, pl.ds(chunk("y", 0, 256), 256)]
        weights = [one[half, 1536:] for one in parts] + [
            (p[half, 1280:1536].astype(F32) - c[half, :].astype(F32) * dots).astype(BF16)
            for p, c in zip(parts, inputs)
        ]
        rows = [one[half, :1280] for one in parts] + embeds
        scratch[i] = lax.dot_general(
            jnp.concatenate(weights), jnp.concatenate(rows), TN, preferred_element_type=F32
        )
        for k in range(4):
            base = ((lax.axis_index("x") + k) & 3) * 64
            here = pl.multiple_of(base + core * 32, 32)
            there = pl.multiple_of(base + (1 - core) * 32, 32)
            mine[k, i] = scratch[i, pl.ds(here, 32), :].astype(BF16)
            other[k, i] = scratch[i, pl.ds(there, 32), :].astype(BF16)


def patch_rows(parts, inputs, row_dot):
    return pl.pallas_call(
        rows_kernel,
        out_shape=[shape((4, 2, 32, 1280), BF16)] * 2,
        scratch_shapes=[pltpu.VMEM((2, 256, 1280), F32)],
        cost_estimate=pl.CostEstimate(flops=335_000_000, bytes_accessed=3_000_000, transcendentals=0),
        compiler_params=MEDIUM,
        name="patch_rows",
    )(*parts, *inputs, row_dot)


def add_kernel(mine, other, o0, o1, o2, o3):
    for k, out in enumerate((o0, o1, o2, o3)):
        out[...] = add(mine[k], other[k])


def add_cores(mine, other):
    return pl.pallas_call(
        add_kernel,
        out_shape=[shape((2, 32, 1280), BF16)] * 4,
        cost_estimate=pl.CostEstimate(flops=327_680, bytes_accessed=2_000_000, transcendentals=0),
        compiler_params=SMALL,
        name="add_cores",
    )(mine, other)


def after(value, *others):
    return lax.optimization_barrier((value, *others))[0]


def sources(terms):
    return [terms[0], terms[3], terms[2], terms[1]]


def local(tokens, slot_embed, combine, w_in, w_out, grad_out):
    w_in, w_out = w_in[0], w_out[0]
    embed = slot_embed.T
    comb = jnp.transpose(combine, (0, 2, 1)).reshape(64, 1024)

    logits, part = local_softmax(tokens, embed)
    comb_late = after(comb, part)
    out_part = jnp.einsum(
        "ijt,itd->ijd", comb_late.reshape(2, 32, 1024), grad_out, preferred_element_type=F32
    )
    out_part = out_part.astype(BF16).reshape(64, 1280)
    part_other = near(part)
    part, out_part = lax.optimization_barrier((part, out_part))
    out_other = near(out_part)
    part = merge_pair(part, part_other)
    comb_late = after(comb_late, part)
    slot_in, lse = merge_last(part, far(part))
    inputs = sources(scatter_terms(input_blocks(comb_late, embed), "y"))
    out_part = add(after(out_part, slot_in), out_other)
    grad_slot_out = add(out_part, far(out_part))

    pre_act = jnp.dot(slot_in, w_in, preferred_element_type=F32)
    act, slope = gelu_parts(pre_act)
    act = act.astype(BF16)
    out_sum = jnp.dot(act, w_out, preferred_element_type=F32).astype(BF16)
    grad_slot_out = after(grad_slot_out, out_sum)
    out_sum = add(out_sum, near(out_sum))
    out_sum = after(out_sum, *inputs)
    sum_other = far(out_sum)
    grad_act = jnp.einsum("sd,hd->sh", grad_slot_out, w_out, preferred_element_type=F32)
    grad_pre = (grad_act * slope).astype(BF16)
    in_sum = jnp.einsum("sh,dh->sd", grad_pre, w_in, preferred_element_type=F32).astype(BF16)
    in_sum, act_late, slots_late = lax.optimization_barrier(
        (in_sum, act, grad_slot_out, out_sum)
    )[:3]
    in_other = near(in_sum)
    grad_w_out = jnp.einsum("sh,sd->hd", act_late, slots_late, preferred_element_type=F32)
    grad_w_out = grad_w_out.astype(BF16)
    in_sum = add(after(in_sum, grad_w_out), in_other)
    in_other = far(in_sum)

    grad_combine, row_dot = combine_grad(grad_out, out_sum, sum_other, comb)
    grad_slot_in = add(after(in_sum, row_dot), in_other)
    row_dot = row_dot + swap_cores(row_dot)
    late, row_dot = lax.optimization_barrier((grad_slot_in, row_dot))
    row_dot = row_dot + near(row_dot, "x")
    row_dot = row_dot + far(row_dot, "x")
    row_dot = row_dot + near(row_dot, "y")
    row_dot = row_dot + far(row_dot, "y")

    partial_logits, *parts = dispatch_grad(
        tokens, late, slot_in, logits, lse, comb, grad_combine
    )
    parts = sources(scatter_terms(parts, "y"))

    mine, other = patch_rows(parts, inputs, row_dot)
    other_core = swap_cores(other)

    partial_logits, mine = lax.optimization_barrier((partial_logits, mine))
    embed_part = embed_grad(tokens, partial_logits, comb, row_dot)
    embed_other = near(embed_part)
    sums = add_cores(after(mine, embed_part), other_core)
    terms = scatter_terms(sums, "x")
    grad_tokens = sum(term.astype(F32) for term in terms).astype(BF16)
    slot_late = after(slot_in, sums[0])
    grad_w_in = jnp.einsum("sd,sh->dh", slot_late, grad_pre, preferred_element_type=F32)
    grad_w_in = grad_w_in.astype(BF16)

    embed_part = add(after(embed_part, terms[1]), embed_other)
    embed_sum = add(embed_part, far(embed_part))
    z = lax.axis_index("seq")
    grad_embed = lax.dynamic_slice_in_dim(embed_sum, z * 320, 320, axis=1).T
    return (
        grad_tokens,
        grad_embed,
        grad_w_in[None],
        grad_w_out[None],
    )


def solution(mesh):
    fine = Mesh(mesh.devices.reshape(4, 4, 4, 2), ("seq", "y", "x", "core"))
    expert = ("y", "x", "core")
    return jax.shard_map(
        local,
        mesh=fine,
        in_specs=(
            P(None, "seq", None),
            P(None, expert),
            P(None, "seq", expert),
            P(expert, None, "seq"),
            P(expert, "seq", None),
            P(None, "seq", None),
        ),
        out_specs=(
            P(None, ("seq", *expert), None),
            P("seq", expert),
            P(expert, None, "seq"),
            P(expert, "seq", None),
        ),
        check_vma=False,
    )
```

```python
import math

import jax
import jax.numpy as jnp
from jax import lax
from jax.experimental import pallas as pl
from jax.experimental.pallas import tpu as pltpu
from jax.sharding import Mesh, PartitionSpec as P

F32 = jnp.float32
BF16 = jnp.bfloat16
NT = (((1,), (1,)), ((), ()))
TN = (((0,), (0,)), ((), ()))
LARGE = pltpu.CompilerParams(vmem_limit_bytes=16 * 1024 * 1024)
MEDIUM = pltpu.CompilerParams(vmem_limit_bytes=10 * 1024 * 1024)
SMALL = pltpu.CompilerParams(vmem_limit_bytes=4 * 1024 * 1024)


def shape(dims, dtype):
    return jax.ShapeDtypeStruct(dims, dtype)


def gelu_parts(values):
    cdf = 0.5 * (1.0 + jax.scipy.special.erf(values / math.sqrt(2.0)))
    slope = cdf + values * jnp.exp(-0.5 * values * values) / math.sqrt(2.0 * math.pi)
    return values * cdf, slope


def shift(value, axis, by):
    return lax.ppermute(value, axis, [(i, (i + by) % 4) for i in range(4)])


def swap_cores(value):
    return lax.ppermute(value, "core", [(0, 1), (1, 0)])


def near(value, axis="seq"):
    return lax.ppermute(value, axis, [(0, 1), (1, 0), (2, 3), (3, 2)])


def far(value, axis="seq"):
    return lax.ppermute(value, axis, [(0, 3), (3, 0), (1, 2), (2, 1)])


def add(one, two):
    return (one.astype(F32) + two.astype(F32)).astype(BF16)


def scatter_terms(blocks, axis):
    return [blocks[0]] + [shift(blocks[k], axis, k) for k in (1, 2, 3)]


def gather_blocks(block, axis):
    return [block] + [shift(block, axis, -k) for k in (1, 2, 3)]


def chunk(axis, k, size):
    return pl.multiple_of(((lax.axis_index(axis) + k) & 3) * size, size)


def lse_lanes(lse):
    high = lse.astype(BF16).astype(F32)
    middle = (lse - high).astype(BF16).astype(F32)
    low = lse - high - middle
    lane = lax.broadcasted_iota(jnp.int32, (lse.shape[0], 128), 1)
    lanes = jnp.where(lane == 0, high, jnp.where(lane == 1, middle, low))
    return jnp.where(lane < 3, lanes, 0.0).astype(BF16)


def lse_column(lanes):
    lanes = lanes.astype(F32)
    return lanes[:, 0:1] + lanes[:, 1:2] + lanes[:, 2:3]


def softmax_kernel(t00, t01, t10, t11, embed, logits, part, peak, total, sums):
    step = pl.program_id(0)

    @pl.when(step == 0)
    def _():
        peak[...] = jnp.full_like(peak, -jnp.inf)
        total[...] = jnp.zeros_like(total)
        sums[...] = jnp.zeros_like(sums)

    slots = embed[...]
    blocks = [[t00[0], t01[0]], [t10[0], t11[0]]]
    scores = [
        jnp.concatenate(
            [lax.dot_general(one, slots, NT, preferred_element_type=F32).T for one in pair],
            axis=1,
        )
        for pair in blocks
    ]
    for i in range(2):
        half = slice(32 * i, 32 * i + 32)
        logits[half, :] = scores[i]
        before = peak[half, :1]
        top = jnp.maximum(before, jnp.max(scores[i], axis=1, keepdims=True))
        scale = jnp.exp(before - top)
        weight = jnp.exp(scores[i] - top)
        new_total = total[half, :1] * scale + jnp.sum(weight, axis=1, keepdims=True)
        weight = weight.astype(BF16)
        new_sums = sums[half, :] * scale
        for n in range(2):
            new_sums = new_sums + jnp.dot(
                weight[:, 256 * n : 256 * n + 256], blocks[i][n], preferred_element_type=F32
            )
        peak[half, :] = jnp.broadcast_to(top, (32, 128))
        total[half, :] = jnp.broadcast_to(new_total, (32, 128))
        sums[half, :] = new_sums

        @pl.when(step == pl.num_programs(0) - 1)
        def _():
            part[half, :1280] = (new_sums / new_total).astype(BF16)
            part[half, 1280:] = lse_lanes(top + jnp.log(new_total))


def in_hbm(value):
    return pltpu.with_memory_space_constraint(value, pltpu.HBM)


def local_softmax(tokens, embed):
    return pl.pallas_call(
        softmax_kernel,
        grid=(2,),
        in_specs=[
            *patch_streams(),
            pl.BlockSpec((32, 1280), lambda t: (0, 0)),
        ],
        out_specs=[
            pl.BlockSpec((64, 512), lambda t: (0, t)),
            pl.BlockSpec((64, 1408), lambda t: (0, 0)),
        ],
        out_shape=[shape((64, 1024), F32), shape((64, 1408), BF16)],
        scratch_shapes=[
            pltpu.VMEM((64, 128), F32),
            pltpu.VMEM((64, 128), F32),
            pltpu.VMEM((64, 1280), F32),
        ],
        cost_estimate=pl.CostEstimate(flops=700_000_000, bytes_accessed=6_000_000, transcendentals=65536),
        compiler_params=LARGE,
        name="local_softmax",
    )(*[in_hbm(tokens)] * 4, in_hbm(embed))


def merge_kernel(one, two, sums, lse):
    lse_a, lse_b = lse_column(one[:, 1280:]), lse_column(two[:, 1280:])
    top = jnp.maximum(lse_a, lse_b)
    weight_a, weight_b = jnp.exp(lse_a - top), jnp.exp(lse_b - top)
    total = weight_a + weight_b
    part = (weight_a / total) * one[:, :1280].astype(F32)
    part = part + (weight_b / total) * two[:, :1280].astype(F32)
    lse_all = top + jnp.log(total)
    sums[:, :1280] = part.astype(BF16)
    if lse is None:
        sums[:, 1280:] = lse_lanes(lse_all)
    else:
        lse[...] = jnp.broadcast_to(lse_all, lse.shape)


def merge_pair(one, two):
    return pl.pallas_call(
        lambda a, b, out: merge_kernel(a, b, out, None),
        out_shape=shape((64, 1408), BF16),
        cost_estimate=pl.CostEstimate(flops=300_000, bytes_accessed=540_000, transcendentals=256),
        compiler_params=SMALL,
        name="merge_pair",
    )(one, two)


def merge_last(one, two):
    return pl.pallas_call(
        merge_kernel,
        out_shape=[shape((64, 1280), BF16), shape((64, 128), F32)],
        cost_estimate=pl.CostEstimate(flops=300_000, bytes_accessed=540_000, transcendentals=256),
        compiler_params=SMALL,
        name="merge_last",
    )(one, two)


def combine_grad_kernel(gout, sum_a, sum_b, comb, grad, row):
    slot_out = add(sum_a[...], sum_b[...])
    value = lax.dot_general(gout[0], slot_out, NT, preferred_element_type=F32).T
    grad[...] = value
    row[0] = jnp.sum(comb[...].astype(F32) * value, axis=0, keepdims=True)


def combine_grad(grad_out, sum_a, sum_b, comb):
    return pl.pallas_call(
        combine_grad_kernel,
        grid=(2, 2),
        in_specs=[
            pl.BlockSpec((1, 512, 1280), lambda i, t: (i, t, 0)),
            pl.BlockSpec((32, 1280), lambda i, t: (i, 0)),
            pl.BlockSpec((32, 1280), lambda i, t: (i, 0)),
            pl.BlockSpec((32, 512), lambda i, t: (i, t)),
        ],
        out_specs=[
            pl.BlockSpec((32, 512), lambda i, t: (i, t)),
            pl.BlockSpec((1, 1, 512), lambda i, t: (i, 0, t)),
        ],
        out_shape=[shape((64, 1024), F32), shape((2, 1, 1024), F32)],
        cost_estimate=pl.CostEstimate(flops=350_000_000, bytes_accessed=6_000_000, transcendentals=0),
        compiler_params=MEDIUM,
        name="combine_grad",
    )(grad_out, sum_a, sum_b, comb)


def dispatch_grad_kernel(tok, gslot, slot_in, logits, lse, comb, gcomb, full, c0, c1, c2, c3, all_weight):
    rows = gslot[...]
    col_dot = jnp.sum(slot_in[...].astype(F32) * rows.astype(F32), axis=1, keepdims=True)
    grad = lax.dot_general(tok[0], rows, NT, preferred_element_type=F32).T
    weight = jnp.exp(logits[...] - lse[:, :1])
    full[...] = weight * (grad - col_dot) + comb[...].astype(F32) * gcomb[...]
    all_weight[...] = weight
    for k, out in enumerate((c0, c1, c2, c3)):
        piece = pl.ds(chunk("y", k, 256), 256)
        out[:, :1280] = rows
        out[:, 1280:1536] = full[:, piece].astype(BF16)
        out[:, 1536:] = all_weight[:, piece].astype(BF16)


def dispatch_grad(tokens, gslot, slot_in, logits, lse, comb, gcomb):
    rows = pl.BlockSpec((32, 1280), lambda i: (i, 0))
    wide = pl.BlockSpec((32, 1024), lambda i: (i, 0))
    part = pl.BlockSpec((32, 1792), lambda i: (i, 0))
    return pl.pallas_call(
        dispatch_grad_kernel,
        grid=(2,),
        in_specs=[
            pl.BlockSpec((1, 1024, 1280), lambda i: (i, 0, 0)),
            rows,
            rows,
            wide,
            pl.BlockSpec((32, 128), lambda i: (i, 0)),
            wide,
            wide,
        ],
        out_specs=[wide] + [part] * 4,
        out_shape=[shape((64, 1024), F32)] + [shape((64, 1792), BF16)] * 4,
        scratch_shapes=[pltpu.VMEM((32, 1024), F32)],
        cost_estimate=pl.CostEstimate(flops=350_000_000, bytes_accessed=7_000_000, transcendentals=65536),
        compiler_params=MEDIUM,
        name="dispatch_grad",
    )(tokens, gslot, slot_in, logits, lse, comb, gcomb)


def inputs_kernel(comb, embed, o0, o1, o2, o3):
    for k, out in enumerate((o0, o1, o2, o3)):
        out[:64, :] = comb[:, pl.ds(chunk("y", k, 256), 256)]
        for n in range(5):
            out[64 + 32 * n : 96 + 32 * n, :] = embed[:, 256 * n : 256 * n + 256]


def input_blocks(comb, embed):
    return pl.pallas_call(
        inputs_kernel,
        out_shape=[shape((224, 256), BF16)] * 4,
        cost_estimate=pl.CostEstimate(flops=0, bytes_accessed=700_000, transcendentals=0),
        compiler_params=SMALL,
        name="input_blocks",
    )(comb, embed)


def embed_grad_kernel(t00, t01, t10, t11, partial_logits, comb, row_dot, out, sums):
    value = 0.0
    for i, pair in enumerate(((t00, t01), (t10, t11))):
        half = slice(32 * i, 32 * i + 32)
        grad = partial_logits[half, :] - comb[half, :].astype(F32) * row_dot[i]
        grad = grad.astype(BF16)
        for n in range(2):
            value = value + jnp.dot(
                grad[:, 256 * n : 256 * n + 256], pair[n][0], preferred_element_type=F32
            )

    @pl.when(pl.program_id(0) == 0)
    def _():
        sums[...] = value

    @pl.when(pl.program_id(0) == 1)
    def _():
        out[...] = (sums[...] + value).astype(BF16)


def patch_streams():
    return [
        pl.BlockSpec((1, 256, 1280), lambda t, i=i, n=n: (i, 2 * t + n, 0))
        for i in range(2)
        for n in range(2)
    ]


def embed_grad(tokens, partial_logits, comb, row_dot):
    wide = pl.BlockSpec((64, 512), lambda t: (0, t))
    return pl.pallas_call(
        embed_grad_kernel,
        grid=(2,),
        in_specs=[*patch_streams(), wide, wide, pl.BlockSpec((2, 1, 512), lambda t: (0, 0, t))],
        out_specs=pl.BlockSpec((32, 1280), lambda t: (0, 0)),
        out_shape=shape((32, 1280), BF16),
        scratch_shapes=[pltpu.VMEM((32, 1280), F32)],
        cost_estimate=pl.CostEstimate(flops=170_000_000, bytes_accessed=6_000_000, transcendentals=0),
        compiler_params=MEDIUM,
        name="embed_grad",
    )(*[in_hbm(tokens)] * 4, partial_logits, comb, row_dot)


def rows_kernel(*refs):
    parts, inputs = refs[:4], refs[4:8]
    row_dot, mine, other, scratch = refs[8:]
    core = lax.axis_index("core")
    embeds = [
        jnp.concatenate([one[64 + 32 * n : 96 + 32 * n, :] for n in range(5)], axis=1)
        for one in inputs
    ]
    for i in range(2):
        half = slice(32 * i, 32 * i + 32)
        dots = row_dot[i, :, pl.ds(chunk("y", 0, 256), 256)]
        weights = [one[half, 1536:] for one in parts] + [
            (p[half, 1280:1536].astype(F32) - c[half, :].astype(F32) * dots).astype(BF16)
            for p, c in zip(parts, inputs)
        ]
        rows = [one[half, :1280] for one in parts] + embeds
        scratch[i] = lax.dot_general(
            jnp.concatenate(weights), jnp.concatenate(rows), TN, preferred_element_type=F32
        )
        for k in range(4):
            base = ((lax.axis_index("x") + k) & 3) * 64
            here = pl.multiple_of(base + core * 32, 32)
            there = pl.multiple_of(base + (1 - core) * 32, 32)
            mine[k, i] = scratch[i, pl.ds(here, 32), :].astype(BF16)
            other[k, i] = scratch[i, pl.ds(there, 32), :].astype(BF16)


def patch_rows(parts, inputs, row_dot):
    return pl.pallas_call(
        rows_kernel,
        out_shape=[shape((4, 2, 32, 1280), BF16)] * 2,
        scratch_shapes=[pltpu.VMEM((2, 256, 1280), F32)],
        cost_estimate=pl.CostEstimate(flops=335_000_000, bytes_accessed=3_000_000, transcendentals=0),
        compiler_params=MEDIUM,
        name="patch_rows",
    )(*parts, *inputs, row_dot)


def add_kernel(mine, other, o0, o1, o2, o3):
    for k, out in enumerate((o0, o1, o2, o3)):
        out[...] = add(mine[k], other[k])


def add_cores(mine, other):
    return pl.pallas_call(
        add_kernel,
        out_shape=[pltpu.HBM((2, 32, 1280), BF16)] * 4,
        cost_estimate=pl.CostEstimate(flops=327_680, bytes_accessed=2_000_000, transcendentals=0),
        compiler_params=SMALL,
        name="add_cores",
    )(mine, other)


def after(value, *others):
    return lax.optimization_barrier((value, *others))[0]


def sources(terms):
    return [terms[0], terms[3], terms[2], terms[1]]


def local(tokens, slot_embed, combine, w_in, w_out, grad_out):
    w_in, w_out = w_in[0], w_out[0]
    embed = slot_embed.T
    comb = jnp.transpose(combine, (0, 2, 1)).reshape(64, 1024)

    logits, part = local_softmax(tokens, embed)
    comb_late = after(comb, part)
    out_part = jnp.einsum(
        "ijt,itd->ijd", comb_late.reshape(2, 32, 1024), grad_out, preferred_element_type=F32
    )
    out_part = out_part.astype(BF16).reshape(64, 1280)
    part_other = near(part)
    part, out_part = lax.optimization_barrier((part, out_part))
    out_other = near(out_part)
    part = merge_pair(part, part_other)
    comb_late = after(comb_late, part)
    slot_in, lse = merge_last(part, far(part))
    inputs = list(input_blocks(comb_late, embed))
    out_part = add(after(out_part, slot_in), out_other)
    grad_slot_out = add(out_part, far(out_part))

    pre_act = jnp.dot(slot_in, w_in, preferred_element_type=F32)
    act, slope = gelu_parts(pre_act)
    act = act.astype(BF16)
    out_sum = jnp.dot(act, w_out, preferred_element_type=F32).astype(BF16)
    grad_slot_out = after(grad_slot_out, out_sum)
    inputs[3] = after(inputs[3], out_sum)
    inputs = sources(scatter_terms(inputs, "y"))
    out_sum = add(out_sum, near(out_sum))
    out_sum = after(out_sum, *inputs)
    sum_other = far(out_sum)
    grad_act = jnp.einsum("sd,hd->sh", grad_slot_out, w_out, preferred_element_type=F32)
    grad_pre = (grad_act * slope).astype(BF16)
    in_sum = jnp.einsum("sh,dh->sd", grad_pre, w_in, preferred_element_type=F32).astype(BF16)
    in_sum, act_late, slots_late = lax.optimization_barrier(
        (in_sum, act, grad_slot_out, out_sum)
    )[:3]
    in_other = near(in_sum)
    grad_w_out = jnp.einsum("sh,sd->hd", act_late, slots_late, preferred_element_type=F32)
    grad_w_out = grad_w_out.astype(BF16)
    in_sum = add(after(in_sum, grad_w_out), in_other)
    in_other = far(in_sum)

    grad_combine, row_dot = combine_grad(grad_out, out_sum, sum_other, comb)
    grad_slot_in = add(after(in_sum, row_dot), in_other)
    row_dot = row_dot + swap_cores(row_dot)
    late, row_dot = lax.optimization_barrier((grad_slot_in, row_dot))
    row_dot = row_dot + near(row_dot, "x")
    row_dot = row_dot + far(row_dot, "x")
    row_dot = row_dot + near(row_dot, "y")
    row_dot = row_dot + far(row_dot, "y")

    partial_logits, *parts = dispatch_grad(
        tokens, late, slot_in, logits, lse, comb, grad_combine
    )
    parts = sources(scatter_terms(parts, "y"))

    mine, other = patch_rows(parts, inputs, row_dot)
    other_core = swap_cores(other)

    partial_logits, mine = lax.optimization_barrier((partial_logits, mine))
    embed_part = embed_grad(tokens, partial_logits, comb, row_dot)
    embed_other = near(embed_part)
    sums = add_cores(after(mine, embed_part), other_core)
    terms = scatter_terms(sums, "x")
    grad_tokens = sum(term.astype(F32) for term in terms).astype(BF16)
    slot_late = after(slot_in, sums[0])
    grad_w_in = jnp.einsum("sd,sh->dh", slot_late, grad_pre, preferred_element_type=F32)
    grad_w_in = grad_w_in.astype(BF16)

    embed_part = add(after(embed_part, terms[1]), embed_other)
    embed_sum = add(embed_part, far(embed_part))
    z = lax.axis_index("seq")
    grad_embed = lax.dynamic_slice_in_dim(embed_sum, z * 320, 320, axis=1).T
    return (
        grad_tokens,
        grad_embed,
        grad_w_in[None],
        grad_w_out[None],
    )


def solution(mesh):
    fine = Mesh(mesh.devices.reshape(4, 4, 4, 2), ("seq", "y", "x", "core"))
    expert = ("y", "x", "core")
    return jax.shard_map(
        local,
        mesh=fine,
        in_specs=(
            P(None, "seq", None),
            P(None, expert),
            P(None, "seq", expert),
            P(expert, None, "seq"),
            P(expert, "seq", None),
            P(None, "seq", None),
        ),
        out_specs=(
            P(None, ("seq", *expert), None),
            P("seq", expert),
            P(expert, None, "seq"),
            P(expert, "seq", None),
        ),
        check_vma=False,
    )
```

```python
import math

import jax
import jax.numpy as jnp
from jax import lax
from jax.experimental import pallas as pl
from jax.experimental.pallas import tpu as pltpu
from jax.sharding import Mesh, PartitionSpec as P

F32 = jnp.float32
BF16 = jnp.bfloat16
NT = (((1,), (1,)), ((), ()))
TN = (((0,), (0,)), ((), ()))
LARGE = pltpu.CompilerParams(vmem_limit_bytes=16 * 1024 * 1024)
MEDIUM = pltpu.CompilerParams(vmem_limit_bytes=10 * 1024 * 1024)
SMALL = pltpu.CompilerParams(vmem_limit_bytes=4 * 1024 * 1024)


def shape(dims, dtype):
    return jax.ShapeDtypeStruct(dims, dtype)


def gelu_parts(values):
    cdf = 0.5 * (1.0 + jax.scipy.special.erf(values / math.sqrt(2.0)))
    slope = cdf + values * jnp.exp(-0.5 * values * values) / math.sqrt(2.0 * math.pi)
    return values * cdf, slope


def shift(value, axis, by):
    return lax.ppermute(value, axis, [(i, (i + by) % 4) for i in range(4)])


def swap_cores(value):
    return lax.ppermute(value, "core", [(0, 1), (1, 0)])


def near(value, axis="seq"):
    return lax.ppermute(value, axis, [(0, 1), (1, 0), (2, 3), (3, 2)])


def far(value, axis="seq"):
    return lax.ppermute(value, axis, [(0, 3), (3, 0), (1, 2), (2, 1)])


def add(one, two):
    return (one.astype(F32) + two.astype(F32)).astype(BF16)


def scatter_terms(blocks, axis):
    return [blocks[0]] + [shift(blocks[k], axis, k) for k in (1, 2, 3)]


def gather_blocks(block, axis):
    return [block] + [shift(block, axis, -k) for k in (1, 2, 3)]


def chunk(axis, k, size):
    return pl.multiple_of(((lax.axis_index(axis) + k) & 3) * size, size)


def lse_lanes(lse):
    high = lse.astype(BF16).astype(F32)
    middle = (lse - high).astype(BF16).astype(F32)
    low = lse - high - middle
    lane = lax.broadcasted_iota(jnp.int32, (lse.shape[0], 128), 1)
    lanes = jnp.where(lane == 0, high, jnp.where(lane == 1, middle, low))
    return jnp.where(lane < 3, lanes, 0.0).astype(BF16)


def lse_column(lanes):
    lanes = lanes.astype(F32)
    return lanes[:, 0:1] + lanes[:, 1:2] + lanes[:, 2:3]


def softmax_kernel(t00, t01, t10, t11, embed, logits, part, peak, total, sums):
    step = pl.program_id(0)

    @pl.when(step == 0)
    def _():
        peak[...] = jnp.full_like(peak, -jnp.inf)
        total[...] = jnp.zeros_like(total)
        sums[...] = jnp.zeros_like(sums)

    slots = embed[...]
    blocks = [[t00[0], t01[0]], [t10[0], t11[0]]]
    scores = [
        jnp.concatenate(
            [lax.dot_general(one, slots, NT, preferred_element_type=F32).T for one in pair],
            axis=1,
        )
        for pair in blocks
    ]
    for i in range(2):
        half = slice(32 * i, 32 * i + 32)
        logits[half, :] = scores[i]
        before = peak[half, :1]
        top = jnp.maximum(before, jnp.max(scores[i], axis=1, keepdims=True))
        scale = jnp.exp(before - top)
        weight = jnp.exp(scores[i] - top)
        new_total = total[half, :1] * scale + jnp.sum(weight, axis=1, keepdims=True)
        weight = weight.astype(BF16)
        new_sums = sums[half, :] * scale
        for n in range(2):
            new_sums = new_sums + jnp.dot(
                weight[:, 256 * n : 256 * n + 256], blocks[i][n], preferred_element_type=F32
            )
        peak[half, :] = jnp.broadcast_to(top, (32, 128))
        total[half, :] = jnp.broadcast_to(new_total, (32, 128))
        sums[half, :] = new_sums

        @pl.when(step == pl.num_programs(0) - 1)
        def _():
            part[half, :1280] = (new_sums / new_total).astype(BF16)
            part[half, 1280:] = lse_lanes(top + jnp.log(new_total))


def in_hbm(value):
    return pltpu.with_memory_space_constraint(value, pltpu.HBM)


def local_softmax(tokens, embed):
    return pl.pallas_call(
        softmax_kernel,
        grid=(2,),
        in_specs=[
            *patch_streams(),
            pl.BlockSpec((32, 1280), lambda t: (0, 0)),
        ],
        out_specs=[
            pl.BlockSpec((64, 512), lambda t: (0, t)),
            pl.BlockSpec((64, 1408), lambda t: (0, 0)),
        ],
        out_shape=[shape((64, 1024), F32), shape((64, 1408), BF16)],
        scratch_shapes=[
            pltpu.VMEM((64, 128), F32),
            pltpu.VMEM((64, 128), F32),
            pltpu.VMEM((64, 1280), F32),
        ],
        cost_estimate=pl.CostEstimate(flops=700_000_000, bytes_accessed=6_000_000, transcendentals=65536),
        compiler_params=LARGE,
        name="local_softmax",
    )(*[in_hbm(tokens)] * 4, in_hbm(embed))


def merge_kernel(one, two, sums, lse):
    lse_a, lse_b = lse_column(one[:, 1280:]), lse_column(two[:, 1280:])
    top = jnp.maximum(lse_a, lse_b)
    weight_a, weight_b = jnp.exp(lse_a - top), jnp.exp(lse_b - top)
    total = weight_a + weight_b
    part = (weight_a / total) * one[:, :1280].astype(F32)
    part = part + (weight_b / total) * two[:, :1280].astype(F32)
    lse_all = top + jnp.log(total)
    sums[:, :1280] = part.astype(BF16)
    if lse is None:
        sums[:, 1280:] = lse_lanes(lse_all)
    else:
        lse[...] = jnp.broadcast_to(lse_all, lse.shape)


def merge_pair(one, two):
    return pl.pallas_call(
        lambda a, b, out: merge_kernel(a, b, out, None),
        out_shape=shape((64, 1408), BF16),
        cost_estimate=pl.CostEstimate(flops=300_000, bytes_accessed=540_000, transcendentals=256),
        compiler_params=SMALL,
        name="merge_pair",
    )(one, two)


def merge_last(one, two):
    return pl.pallas_call(
        merge_kernel,
        out_shape=[shape((64, 1280), BF16), shape((64, 128), F32)],
        cost_estimate=pl.CostEstimate(flops=300_000, bytes_accessed=540_000, transcendentals=256),
        compiler_params=SMALL,
        name="merge_last",
    )(one, two)


def combine_grad_kernel(gout, sum_a, sum_b, comb, grad, row):
    slot_out = add(sum_a[...], sum_b[...])
    value = lax.dot_general(gout[0], slot_out, NT, preferred_element_type=F32).T
    grad[...] = value
    row[0] = jnp.sum(comb[...].astype(F32) * value, axis=0, keepdims=True)


def combine_grad(grad_out, sum_a, sum_b, comb):
    return pl.pallas_call(
        combine_grad_kernel,
        grid=(2, 2),
        in_specs=[
            pl.BlockSpec((1, 512, 1280), lambda i, t: (i, t, 0)),
            pl.BlockSpec((32, 1280), lambda i, t: (i, 0)),
            pl.BlockSpec((32, 1280), lambda i, t: (i, 0)),
            pl.BlockSpec((32, 512), lambda i, t: (i, t)),
        ],
        out_specs=[
            pl.BlockSpec((32, 512), lambda i, t: (i, t)),
            pl.BlockSpec((1, 1, 512), lambda i, t: (i, 0, t)),
        ],
        out_shape=[shape((64, 1024), F32), shape((2, 1, 1024), F32)],
        cost_estimate=pl.CostEstimate(flops=350_000_000, bytes_accessed=6_000_000, transcendentals=0),
        compiler_params=MEDIUM,
        name="combine_grad",
    )(grad_out, sum_a, sum_b, comb)


def dispatch_grad_kernel(tok, gslot, slot_in, logits, lse, comb, gcomb, full, c0, c1, c2, c3, all_weight):
    rows = gslot[...]
    col_dot = jnp.sum(slot_in[...].astype(F32) * rows.astype(F32), axis=1, keepdims=True)
    grad = lax.dot_general(tok[0], rows, NT, preferred_element_type=F32).T
    weight = jnp.exp(logits[...] - lse[:, :1])
    full[...] = weight * (grad - col_dot) + comb[...].astype(F32) * gcomb[...]
    all_weight[...] = weight
    for k, out in enumerate((c0, c1, c2, c3)):
        piece = pl.ds(chunk("y", k, 256), 256)
        out[:, :1280] = rows
        out[:, 1280:1536] = full[:, piece].astype(BF16)
        out[:, 1536:] = all_weight[:, piece].astype(BF16)


def dispatch_grad(tokens, gslot, slot_in, logits, lse, comb, gcomb):
    rows = pl.BlockSpec((32, 1280), lambda i: (i, 0))
    wide = pl.BlockSpec((32, 1024), lambda i: (i, 0))
    part = pl.BlockSpec((32, 1792), lambda i: (i, 0))
    return pl.pallas_call(
        dispatch_grad_kernel,
        grid=(2,),
        in_specs=[
            pl.BlockSpec((1, 1024, 1280), lambda i: (i, 0, 0)),
            rows,
            rows,
            wide,
            pl.BlockSpec((32, 128), lambda i: (i, 0)),
            wide,
            wide,
        ],
        out_specs=[wide] + [part] * 4,
        out_shape=[shape((64, 1024), F32)] + [shape((64, 1792), BF16)] * 4,
        scratch_shapes=[pltpu.VMEM((32, 1024), F32)],
        cost_estimate=pl.CostEstimate(flops=350_000_000, bytes_accessed=7_000_000, transcendentals=65536),
        compiler_params=MEDIUM,
        name="dispatch_grad",
    )(tokens, gslot, slot_in, logits, lse, comb, gcomb)


def inputs_kernel(comb, embed, o0, o1, o2, o3):
    for k, out in enumerate((o0, o1, o2, o3)):
        out[:64, :] = comb[:, pl.ds(chunk("y", k, 256), 256)]
        for n in range(5):
            out[64 + 32 * n : 96 + 32 * n, :] = embed[:, 256 * n : 256 * n + 256]


def input_blocks(comb, embed):
    return pl.pallas_call(
        inputs_kernel,
        out_shape=[shape((224, 256), BF16)] * 4,
        cost_estimate=pl.CostEstimate(flops=0, bytes_accessed=700_000, transcendentals=0),
        compiler_params=SMALL,
        name="input_blocks",
    )(comb, embed)


def embed_grad_kernel(t00, t01, t10, t11, partial_logits, comb, row_dot, out, sums):
    value = 0.0
    for i, pair in enumerate(((t00, t01), (t10, t11))):
        half = slice(32 * i, 32 * i + 32)
        grad = partial_logits[half, :] - comb[half, :].astype(F32) * row_dot[i]
        grad = grad.astype(BF16)
        for n in range(2):
            value = value + jnp.dot(
                grad[:, 256 * n : 256 * n + 256], pair[n][0], preferred_element_type=F32
            )

    @pl.when(pl.program_id(0) == 0)
    def _():
        sums[...] = value

    @pl.when(pl.program_id(0) == 1)
    def _():
        out[...] = (sums[...] + value).astype(BF16)


def patch_streams():
    return [
        pl.BlockSpec((1, 256, 1280), lambda t, i=i, n=n: (i, 2 * t + n, 0))
        for i in range(2)
        for n in range(2)
    ]


def embed_grad(tokens, partial_logits, comb, row_dot):
    wide = pl.BlockSpec((64, 512), lambda t: (0, t))
    return pl.pallas_call(
        embed_grad_kernel,
        grid=(2,),
        in_specs=[*patch_streams(), wide, wide, pl.BlockSpec((2, 1, 512), lambda t: (0, 0, t))],
        out_specs=pl.BlockSpec((32, 1280), lambda t: (0, 0)),
        out_shape=shape((32, 1280), BF16),
        scratch_shapes=[pltpu.VMEM((32, 1280), F32)],
        cost_estimate=pl.CostEstimate(flops=170_000_000, bytes_accessed=6_000_000, transcendentals=0),
        compiler_params=MEDIUM,
        name="embed_grad",
    )(*[in_hbm(tokens)] * 4, partial_logits, comb, row_dot)


def rows_kernel(*refs):
    parts, inputs = refs[:4], refs[4:8]
    row_dot, mine, other, scratch = refs[8:]
    core = lax.axis_index("core")
    embeds = [
        jnp.concatenate([one[64 + 32 * n : 96 + 32 * n, :] for n in range(5)], axis=1)
        for one in inputs
    ]
    for i in range(2):
        half = slice(32 * i, 32 * i + 32)
        dots = row_dot[i, :, pl.ds(chunk("y", 0, 256), 256)]
        weights = [one[half, 1536:] for one in parts] + [
            (p[half, 1280:1536].astype(F32) - c[half, :].astype(F32) * dots).astype(BF16)
            for p, c in zip(parts, inputs)
        ]
        rows = [one[half, :1280] for one in parts] + embeds
        scratch[i] = lax.dot_general(
            jnp.concatenate(weights), jnp.concatenate(rows), TN, preferred_element_type=F32
        )
        for k in range(4):
            base = ((lax.axis_index("x") + k) & 3) * 64
            here = pl.multiple_of(base + core * 32, 32)
            there = pl.multiple_of(base + (1 - core) * 32, 32)
            mine[k, i] = scratch[i, pl.ds(here, 32), :].astype(BF16)
            other[k, i] = scratch[i, pl.ds(there, 32), :].astype(BF16)


def patch_rows(parts, inputs, row_dot):
    return pl.pallas_call(
        rows_kernel,
        out_shape=[shape((4, 2, 32, 1280), BF16)] * 2,
        scratch_shapes=[pltpu.VMEM((2, 256, 1280), F32)],
        cost_estimate=pl.CostEstimate(flops=335_000_000, bytes_accessed=3_000_000, transcendentals=0),
        compiler_params=MEDIUM,
        name="patch_rows",
    )(*parts, *inputs, row_dot)


def add_kernel(mine, other, o0, o1, o2, o3):
    for k, out in enumerate((o0, o1, o2, o3)):
        out[...] = add(mine[k], other[k])


def add_cores(mine, other):
    return pl.pallas_call(
        add_kernel,
        out_shape=[pltpu.HBM((2, 32, 1280), BF16)] * 4,
        cost_estimate=pl.CostEstimate(flops=327_680, bytes_accessed=2_000_000, transcendentals=0),
        compiler_params=SMALL,
        name="add_cores",
    )(mine, other)


def after(value, *others):
    return lax.optimization_barrier((value, *others))[0]


def sources(terms):
    return [terms[0], terms[3], terms[2], terms[1]]


def local(tokens, slot_embed, combine, w_in, w_out, grad_out):
    w_in, w_out = w_in[0], w_out[0]
    embed = slot_embed.T
    comb = jnp.transpose(combine, (0, 2, 1)).reshape(64, 1024)

    logits, part = local_softmax(tokens, embed)
    comb_late = after(comb, part)
    out_part = jnp.einsum(
        "ijt,itd->ijd", comb_late.reshape(2, 32, 1024), grad_out, preferred_element_type=F32
    )
    out_part = out_part.astype(BF16).reshape(64, 1280)
    part_other = near(part)
    part, out_part = lax.optimization_barrier((part, out_part))
    out_other = near(out_part)
    part = merge_pair(part, part_other)
    comb_late = after(comb_late, part)
    slot_in, lse = merge_last(part, far(part))
    inputs = list(input_blocks(comb_late, embed))
    out_part = add(after(out_part, slot_in), out_other)
    grad_slot_out = add(out_part, far(out_part))

    pre_act = jnp.dot(slot_in, w_in, preferred_element_type=F32)
    act, slope = gelu_parts(pre_act)
    act = act.astype(BF16)
    out_sum = jnp.dot(act, w_out, preferred_element_type=F32).astype(BF16)
    grad_slot_out = after(grad_slot_out, out_sum)
    inputs[3] = after(inputs[3], out_sum)
    inputs = sources(scatter_terms(inputs, "y"))
    out_sum = add(out_sum, near(out_sum))
    out_sum = after(out_sum, *inputs)
    sum_other = far(out_sum)
    grad_act = jnp.einsum("sd,hd->sh", grad_slot_out, w_out, preferred_element_type=F32)
    grad_pre = (grad_act * slope).astype(BF16)
    in_sum = jnp.einsum("sh,dh->sd", grad_pre, w_in, preferred_element_type=F32).astype(BF16)
    in_sum, act_late, slots_late = lax.optimization_barrier(
        (in_sum, act, grad_slot_out, out_sum)
    )[:3]
    in_other = near(in_sum)
    grad_w_out = jnp.einsum("sh,sd->hd", act_late, slots_late, preferred_element_type=F32)
    grad_w_out = grad_w_out.astype(BF16)
    in_sum = add(after(in_sum, grad_w_out), in_other)
    in_other = far(in_sum)

    grad_combine, row_dot = combine_grad(grad_out, out_sum, sum_other, comb)
    grad_slot_in = add(after(in_sum, row_dot), in_other)
    row_dot = row_dot + swap_cores(row_dot)
    late, row_dot = lax.optimization_barrier((grad_slot_in, row_dot))
    row_dot = row_dot + near(row_dot, "x")
    first_dot = row_dot
    row_dot = row_dot + far(row_dot, "x")
    second_dot = row_dot
    row_dot = row_dot + near(row_dot, "y")
    row_dot = row_dot + far(row_dot, "y")

    partial_logits, *parts = dispatch_grad(
        tokens, late, slot_in, logits, lse, comb, grad_combine
    )
    parts = list(lax.optimization_barrier((*parts, first_dot))[:4])
    parts[3] = after(parts[3], second_dot)
    parts = sources(scatter_terms(parts, "y"))

    mine, other = patch_rows(parts, inputs, row_dot)
    other_core = swap_cores(other)

    partial_logits, mine = lax.optimization_barrier((partial_logits, mine))
    embed_part = embed_grad(tokens, partial_logits, comb, row_dot)
    embed_other = near(embed_part)
    sums = add_cores(after(mine, embed_part), other_core)
    terms = scatter_terms(sums, "x")
    embed_part = add(after(embed_part, terms[1]), embed_other)
    embed_sum = add(embed_part, far(embed_part))
    z = lax.axis_index("seq")
    grad_embed = lax.dynamic_slice_in_dim(embed_sum, z * 320, 320, axis=1).T
    slot_late = after(slot_in, embed_part)
    grad_w_in = jnp.einsum("sd,sh->dh", slot_late, grad_pre, preferred_element_type=F32)
    grad_w_in = grad_w_in.astype(BF16)

    nearer = terms[0].astype(F32) + terms[1].astype(F32) + terms[3].astype(F32)
    nearer, grad_w_in = lax.optimization_barrier((nearer, grad_w_in.astype(BF16)))
    grad_tokens = (nearer + terms[2].astype(F32)).astype(BF16)
    return (
        grad_tokens,
        grad_embed,
        grad_w_in[None],
        grad_w_out[None],
    )


def solution(mesh):
    fine = Mesh(mesh.devices.reshape(4, 4, 4, 2), ("seq", "y", "x", "core"))
    expert = ("y", "x", "core")
    return jax.shard_map(
        local,
        mesh=fine,
        in_specs=(
            P(None, "seq", None),
            P(None, expert),
            P(None, "seq", expert),
            P(expert, None, "seq"),
            P(expert, "seq", None),
            P(None, "seq", None),
        ),
        out_specs=(
            P(None, ("seq", *expert), None),
            P("seq", expert),
            P(expert, None, "seq"),
            P(expert, "seq", None),
        ),
        check_vma=False,
    )
```

```python
import math

import jax
import jax.numpy as jnp
from jax import lax
from jax.experimental import pallas as pl
from jax.experimental.pallas import tpu as pltpu
from jax.sharding import Mesh, PartitionSpec as P

F32 = jnp.float32
BF16 = jnp.bfloat16
NT = (((1,), (1,)), ((), ()))
TN = (((0,), (0,)), ((), ()))
LARGE = pltpu.CompilerParams(vmem_limit_bytes=16 * 1024 * 1024)
MEDIUM = pltpu.CompilerParams(vmem_limit_bytes=10 * 1024 * 1024)
SMALL = pltpu.CompilerParams(vmem_limit_bytes=4 * 1024 * 1024)


def shape(dims, dtype):
    return jax.ShapeDtypeStruct(dims, dtype)


def gelu_parts(values):
    cdf = 0.5 * (1.0 + jax.scipy.special.erf(values / math.sqrt(2.0)))
    slope = cdf + values * jnp.exp(-0.5 * values * values) / math.sqrt(2.0 * math.pi)
    return values * cdf, slope


def shift(value, axis, by):
    return lax.ppermute(value, axis, [(i, (i + by) % 4) for i in range(4)])


def swap_cores(value):
    return lax.ppermute(value, "core", [(0, 1), (1, 0)])


def near(value, axis="seq"):
    return lax.ppermute(value, axis, [(0, 1), (1, 0), (2, 3), (3, 2)])


def far(value, axis="seq"):
    return lax.ppermute(value, axis, [(0, 3), (3, 0), (1, 2), (2, 1)])


def add(one, two):
    return (one.astype(F32) + two.astype(F32)).astype(BF16)


def scatter_terms(blocks, axis):
    return [blocks[0]] + [shift(blocks[k], axis, k) for k in (1, 2, 3)]


def gather_blocks(block, axis):
    return [block] + [shift(block, axis, -k) for k in (1, 2, 3)]


def chunk(axis, k, size):
    return pl.multiple_of(((lax.axis_index(axis) + k) & 3) * size, size)


def lse_lanes(lse):
    high = lse.astype(BF16).astype(F32)
    middle = (lse - high).astype(BF16).astype(F32)
    low = lse - high - middle
    lane = lax.broadcasted_iota(jnp.int32, (lse.shape[0], 128), 1)
    lanes = jnp.where(lane == 0, high, jnp.where(lane == 1, middle, low))
    return jnp.where(lane < 3, lanes, 0.0).astype(BF16)


def lse_column(lanes):
    lanes = lanes.astype(F32)
    return lanes[:, 0:1] + lanes[:, 1:2] + lanes[:, 2:3]


def start_patches(source, target, sems):
    copies = [
        [
            pltpu.make_async_copy(
                source.at[i, pl.ds(256 * n, 256)],
                target.at[i, pl.ds(256 * n, 256)],
                sems.at[4 * i + n],
            )
            for n in range(4)
        ]
        for i in range(2)
    ]
    for i in range(2):
        for n in range(4):
            copies[i][n].start()
    return lambda i, n: copies[i][n].wait()


def softmax_kernel(tok, embed, logits, part, patches, slots, sems, embed_sem):
    embed_copy = pltpu.make_async_copy(embed, slots, embed_sem)
    embed_copy.start()
    wait = start_patches(tok, patches, sems)
    embed_copy.wait()
    columns = slots[...]
    scores = []
    for i in range(2):
        pieces = []
        for n in range(4):
            wait(i, n)
            rows = patches[i, 256 * n : 256 * n + 256, :]
            pieces.append(lax.dot_general(rows, columns, NT, preferred_element_type=F32).T)
        scores.append(jnp.concatenate(pieces, axis=1))
    for i in range(2):
        half = slice(32 * i, 32 * i + 32)
        logits[half, :] = scores[i]
        peak = jnp.max(scores[i], axis=1, keepdims=True)
        weight = jnp.exp(scores[i] - peak)
        total = jnp.sum(weight, axis=1, keepdims=True)
        sums = jnp.dot(weight.astype(BF16), patches[i], preferred_element_type=F32)
        part[half, :1280] = (sums / total).astype(BF16)
        part[half, 1280:] = lse_lanes(peak + jnp.log(total))


def in_hbm(value):
    return pltpu.with_memory_space_constraint(value, pltpu.HBM)


def local_softmax(tokens, embed):
    return pl.pallas_call(
        softmax_kernel,
        in_specs=[pl.BlockSpec(memory_space=pl.ANY)] * 2,
        out_shape=[shape((64, 1024), F32), shape((64, 1408), BF16)],
        scratch_shapes=[
            pltpu.VMEM((2, 1024, 1280), BF16),
            pltpu.VMEM((32, 1280), BF16),
            pltpu.SemaphoreType.DMA((8,)),
            pltpu.SemaphoreType.DMA,
        ],
        cost_estimate=pl.CostEstimate(flops=700_000_000, bytes_accessed=6_000_000, transcendentals=65536),
        compiler_params=LARGE,
        name="local_softmax",
    )(in_hbm(tokens), in_hbm(embed))


def merge_kernel(one, two, sums, lse):
    lse_a, lse_b = lse_column(one[:, 1280:]), lse_column(two[:, 1280:])
    top = jnp.maximum(lse_a, lse_b)
    weight_a, weight_b = jnp.exp(lse_a - top), jnp.exp(lse_b - top)
    total = weight_a + weight_b
    part = (weight_a / total) * one[:, :1280].astype(F32)
    part = part + (weight_b / total) * two[:, :1280].astype(F32)
    lse_all = top + jnp.log(total)
    sums[:, :1280] = part.astype(BF16)
    if lse is None:
        sums[:, 1280:] = lse_lanes(lse_all)
    else:
        lse[...] = jnp.broadcast_to(lse_all, lse.shape)


def merge_pair(one, two):
    return pl.pallas_call(
        lambda a, b, out: merge_kernel(a, b, out, None),
        out_shape=shape((64, 1408), BF16),
        cost_estimate=pl.CostEstimate(flops=300_000, bytes_accessed=540_000, transcendentals=256),
        compiler_params=SMALL,
        name="merge_pair",
    )(one, two)


def merge_last(one, two):
    return pl.pallas_call(
        merge_kernel,
        out_shape=[shape((64, 1280), BF16), shape((64, 128), F32)],
        cost_estimate=pl.CostEstimate(flops=300_000, bytes_accessed=540_000, transcendentals=256),
        compiler_params=SMALL,
        name="merge_last",
    )(one, two)


def combine_grad_kernel(gout, sum_a, sum_b, comb, grad, row):
    slot_out = add(sum_a[...], sum_b[...])
    for i in range(2):
        half = slice(32 * i, 32 * i + 32)
        value = lax.dot_general(gout[i], slot_out[half, :], NT, preferred_element_type=F32).T
        grad[half, :] = value
        row[i] = jnp.sum(comb[half, :].astype(F32) * value, axis=0, keepdims=True)


def combine_grad(grad_out, sum_a, sum_b, comb):
    return pl.pallas_call(
        combine_grad_kernel,
        out_shape=[shape((64, 1024), F32), shape((2, 1, 1024), F32)],
        cost_estimate=pl.CostEstimate(flops=350_000_000, bytes_accessed=6_000_000, transcendentals=0),
        compiler_params=MEDIUM,
        name="combine_grad",
    )(grad_out, sum_a, sum_b, comb)


def dispatch_grad_kernel(tok, gslot, slot_in, logits, lse, comb, gcomb, full, c0, c1, c2, c3, all_weight):
    for i in range(2):
        half = slice(32 * i, 32 * i + 32)
        rows = gslot[half, :]
        col_dot = jnp.sum(slot_in[half, :].astype(F32) * rows.astype(F32), axis=1, keepdims=True)
        grad = lax.dot_general(tok[i], rows, NT, preferred_element_type=F32).T
        weight = jnp.exp(logits[half, :] - lse[half, :1])
        full[half, :] = weight * (grad - col_dot) + comb[half, :].astype(F32) * gcomb[half, :]
        all_weight[half, :] = weight
        for k, out in enumerate((c0, c1, c2, c3)):
            piece = pl.ds(chunk("y", k, 256), 256)
            out[half, :1280] = rows
            out[half, 1280:1536] = full[half, piece].astype(BF16)
            out[half, 1536:] = all_weight[half, piece].astype(BF16)


def dispatch_grad(tokens, gslot, slot_in, logits, lse, comb, gcomb):
    return pl.pallas_call(
        dispatch_grad_kernel,
        out_shape=[shape((64, 1024), F32)] + [shape((64, 1792), BF16)] * 4,
        scratch_shapes=[pltpu.VMEM((64, 1024), F32)],
        cost_estimate=pl.CostEstimate(flops=350_000_000, bytes_accessed=7_000_000, transcendentals=65536),
        compiler_params=MEDIUM,
        name="dispatch_grad",
    )(tokens, gslot, slot_in, logits, lse, comb, gcomb)


def inputs_kernel(comb, embed, o0, o1, o2, o3):
    for k, out in enumerate((o0, o1, o2, o3)):
        out[:64, :] = comb[:, pl.ds(chunk("y", k, 256), 256)]
        for n in range(5):
            out[64 + 32 * n : 96 + 32 * n, :] = embed[:, 256 * n : 256 * n + 256]


def input_blocks(comb, embed):
    return pl.pallas_call(
        inputs_kernel,
        out_shape=[shape((224, 256), BF16)] * 4,
        cost_estimate=pl.CostEstimate(flops=0, bytes_accessed=700_000, transcendentals=0),
        compiler_params=SMALL,
        name="input_blocks",
    )(comb, embed)


def embed_grad_kernel(tok, partial_logits, comb, row_dot, out, patches, sems):
    wait = start_patches(tok, patches, sems)
    value = 0.0
    for i in range(2):
        half = slice(32 * i, 32 * i + 32)
        grad = partial_logits[half, :] - comb[half, :].astype(F32) * row_dot[i]
        grad = grad.astype(BF16)
        for n in range(4):
            wait(i, n)
            span = slice(256 * n, 256 * n + 256)
            value = value + jnp.dot(
                grad[:, span], patches[i, span, :], preferred_element_type=F32
            )
    out[...] = value.astype(BF16)


def embed_grad(tokens, partial_logits, comb, row_dot):
    return pl.pallas_call(
        embed_grad_kernel,
        in_specs=[pl.BlockSpec(memory_space=pl.ANY)]
        + [pl.BlockSpec(memory_space=pltpu.VMEM)] * 3,
        out_shape=shape((32, 1280), BF16),
        scratch_shapes=[pltpu.VMEM((2, 1024, 1280), BF16), pltpu.SemaphoreType.DMA((8,))],
        cost_estimate=pl.CostEstimate(flops=170_000_000, bytes_accessed=6_000_000, transcendentals=0),
        compiler_params=MEDIUM,
        name="embed_grad",
    )(in_hbm(tokens), partial_logits, comb, row_dot)


def rows_kernel(*refs):
    parts, inputs = refs[:4], refs[4:8]
    row_dot, mine, other, scratch = refs[8:]
    core = lax.axis_index("core")
    embeds = [
        jnp.concatenate([one[64 + 32 * n : 96 + 32 * n, :] for n in range(5)], axis=1)
        for one in inputs
    ]
    for i in range(2):
        half = slice(32 * i, 32 * i + 32)
        dots = row_dot[i, :, pl.ds(chunk("y", 0, 256), 256)]
        weights = [one[half, 1536:] for one in parts] + [
            (p[half, 1280:1536].astype(F32) - c[half, :].astype(F32) * dots).astype(BF16)
            for p, c in zip(parts, inputs)
        ]
        rows = [one[half, :1280] for one in parts] + embeds
        scratch[i] = lax.dot_general(
            jnp.concatenate(weights), jnp.concatenate(rows), TN, preferred_element_type=F32
        )
        for k in range(4):
            base = ((lax.axis_index("x") + k) & 3) * 64
            here = pl.multiple_of(base + core * 32, 32)
            there = pl.multiple_of(base + (1 - core) * 32, 32)
            mine[k, i] = scratch[i, pl.ds(here, 32), :].astype(BF16)
            other[k, i] = scratch[i, pl.ds(there, 32), :].astype(BF16)


def patch_rows(parts, inputs, row_dot):
    return pl.pallas_call(
        rows_kernel,
        out_shape=[shape((4, 2, 32, 1280), BF16)] * 2,
        scratch_shapes=[pltpu.VMEM((2, 256, 1280), F32)],
        cost_estimate=pl.CostEstimate(flops=335_000_000, bytes_accessed=3_000_000, transcendentals=0),
        compiler_params=MEDIUM,
        name="patch_rows",
    )(*parts, *inputs, row_dot)


def add_kernel(mine, other, o0, o1, o2, o3):
    for k, out in enumerate((o0, o1, o2, o3)):
        out[...] = add(mine[k], other[k])


def add_cores(mine, other):
    return pl.pallas_call(
        add_kernel,
        out_shape=[pltpu.HBM((2, 32, 1280), BF16)] * 4,
        cost_estimate=pl.CostEstimate(flops=327_680, bytes_accessed=2_000_000, transcendentals=0),
        compiler_params=SMALL,
        name="add_cores",
    )(mine, other)


def after(value, *others):
    return lax.optimization_barrier((value, *others))[0]


def sources(terms):
    return [terms[0], terms[3], terms[2], terms[1]]


def local(tokens, slot_embed, combine, w_in, w_out, grad_out):
    w_in, w_out = w_in[0], w_out[0]
    embed = slot_embed.T
    comb = jnp.transpose(combine, (0, 2, 1)).reshape(64, 1024)

    logits, part = local_softmax(tokens, embed)
    comb_late = after(comb, part)
    out_part = jnp.einsum(
        "ijt,itd->ijd", comb_late.reshape(2, 32, 1024), grad_out, preferred_element_type=F32
    )
    out_part = out_part.astype(BF16).reshape(64, 1280)
    part_other = near(part)
    part, out_part = lax.optimization_barrier((part, out_part))
    out_other = near(out_part)
    part = merge_pair(part, part_other)
    comb_late = after(comb_late, part)
    slot_in, lse = merge_last(part, far(part))
    inputs = list(input_blocks(comb_late, embed))
    out_part = add(after(out_part, slot_in), out_other)
    grad_slot_out = add(out_part, far(out_part))

    pre_act = jnp.dot(slot_in, w_in, preferred_element_type=F32)
    act, slope = gelu_parts(pre_act)
    act = act.astype(BF16)
    out_sum = jnp.dot(act, w_out, preferred_element_type=F32).astype(BF16)
    grad_slot_out = after(grad_slot_out, out_sum)
    inputs[3] = after(inputs[3], out_sum)
    inputs = sources(scatter_terms(inputs, "y"))
    out_sum = add(out_sum, near(out_sum))
    out_sum = after(out_sum, *inputs)
    sum_other = far(out_sum)
    grad_act = jnp.einsum("sd,hd->sh", grad_slot_out, w_out, preferred_element_type=F32)
    grad_pre = (grad_act * slope).astype(BF16)
    in_sum = jnp.einsum("sh,dh->sd", grad_pre, w_in, preferred_element_type=F32).astype(BF16)
    in_sum, act_late, slots_late = lax.optimization_barrier(
        (in_sum, act, grad_slot_out, out_sum)
    )[:3]
    in_other = near(in_sum)
    grad_w_out = jnp.einsum("sh,sd->hd", act_late, slots_late, preferred_element_type=F32)
    grad_w_out = grad_w_out.astype(BF16)
    in_sum = add(after(in_sum, grad_w_out), in_other)
    in_other = far(in_sum)

    grad_combine, row_dot = combine_grad(grad_out, out_sum, sum_other, comb)
    grad_slot_in = add(after(in_sum, row_dot), in_other)
    row_dot = row_dot + swap_cores(row_dot)
    late, row_dot = lax.optimization_barrier((grad_slot_in, row_dot))
    row_dot = row_dot + near(row_dot, "x")
    row_dot = row_dot + far(row_dot, "x")
    row_dot = row_dot + near(row_dot, "y")
    row_dot = row_dot + far(row_dot, "y")

    partial_logits, *parts = dispatch_grad(
        tokens, late, slot_in, logits, lse, comb, grad_combine
    )
    parts = sources(scatter_terms(parts, "y"))

    mine, other = patch_rows(parts, inputs, row_dot)
    other_core = swap_cores(other)

    partial_logits, mine = lax.optimization_barrier((partial_logits, mine))
    embed_part = embed_grad(tokens, partial_logits, comb, row_dot)
    sums = add_cores(after(mine, embed_part), other_core)
    embed_part = after(embed_part, sums[0])
    embed_other = near(embed_part)
    terms = scatter_terms(sums, "x")
    grad_tokens = sum(term.astype(F32) for term in terms).astype(BF16)
    embed_part = add(embed_part, embed_other)
    embed_sum = add(embed_part, far(embed_part))
    z = lax.axis_index("seq")
    grad_embed = lax.dynamic_slice_in_dim(embed_sum, z * 320, 320, axis=1).T
    slot_late = after(slot_in, embed_part)
    grad_w_in = jnp.einsum("sd,sh->dh", slot_late, grad_pre, preferred_element_type=F32)
    grad_w_in = grad_w_in.astype(BF16)

    return (
        grad_tokens,
        grad_embed,
        grad_w_in[None],
        grad_w_out[None],
    )


def solution(mesh):
    fine = Mesh(mesh.devices.reshape(4, 4, 4, 2), ("seq", "y", "x", "core"))
    expert = ("y", "x", "core")
    return jax.shard_map(
        local,
        mesh=fine,
        in_specs=(
            P(None, "seq", None),
            P(None, expert),
            P(None, "seq", expert),
            P(expert, None, "seq"),
            P(expert, "seq", None),
            P(None, "seq", None),
        ),
        out_specs=(
            P(None, ("seq", *expert), None),
            P("seq", expert),
            P(expert, None, "seq"),
            P(expert, "seq", None),
        ),
        check_vma=False,
    )
```

```python
import math

import jax
import jax.numpy as jnp
from jax import lax
from jax.experimental import pallas as pl
from jax.experimental.pallas import tpu as pltpu
from jax.sharding import Mesh, PartitionSpec as P

F32 = jnp.float32
BF16 = jnp.bfloat16
NT = (((1,), (1,)), ((), ()))
TN = (((0,), (0,)), ((), ()))
LARGE = pltpu.CompilerParams(vmem_limit_bytes=16 * 1024 * 1024)
MEDIUM = pltpu.CompilerParams(vmem_limit_bytes=10 * 1024 * 1024)
SMALL = pltpu.CompilerParams(vmem_limit_bytes=4 * 1024 * 1024)


def shape(dims, dtype):
    return jax.ShapeDtypeStruct(dims, dtype)


def gelu_parts(values):
    cdf = 0.5 * (1.0 + jax.scipy.special.erf(values / math.sqrt(2.0)))
    slope = cdf + values * jnp.exp(-0.5 * values * values) / math.sqrt(2.0 * math.pi)
    return values * cdf, slope


def shift(value, axis, by):
    return lax.ppermute(value, axis, [(i, (i + by) % 4) for i in range(4)])


def swap_cores(value):
    return lax.ppermute(value, "core", [(0, 1), (1, 0)])


def near(value, axis="seq"):
    return lax.ppermute(value, axis, [(0, 1), (1, 0), (2, 3), (3, 2)])


def far(value, axis="seq"):
    return lax.ppermute(value, axis, [(0, 3), (3, 0), (1, 2), (2, 1)])


def add(one, two):
    return (one.astype(F32) + two.astype(F32)).astype(BF16)


def scatter_terms(blocks, axis):
    return [blocks[0]] + [shift(blocks[k], axis, k) for k in (1, 2, 3)]


def gather_blocks(block, axis):
    return [block] + [shift(block, axis, -k) for k in (1, 2, 3)]


def chunk(axis, k, size):
    return pl.multiple_of(((lax.axis_index(axis) + k) & 3) * size, size)


def lse_lanes(lse):
    high = lse.astype(BF16).astype(F32)
    middle = (lse - high).astype(BF16).astype(F32)
    low = lse - high - middle
    lane = lax.broadcasted_iota(jnp.int32, (lse.shape[0], 128), 1)
    lanes = jnp.where(lane == 0, high, jnp.where(lane == 1, middle, low))
    return jnp.where(lane < 3, lanes, 0.0).astype(BF16)


def lse_column(lanes):
    lanes = lanes.astype(F32)
    return lanes[:, 0:1] + lanes[:, 1:2] + lanes[:, 2:3]


def start_patches(source, target, sems):
    copies = [
        [
            pltpu.make_async_copy(
                source.at[i, pl.ds(256 * n, 256)],
                target.at[i, pl.ds(256 * n, 256)],
                sems.at[4 * i + n],
            )
            for n in range(4)
        ]
        for i in range(2)
    ]
    for i in range(2):
        for n in range(4):
            copies[i][n].start()
    return lambda i, n: copies[i][n].wait()


def softmax_kernel(*refs):
    embed, logits, part = refs[8:]
    columns = embed[...]
    blocks = [[one[0] for one in refs[4 * i : 4 * i + 4]] for i in range(2)]
    scores = [
        jnp.concatenate(
            [lax.dot_general(one, columns, NT, preferred_element_type=F32).T for one in four],
            axis=1,
        )
        for four in blocks
    ]
    for i in range(2):
        half = slice(32 * i, 32 * i + 32)
        logits[half, :] = scores[i]
        peak = jnp.max(scores[i], axis=1, keepdims=True)
        weight = jnp.exp(scores[i] - peak)
        total = jnp.sum(weight, axis=1, keepdims=True)
        weight = weight.astype(BF16)
        sums = 0.0
        for n in range(4):
            sums = sums + jnp.dot(
                weight[:, 256 * n : 256 * n + 256], blocks[i][n], preferred_element_type=F32
            )
        part[half, :1280] = (sums / total).astype(BF16)
        part[half, 1280:] = lse_lanes(peak + jnp.log(total))


def in_hbm(value):
    return pltpu.with_memory_space_constraint(value, pltpu.HBM)


def local_softmax(tokens, embed):
    return pl.pallas_call(
        softmax_kernel,
        grid=(1,),
        in_specs=[
            pl.BlockSpec((1, 256, 1280), lambda t, i=i, n=n: (i, n, 0))
            for i in range(2)
            for n in range(4)
        ]
        + [pl.BlockSpec((32, 1280), lambda t: (0, 0))],
        out_specs=[
            pl.BlockSpec((64, 1024), lambda t: (0, 0)),
            pl.BlockSpec((64, 1408), lambda t: (0, 0)),
        ],
        out_shape=[shape((64, 1024), F32), shape((64, 1408), BF16)],
        cost_estimate=pl.CostEstimate(flops=700_000_000, bytes_accessed=6_000_000, transcendentals=65536),
        compiler_params=LARGE,
        name="local_softmax",
    )(*[in_hbm(tokens)] * 8, in_hbm(embed))


def merge_kernel(one, two, sums, lse):
    lse_a, lse_b = lse_column(one[:, 1280:]), lse_column(two[:, 1280:])
    top = jnp.maximum(lse_a, lse_b)
    weight_a, weight_b = jnp.exp(lse_a - top), jnp.exp(lse_b - top)
    total = weight_a + weight_b
    part = (weight_a / total) * one[:, :1280].astype(F32)
    part = part + (weight_b / total) * two[:, :1280].astype(F32)
    lse_all = top + jnp.log(total)
    sums[:, :1280] = part.astype(BF16)
    if lse is None:
        sums[:, 1280:] = lse_lanes(lse_all)
    else:
        lse[...] = jnp.broadcast_to(lse_all, lse.shape)


def merge_pair(one, two):
    return pl.pallas_call(
        lambda a, b, out: merge_kernel(a, b, out, None),
        out_shape=shape((64, 1408), BF16),
        cost_estimate=pl.CostEstimate(flops=300_000, bytes_accessed=540_000, transcendentals=256),
        compiler_params=SMALL,
        name="merge_pair",
    )(one, two)


def merge_last(one, two):
    return pl.pallas_call(
        merge_kernel,
        out_shape=[shape((64, 1280), BF16), shape((64, 128), F32)],
        cost_estimate=pl.CostEstimate(flops=300_000, bytes_accessed=540_000, transcendentals=256),
        compiler_params=SMALL,
        name="merge_last",
    )(one, two)


def combine_grad_kernel(gout, sum_a, sum_b, comb, grad, row):
    slot_out = add(sum_a[...], sum_b[...])
    for i in range(2):
        half = slice(32 * i, 32 * i + 32)
        value = lax.dot_general(gout[i], slot_out[half, :], NT, preferred_element_type=F32).T
        grad[half, :] = value
        row[i] = jnp.sum(comb[half, :].astype(F32) * value, axis=0, keepdims=True)


def combine_grad(grad_out, sum_a, sum_b, comb):
    return pl.pallas_call(
        combine_grad_kernel,
        out_shape=[shape((64, 1024), F32), shape((2, 1, 1024), F32)],
        cost_estimate=pl.CostEstimate(flops=350_000_000, bytes_accessed=6_000_000, transcendentals=0),
        compiler_params=MEDIUM,
        name="combine_grad",
    )(grad_out, sum_a, sum_b, comb)


def dispatch_grad_kernel(tok, gslot, slot_in, logits, lse, comb, gcomb, full, c0, c1, c2, c3, all_weight):
    for i in range(2):
        half = slice(32 * i, 32 * i + 32)
        rows = gslot[half, :]
        col_dot = jnp.sum(slot_in[half, :].astype(F32) * rows.astype(F32), axis=1, keepdims=True)
        grad = lax.dot_general(tok[i], rows, NT, preferred_element_type=F32).T
        weight = jnp.exp(logits[half, :] - lse[half, :1])
        full[half, :] = weight * (grad - col_dot) + comb[half, :].astype(F32) * gcomb[half, :]
        all_weight[half, :] = weight
        for k, out in enumerate((c0, c1, c2, c3)):
            piece = pl.ds(chunk("y", k, 256), 256)
            out[half, :1280] = rows
            out[half, 1280:1536] = full[half, piece].astype(BF16)
            out[half, 1536:] = all_weight[half, piece].astype(BF16)


def dispatch_grad(tokens, gslot, slot_in, logits, lse, comb, gcomb):
    return pl.pallas_call(
        dispatch_grad_kernel,
        out_shape=[shape((64, 1024), F32)] + [shape((64, 1792), BF16)] * 4,
        scratch_shapes=[pltpu.VMEM((64, 1024), F32)],
        cost_estimate=pl.CostEstimate(flops=350_000_000, bytes_accessed=7_000_000, transcendentals=65536),
        compiler_params=MEDIUM,
        name="dispatch_grad",
    )(tokens, gslot, slot_in, logits, lse, comb, gcomb)


def inputs_kernel(comb, embed, o0, o1, o2, o3):
    for k, out in enumerate((o0, o1, o2, o3)):
        out[:64, :] = comb[:, pl.ds(chunk("y", k, 256), 256)]
        for n in range(5):
            out[64 + 32 * n : 96 + 32 * n, :] = embed[:, 256 * n : 256 * n + 256]


def input_blocks(comb, embed):
    return pl.pallas_call(
        inputs_kernel,
        out_shape=[shape((224, 256), BF16)] * 4,
        cost_estimate=pl.CostEstimate(flops=0, bytes_accessed=700_000, transcendentals=0),
        compiler_params=SMALL,
        name="input_blocks",
    )(comb, embed)


def embed_grad_kernel(tok, partial_logits, comb, row_dot, out, patches, sems):
    wait = start_patches(tok, patches, sems)
    value = 0.0
    for i in range(2):
        half = slice(32 * i, 32 * i + 32)
        grad = partial_logits[half, :] - comb[half, :].astype(F32) * row_dot[i]
        grad = grad.astype(BF16)
        for n in range(4):
            wait(i, n)
            span = slice(256 * n, 256 * n + 256)
            value = value + jnp.dot(
                grad[:, span], patches[i, span, :], preferred_element_type=F32
            )
    out[...] = value.astype(BF16)


def embed_grad(tokens, partial_logits, comb, row_dot):
    return pl.pallas_call(
        embed_grad_kernel,
        in_specs=[pl.BlockSpec(memory_space=pl.ANY)]
        + [pl.BlockSpec(memory_space=pltpu.VMEM)] * 3,
        out_shape=shape((32, 1280), BF16),
        scratch_shapes=[pltpu.VMEM((2, 1024, 1280), BF16), pltpu.SemaphoreType.DMA((8,))],
        cost_estimate=pl.CostEstimate(flops=170_000_000, bytes_accessed=6_000_000, transcendentals=0),
        compiler_params=MEDIUM,
        name="embed_grad",
    )(in_hbm(tokens), partial_logits, comb, row_dot)


def rows_kernel(*refs):
    parts, inputs = refs[:4], refs[4:8]
    row_dot, mine, other, scratch = refs[8:]
    core = lax.axis_index("core")
    embeds = [
        jnp.concatenate([one[64 + 32 * n : 96 + 32 * n, :] for n in range(5)], axis=1)
        for one in inputs
    ]
    for i in range(2):
        half = slice(32 * i, 32 * i + 32)
        dots = row_dot[i, :, pl.ds(chunk("y", 0, 256), 256)]
        weights = [one[half, 1536:] for one in parts] + [
            (p[half, 1280:1536].astype(F32) - c[half, :].astype(F32) * dots).astype(BF16)
            for p, c in zip(parts, inputs)
        ]
        rows = [one[half, :1280] for one in parts] + embeds
        scratch[i] = lax.dot_general(
            jnp.concatenate(weights), jnp.concatenate(rows), TN, preferred_element_type=F32
        )
        for k in range(4):
            base = ((lax.axis_index("x") + k) & 3) * 64
            here = pl.multiple_of(base + core * 32, 32)
            there = pl.multiple_of(base + (1 - core) * 32, 32)
            mine[k, i] = scratch[i, pl.ds(here, 32), :].astype(BF16)
            other[k, i] = scratch[i, pl.ds(there, 32), :].astype(BF16)


def patch_rows(parts, inputs, row_dot):
    return pl.pallas_call(
        rows_kernel,
        out_shape=[shape((4, 2, 32, 1280), BF16)] * 2,
        scratch_shapes=[pltpu.VMEM((2, 256, 1280), F32)],
        cost_estimate=pl.CostEstimate(flops=335_000_000, bytes_accessed=3_000_000, transcendentals=0),
        compiler_params=MEDIUM,
        name="patch_rows",
    )(*parts, *inputs, row_dot)


def add_kernel(mine, other, o0, o1, o2, o3):
    for k, out in enumerate((o0, o1, o2, o3)):
        out[...] = add(mine[k], other[k])


def add_cores(mine, other):
    return pl.pallas_call(
        add_kernel,
        out_shape=[pltpu.HBM((2, 32, 1280), BF16)] * 4,
        cost_estimate=pl.CostEstimate(flops=327_680, bytes_accessed=2_000_000, transcendentals=0),
        compiler_params=SMALL,
        name="add_cores",
    )(mine, other)


def after(value, *others):
    return lax.optimization_barrier((value, *others))[0]


def sources(terms):
    return [terms[0], terms[3], terms[2], terms[1]]


def local(tokens, slot_embed, combine, w_in, w_out, grad_out):
    w_in, w_out = w_in[0], w_out[0]
    embed = slot_embed.T
    comb = jnp.transpose(combine, (0, 2, 1)).reshape(64, 1024)

    logits, part = local_softmax(tokens, embed)
    comb_late = after(comb, part)
    out_part = jnp.einsum(
        "ijt,itd->ijd", comb_late.reshape(2, 32, 1024), grad_out, preferred_element_type=F32
    )
    out_part = out_part.astype(BF16).reshape(64, 1280)
    part_other = near(part)
    part, out_part = lax.optimization_barrier((part, out_part))
    out_other = near(out_part)
    part = merge_pair(part, part_other)
    comb_late = after(comb_late, part)
    slot_in, lse = merge_last(part, far(part))
    inputs = list(input_blocks(comb_late, embed))
    out_part = add(after(out_part, slot_in), out_other)
    grad_slot_out = add(out_part, far(out_part))

    pre_act = jnp.dot(slot_in, w_in, preferred_element_type=F32)
    act, slope = gelu_parts(pre_act)
    act = act.astype(BF16)
    out_sum = jnp.dot(act, w_out, preferred_element_type=F32).astype(BF16)
    grad_slot_out = after(grad_slot_out, out_sum)
    inputs[3] = after(inputs[3], out_sum)
    inputs = sources(scatter_terms(inputs, "y"))
    out_sum = add(out_sum, near(out_sum))
    out_sum = after(out_sum, *inputs)
    sum_other = far(out_sum)
    grad_act = jnp.einsum("sd,hd->sh", grad_slot_out, w_out, preferred_element_type=F32)
    grad_pre = (grad_act * slope).astype(BF16)
    in_sum = jnp.einsum("sh,dh->sd", grad_pre, w_in, preferred_element_type=F32).astype(BF16)
    in_sum, act_late, slots_late = lax.optimization_barrier(
        (in_sum, act, grad_slot_out, out_sum)
    )[:3]
    in_other = near(in_sum)
    grad_w_out = jnp.einsum("sh,sd->hd", act_late, slots_late, preferred_element_type=F32)
    grad_w_out = grad_w_out.astype(BF16)
    in_sum = add(after(in_sum, grad_w_out), in_other)
    in_other = far(in_sum)

    grad_combine, row_dot = combine_grad(grad_out, out_sum, sum_other, comb)
    grad_slot_in = add(after(in_sum, row_dot), in_other)
    row_dot = row_dot + swap_cores(row_dot)
    late, row_dot = lax.optimization_barrier((grad_slot_in, row_dot))
    row_dot = row_dot + near(row_dot, "x")
    row_dot = row_dot + far(row_dot, "x")
    row_dot = row_dot + near(row_dot, "y")
    row_dot = row_dot + far(row_dot, "y")

    partial_logits, *parts = dispatch_grad(
        tokens, late, slot_in, logits, lse, comb, grad_combine
    )
    parts = sources(scatter_terms(parts, "y"))

    mine, other = patch_rows(parts, inputs, row_dot)
    other_core = swap_cores(other)

    partial_logits, mine = lax.optimization_barrier((partial_logits, mine))
    embed_part = embed_grad(tokens, partial_logits, comb, row_dot)
    sums = add_cores(after(mine, embed_part), other_core)
    embed_part = after(embed_part, sums[0])
    embed_other = near(embed_part)
    terms = scatter_terms(sums, "x")
    grad_tokens = sum(term.astype(F32) for term in terms).astype(BF16)
    embed_part = add(embed_part, embed_other)
    embed_sum = add(embed_part, far(embed_part))
    z = lax.axis_index("seq")
    grad_embed = lax.dynamic_slice_in_dim(embed_sum, z * 320, 320, axis=1).T
    slot_late = after(slot_in, embed_part)
    grad_w_in = jnp.einsum("sd,sh->dh", slot_late, grad_pre, preferred_element_type=F32)
    grad_w_in = grad_w_in.astype(BF16)

    return (
        grad_tokens,
        grad_embed,
        grad_w_in[None],
        grad_w_out[None],
    )


def solution(mesh):
    fine = Mesh(mesh.devices.reshape(4, 4, 4, 2), ("seq", "y", "x", "core"))
    expert = ("y", "x", "core")
    return jax.shard_map(
        local,
        mesh=fine,
        in_specs=(
            P(None, "seq", None),
            P(None, expert),
            P(None, "seq", expert),
            P(expert, None, "seq"),
            P(expert, "seq", None),
            P(None, "seq", None),
        ),
        out_specs=(
            P(None, ("seq", *expert), None),
            P("seq", expert),
            P(expert, None, "seq"),
            P(expert, "seq", None),
        ),
        check_vma=False,
    )
```

```python
import math

import jax
import jax.numpy as jnp
from jax import lax
from jax.experimental import pallas as pl
from jax.experimental.pallas import tpu as pltpu
from jax.sharding import Mesh, PartitionSpec as P

F32 = jnp.float32
BF16 = jnp.bfloat16
NT = (((1,), (1,)), ((), ()))
TN = (((0,), (0,)), ((), ()))
LARGE = pltpu.CompilerParams(vmem_limit_bytes=16 * 1024 * 1024)
MEDIUM = pltpu.CompilerParams(vmem_limit_bytes=10 * 1024 * 1024)
SMALL = pltpu.CompilerParams(vmem_limit_bytes=4 * 1024 * 1024)


def shape(dims, dtype):
    return jax.ShapeDtypeStruct(dims, dtype)


def gelu_parts(values):
    cdf = 0.5 * (1.0 + jax.scipy.special.erf(values / math.sqrt(2.0)))
    slope = cdf + values * jnp.exp(-0.5 * values * values) / math.sqrt(2.0 * math.pi)
    return values * cdf, slope


def shift(value, axis, by):
    return lax.ppermute(value, axis, [(i, (i + by) % 4) for i in range(4)])


def swap_cores(value):
    return lax.ppermute(value, "core", [(0, 1), (1, 0)])


def near(value, axis="seq"):
    return lax.ppermute(value, axis, [(0, 1), (1, 0), (2, 3), (3, 2)])


def far(value, axis="seq"):
    return lax.ppermute(value, axis, [(0, 3), (3, 0), (1, 2), (2, 1)])


def add(one, two):
    return (one.astype(F32) + two.astype(F32)).astype(BF16)


def scatter_terms(blocks, axis):
    return [blocks[0]] + [shift(blocks[k], axis, k) for k in (1, 2, 3)]


def gather_blocks(block, axis):
    return [block] + [shift(block, axis, -k) for k in (1, 2, 3)]


def chunk(axis, k, size):
    return pl.multiple_of(((lax.axis_index(axis) + k) & 3) * size, size)


def lse_lanes(lse):
    high = lse.astype(BF16).astype(F32)
    middle = (lse - high).astype(BF16).astype(F32)
    low = lse - high - middle
    lane = lax.broadcasted_iota(jnp.int32, (lse.shape[0], 128), 1)
    lanes = jnp.where(lane == 0, high, jnp.where(lane == 1, middle, low))
    return jnp.where(lane < 3, lanes, 0.0).astype(BF16)


def lse_column(lanes):
    lanes = lanes.astype(F32)
    return lanes[:, 0:1] + lanes[:, 1:2] + lanes[:, 2:3]


def start_patches(source, target, sems):
    copies = [
        [
            pltpu.make_async_copy(
                source.at[i, pl.ds(256 * n, 256)],
                target.at[i, pl.ds(256 * n, 256)],
                sems.at[4 * i + n],
            )
            for n in range(4)
        ]
        for i in range(2)
    ]
    for i in range(2):
        for n in range(4):
            copies[i][n].start()
    return lambda i, n: copies[i][n].wait()


def softmax_kernel(*refs):
    embed, logits, part = refs[8:]
    columns = embed[...]
    blocks = [[one[0] for one in refs[4 * i : 4 * i + 4]] for i in range(2)]
    scores = [
        jnp.concatenate(
            [lax.dot_general(one, columns, NT, preferred_element_type=F32).T for one in four],
            axis=1,
        )
        for four in blocks
    ]
    for i in range(2):
        half = slice(32 * i, 32 * i + 32)
        logits[half, :] = scores[i]
        peak = jnp.max(scores[i], axis=1, keepdims=True)
        weight = jnp.exp(scores[i] - peak)
        total = jnp.sum(weight, axis=1, keepdims=True)
        weight = weight.astype(BF16)
        sums = 0.0
        for n in range(4):
            sums = sums + jnp.dot(
                weight[:, 256 * n : 256 * n + 256], blocks[i][n], preferred_element_type=F32
            )
        part[half, :1280] = (sums / total).astype(BF16)
        part[half, 1280:] = lse_lanes(peak + jnp.log(total))


def in_hbm(value):
    return pltpu.with_memory_space_constraint(value, pltpu.HBM)


def local_softmax(tokens, embed):
    return pl.pallas_call(
        softmax_kernel,
        grid=(1,),
        in_specs=[
            pl.BlockSpec((1, 256, 1280), lambda t, i=i, n=n: (i, n, 0))
            for i in range(2)
            for n in range(4)
        ]
        + [pl.BlockSpec((32, 1280), lambda t: (0, 0))],
        out_specs=[
            pl.BlockSpec((64, 1024), lambda t: (0, 0)),
            pl.BlockSpec((64, 1408), lambda t: (0, 0)),
        ],
        out_shape=[shape((64, 1024), F32), shape((64, 1408), BF16)],
        cost_estimate=pl.CostEstimate(flops=700_000_000, bytes_accessed=6_000_000, transcendentals=65536),
        compiler_params=LARGE,
        name="local_softmax",
    )(*[in_hbm(tokens)] * 8, in_hbm(embed))


def merge_kernel(one, two, sums, lse):
    lse_a, lse_b = lse_column(one[:, 1280:]), lse_column(two[:, 1280:])
    top = jnp.maximum(lse_a, lse_b)
    weight_a, weight_b = jnp.exp(lse_a - top), jnp.exp(lse_b - top)
    total = weight_a + weight_b
    part = (weight_a / total) * one[:, :1280].astype(F32)
    part = part + (weight_b / total) * two[:, :1280].astype(F32)
    lse_all = top + jnp.log(total)
    sums[:, :1280] = part.astype(BF16)
    if lse is None:
        sums[:, 1280:] = lse_lanes(lse_all)
    else:
        lse[...] = jnp.broadcast_to(lse_all, lse.shape)


def merge_pair(one, two):
    return pl.pallas_call(
        lambda a, b, out: merge_kernel(a, b, out, None),
        out_shape=shape((64, 1408), BF16),
        cost_estimate=pl.CostEstimate(flops=300_000, bytes_accessed=540_000, transcendentals=256),
        compiler_params=SMALL,
        name="merge_pair",
    )(one, two)


def merge_last(one, two):
    return pl.pallas_call(
        merge_kernel,
        out_shape=[shape((64, 1280), BF16), shape((64, 128), F32)],
        cost_estimate=pl.CostEstimate(flops=300_000, bytes_accessed=540_000, transcendentals=256),
        compiler_params=SMALL,
        name="merge_last",
    )(one, two)


def combine_grad_kernel(gout, sum_a, sum_b, comb, grad, row):
    slot_out = add(sum_a[...], sum_b[...])
    for i in range(2):
        half = slice(32 * i, 32 * i + 32)
        value = lax.dot_general(gout[i], slot_out[half, :], NT, preferred_element_type=F32).T
        grad[half, :] = value
        row[i] = jnp.sum(comb[half, :].astype(F32) * value, axis=0, keepdims=True)


def combine_grad(grad_out, sum_a, sum_b, comb):
    return pl.pallas_call(
        combine_grad_kernel,
        out_shape=[shape((64, 1024), F32), shape((2, 1, 1024), F32)],
        cost_estimate=pl.CostEstimate(flops=350_000_000, bytes_accessed=6_000_000, transcendentals=0),
        compiler_params=MEDIUM,
        name="combine_grad",
    )(grad_out, sum_a, sum_b, comb)


def dispatch_grad_kernel(tok, gslot, slot_in, logits, lse, comb, gcomb, full, c0, c1, c2, c3, all_weight):
    for i in range(2):
        half = slice(32 * i, 32 * i + 32)
        rows = gslot[half, :]
        col_dot = jnp.sum(slot_in[half, :].astype(F32) * rows.astype(F32), axis=1, keepdims=True)
        grad = lax.dot_general(tok[i], rows, NT, preferred_element_type=F32).T
        weight = jnp.exp(logits[half, :] - lse[half, :1])
        full[half, :] = weight * (grad - col_dot) + comb[half, :].astype(F32) * gcomb[half, :]
        all_weight[half, :] = weight
        for k, out in enumerate((c0, c1, c2, c3)):
            piece = pl.ds(chunk("y", k, 256), 256)
            out[half, :1280] = rows
            out[half, 1280:1536] = full[half, piece].astype(BF16)
            out[half, 1536:] = all_weight[half, piece].astype(BF16)


def dispatch_grad(tokens, gslot, slot_in, logits, lse, comb, gcomb):
    return pl.pallas_call(
        dispatch_grad_kernel,
        out_shape=[shape((64, 1024), F32)] + [shape((64, 1792), BF16)] * 4,
        scratch_shapes=[pltpu.VMEM((64, 1024), F32)],
        cost_estimate=pl.CostEstimate(flops=350_000_000, bytes_accessed=7_000_000, transcendentals=65536),
        compiler_params=MEDIUM,
        name="dispatch_grad",
    )(tokens, gslot, slot_in, logits, lse, comb, gcomb)


def inputs_kernel(comb, embed, o0, o1, o2, o3):
    for k, out in enumerate((o0, o1, o2, o3)):
        out[:64, :] = comb[:, pl.ds(chunk("y", k, 256), 256)]
        for n in range(5):
            out[64 + 32 * n : 96 + 32 * n, :] = embed[:, 256 * n : 256 * n + 256]


def input_blocks(comb, embed):
    return pl.pallas_call(
        inputs_kernel,
        out_shape=[shape((224, 256), BF16)] * 4,
        cost_estimate=pl.CostEstimate(flops=0, bytes_accessed=700_000, transcendentals=0),
        compiler_params=SMALL,
        name="input_blocks",
    )(comb, embed)


def embed_grad_kernel(tok, partial_logits, comb, row_dot, out, patches, sems):
    wait = start_patches(tok, patches, sems)
    value = 0.0
    for i in range(2):
        half = slice(32 * i, 32 * i + 32)
        grad = partial_logits[half, :] - comb[half, :].astype(F32) * row_dot[i]
        grad = grad.astype(BF16)
        for n in range(4):
            wait(i, n)
            span = slice(256 * n, 256 * n + 256)
            value = value + jnp.dot(
                grad[:, span], patches[i, span, :], preferred_element_type=F32
            )
    out[...] = value.astype(BF16)


def embed_grad(tokens, partial_logits, comb, row_dot):
    return pl.pallas_call(
        embed_grad_kernel,
        in_specs=[pl.BlockSpec(memory_space=pl.ANY)]
        + [pl.BlockSpec(memory_space=pltpu.VMEM)] * 3,
        out_shape=shape((32, 1280), BF16),
        scratch_shapes=[pltpu.VMEM((2, 1024, 1280), BF16), pltpu.SemaphoreType.DMA((8,))],
        cost_estimate=pl.CostEstimate(flops=170_000_000, bytes_accessed=6_000_000, transcendentals=0),
        compiler_params=MEDIUM,
        name="embed_grad",
    )(in_hbm(tokens), partial_logits, comb, row_dot)


def rows_kernel(*refs):
    parts, inputs = refs[:4], refs[4:8]
    row_dot, mine, other, scratch = refs[8:]
    core = lax.axis_index("core")
    embeds = [
        jnp.concatenate([one[64 + 32 * n : 96 + 32 * n, :] for n in range(5)], axis=1)
        for one in inputs
    ]
    for i in range(2):
        half = slice(32 * i, 32 * i + 32)
        dots = row_dot[i, :, pl.ds(chunk("y", 0, 256), 256)]
        weights = [one[half, 1536:] for one in parts] + [
            (p[half, 1280:1536].astype(F32) - c[half, :].astype(F32) * dots).astype(BF16)
            for p, c in zip(parts, inputs)
        ]
        rows = [one[half, :1280] for one in parts] + embeds
        scratch[i] = lax.dot_general(
            jnp.concatenate(weights), jnp.concatenate(rows), TN, preferred_element_type=F32
        )
        for k in range(4):
            base = ((lax.axis_index("x") + k) & 3) * 64
            here = pl.multiple_of(base + core * 32, 32)
            there = pl.multiple_of(base + (1 - core) * 32, 32)
            mine[k, i] = scratch[i, pl.ds(here, 32), :].astype(BF16)
            other[k, i] = scratch[i, pl.ds(there, 32), :].astype(BF16)


def patch_rows(parts, inputs, row_dot):
    return pl.pallas_call(
        rows_kernel,
        out_shape=[shape((4, 2, 32, 1280), BF16)] * 2,
        scratch_shapes=[pltpu.VMEM((2, 256, 1280), F32)],
        cost_estimate=pl.CostEstimate(flops=335_000_000, bytes_accessed=3_000_000, transcendentals=0),
        compiler_params=MEDIUM,
        name="patch_rows",
    )(*parts, *inputs, row_dot)


def add_kernel(mine, other, o0, o1, o2, o3):
    for k, out in enumerate((o0, o1, o2, o3)):
        out[...] = add(mine[k], other[k])


def add_cores(mine, other):
    return pl.pallas_call(
        add_kernel,
        out_shape=[pltpu.HBM((2, 32, 1280), BF16)] * 4,
        cost_estimate=pl.CostEstimate(flops=327_680, bytes_accessed=2_000_000, transcendentals=0),
        compiler_params=SMALL,
        name="add_cores",
    )(mine, other)


def after(value, *others):
    return lax.optimization_barrier((value, *others))[0]


def sources(terms):
    return [terms[0], terms[3], terms[2], terms[1]]


def local(tokens, slot_embed, combine, w_in, w_out, grad_out):
    w_in, w_out = w_in[0], w_out[0]
    embed = slot_embed.T
    comb = jnp.transpose(combine, (0, 2, 1)).reshape(64, 1024)

    logits, part = local_softmax(tokens, embed)
    comb_late = after(comb, part)
    out_part = jnp.einsum(
        "ijt,itd->ijd", comb_late.reshape(2, 32, 1024), grad_out, preferred_element_type=F32
    )
    out_part = out_part.astype(BF16).reshape(64, 1280)
    part_other = near(part)
    part, out_part = lax.optimization_barrier((part, out_part))
    out_other = far(out_part)
    part = merge_pair(part, part_other)
    out_part = add(after(out_part, part), out_other)
    grad_slot_out = add(out_part, near(out_part))
    slot_in, lse = merge_last(part, far(part))
    inputs = list(input_blocks(after(comb_late, out_part), embed))

    pre_act = jnp.dot(slot_in, w_in, preferred_element_type=F32)
    act, slope = gelu_parts(pre_act)
    act = act.astype(BF16)
    out_sum = jnp.dot(act, w_out, preferred_element_type=F32).astype(BF16)
    grad_slot_out = after(grad_slot_out, out_sum)
    inputs[3] = after(inputs[3], out_sum)
    inputs = sources(scatter_terms(inputs, "y"))
    out_sum = add(out_sum, near(out_sum))
    out_sum = after(out_sum, *inputs)
    sum_other = far(out_sum)
    grad_act = jnp.einsum("sd,hd->sh", grad_slot_out, w_out, preferred_element_type=F32)
    grad_pre = (grad_act * slope).astype(BF16)
    in_sum = jnp.einsum("sh,dh->sd", grad_pre, w_in, preferred_element_type=F32).astype(BF16)
    in_sum, act_late, slots_late = lax.optimization_barrier(
        (in_sum, act, grad_slot_out, out_sum)
    )[:3]
    in_other = near(in_sum)
    grad_w_out = jnp.einsum("sh,sd->hd", act_late, slots_late, preferred_element_type=F32)
    grad_w_out = grad_w_out.astype(BF16)
    in_sum = add(after(in_sum, grad_w_out), in_other)
    in_other = far(in_sum)

    grad_combine, row_dot = combine_grad(grad_out, out_sum, sum_other, comb)
    grad_slot_in = add(after(in_sum, row_dot), in_other)
    row_dot = row_dot + swap_cores(row_dot)
    late, row_dot = lax.optimization_barrier((grad_slot_in, row_dot))
    row_dot = row_dot + near(row_dot, "x")
    row_dot = row_dot + far(row_dot, "x")
    row_dot = row_dot + near(row_dot, "y")
    row_dot = row_dot + far(row_dot, "y")

    partial_logits, *parts = dispatch_grad(
        tokens, late, slot_in, logits, lse, comb, grad_combine
    )
    parts = sources(scatter_terms(parts, "y"))

    mine, other = patch_rows(parts, inputs, row_dot)
    other_core = swap_cores(other)

    partial_logits, mine = lax.optimization_barrier((partial_logits, mine))
    embed_part = embed_grad(tokens, partial_logits, comb, row_dot)
    sums = add_cores(after(mine, embed_part), other_core)
    embed_part = after(embed_part, sums[0])
    embed_other = near(embed_part)
    terms = scatter_terms(sums, "x")
    grad_tokens = sum(term.astype(F32) for term in terms).astype(BF16)
    embed_part = add(embed_part, embed_other)
    embed_sum = add(embed_part, far(embed_part))
    z = lax.axis_index("seq")
    grad_embed = lax.dynamic_slice_in_dim(embed_sum, z * 320, 320, axis=1).T
    slot_late = after(slot_in, embed_part)
    grad_w_in = jnp.einsum("sd,sh->dh", slot_late, grad_pre, preferred_element_type=F32)
    grad_w_in = grad_w_in.astype(BF16)

    return (
        grad_tokens,
        grad_embed,
        grad_w_in[None],
        grad_w_out[None],
    )


def solution(mesh):
    fine = Mesh(mesh.devices.reshape(4, 4, 4, 2), ("seq", "y", "x", "core"))
    expert = ("y", "x", "core")
    return jax.shard_map(
        local,
        mesh=fine,
        in_specs=(
            P(None, "seq", None),
            P(None, expert),
            P(None, "seq", expert),
            P(expert, None, "seq"),
            P(expert, "seq", None),
            P(None, "seq", None),
        ),
        out_specs=(
            P(None, ("seq", *expert), None),
            P("seq", expert),
            P(expert, None, "seq"),
            P(expert, "seq", None),
        ),
        check_vma=False,
    )
```

```python
import math

import jax
import jax.numpy as jnp
from jax import lax
from jax.experimental import pallas as pl
from jax.experimental.pallas import tpu as pltpu
from jax.sharding import Mesh, PartitionSpec as P

F32 = jnp.float32
BF16 = jnp.bfloat16
NT = (((1,), (1,)), ((), ()))
TN = (((0,), (0,)), ((), ()))
LARGE = pltpu.CompilerParams(vmem_limit_bytes=16 * 1024 * 1024)
MEDIUM = pltpu.CompilerParams(vmem_limit_bytes=10 * 1024 * 1024)
SMALL = pltpu.CompilerParams(vmem_limit_bytes=4 * 1024 * 1024)


def shape(dims, dtype):
    return jax.ShapeDtypeStruct(dims, dtype)


def gelu_parts(values):
    cdf = 0.5 * (1.0 + jax.scipy.special.erf(values / math.sqrt(2.0)))
    slope = cdf + values * jnp.exp(-0.5 * values * values) / math.sqrt(2.0 * math.pi)
    return values * cdf, slope


def shift(value, axis, by):
    return lax.ppermute(value, axis, [(i, (i + by) % 4) for i in range(4)])


def swap_cores(value):
    return lax.ppermute(value, "core", [(0, 1), (1, 0)])


def near(value, axis="seq"):
    return lax.ppermute(value, axis, [(0, 1), (1, 0), (2, 3), (3, 2)])


def far(value, axis="seq"):
    return lax.ppermute(value, axis, [(0, 3), (3, 0), (1, 2), (2, 1)])


def add(one, two):
    return (one.astype(F32) + two.astype(F32)).astype(BF16)


def scatter_terms(blocks, axis):
    return [blocks[0]] + [shift(blocks[k], axis, k) for k in (1, 2, 3)]


def gather_blocks(block, axis):
    return [block] + [shift(block, axis, -k) for k in (1, 2, 3)]


def chunk(axis, k, size):
    return pl.multiple_of(((lax.axis_index(axis) + k) & 3) * size, size)


def lse_lanes(lse):
    high = lse.astype(BF16).astype(F32)
    middle = (lse - high).astype(BF16).astype(F32)
    low = lse - high - middle
    lane = lax.broadcasted_iota(jnp.int32, (lse.shape[0], 128), 1)
    lanes = jnp.where(lane == 0, high, jnp.where(lane == 1, middle, low))
    return jnp.where(lane < 3, lanes, 0.0).astype(BF16)


def lse_column(lanes):
    lanes = lanes.astype(F32)
    return lanes[:, 0:1] + lanes[:, 1:2] + lanes[:, 2:3]


def start_patches(source, target, sems):
    copies = [
        [
            pltpu.make_async_copy(
                source.at[i, pl.ds(256 * n, 256)],
                target.at[i, pl.ds(256 * n, 256)],
                sems.at[4 * i + n],
            )
            for n in range(4)
        ]
        for i in range(2)
    ]
    for i in range(2):
        for n in range(4):
            copies[i][n].start()
    return lambda i, n: copies[i][n].wait()


def softmax_kernel(*refs):
    embed, logits, part = refs[8:]
    columns = embed[...]
    blocks = [[one[0] for one in refs[4 * i : 4 * i + 4]] for i in range(2)]
    scores = [
        jnp.concatenate(
            [lax.dot_general(one, columns, NT, preferred_element_type=F32).T for one in four],
            axis=1,
        )
        for four in blocks
    ]
    for i in range(2):
        half = slice(32 * i, 32 * i + 32)
        logits[half, :] = scores[i]
        peak = jnp.max(scores[i], axis=1, keepdims=True)
        weight = jnp.exp(scores[i] - peak)
        total = jnp.sum(weight, axis=1, keepdims=True)
        weight = weight.astype(BF16)
        sums = 0.0
        for n in range(4):
            sums = sums + jnp.dot(
                weight[:, 256 * n : 256 * n + 256], blocks[i][n], preferred_element_type=F32
            )
        part[half, :1280] = (sums / total).astype(BF16)
        part[half, 1280:] = lse_lanes(peak + jnp.log(total))


def in_hbm(value):
    return pltpu.with_memory_space_constraint(value, pltpu.HBM)


def local_softmax(tokens, embed):
    return pl.pallas_call(
        softmax_kernel,
        grid=(1,),
        in_specs=[
            pl.BlockSpec((1, 256, 1280), lambda t, i=i, n=n: (i, n, 0))
            for i in range(2)
            for n in range(4)
        ]
        + [pl.BlockSpec((32, 1280), lambda t: (0, 0))],
        out_specs=[
            pl.BlockSpec((64, 1024), lambda t: (0, 0)),
            pl.BlockSpec((64, 1408), lambda t: (0, 0)),
        ],
        out_shape=[shape((64, 1024), F32), shape((64, 1408), BF16)],
        cost_estimate=pl.CostEstimate(flops=700_000_000, bytes_accessed=6_000_000, transcendentals=65536),
        compiler_params=LARGE,
        name="local_softmax",
    )(*[in_hbm(tokens)] * 8, in_hbm(embed))


def merge_kernel(one, two, sums, lse):
    lse_a, lse_b = lse_column(one[:, 1280:]), lse_column(two[:, 1280:])
    top = jnp.maximum(lse_a, lse_b)
    weight_a, weight_b = jnp.exp(lse_a - top), jnp.exp(lse_b - top)
    total = weight_a + weight_b
    part = (weight_a / total) * one[:, :1280].astype(F32)
    part = part + (weight_b / total) * two[:, :1280].astype(F32)
    lse_all = top + jnp.log(total)
    sums[:, :1280] = part.astype(BF16)
    if lse is None:
        sums[:, 1280:] = lse_lanes(lse_all)
    else:
        lse[...] = jnp.broadcast_to(lse_all, lse.shape)


def merge_pair(one, two):
    return pl.pallas_call(
        lambda a, b, out: merge_kernel(a, b, out, None),
        out_shape=shape((64, 1408), BF16),
        cost_estimate=pl.CostEstimate(flops=300_000, bytes_accessed=540_000, transcendentals=256),
        compiler_params=SMALL,
        name="merge_pair",
    )(one, two)


def merge_last(one, two):
    return pl.pallas_call(
        merge_kernel,
        out_shape=[shape((64, 1280), BF16), shape((64, 128), F32)],
        cost_estimate=pl.CostEstimate(flops=300_000, bytes_accessed=540_000, transcendentals=256),
        compiler_params=SMALL,
        name="merge_last",
    )(one, two)


def combine_grad_kernel(gout, sum_a, sum_b, comb, grad, row):
    slot_out = add(sum_a[...], sum_b[...])
    for i in range(2):
        half = slice(32 * i, 32 * i + 32)
        value = lax.dot_general(gout[i], slot_out[half, :], NT, preferred_element_type=F32).T
        grad[half, :] = value
        row[i] = jnp.sum(comb[half, :].astype(F32) * value, axis=0, keepdims=True)


def combine_grad(grad_out, sum_a, sum_b, comb):
    return pl.pallas_call(
        combine_grad_kernel,
        out_shape=[shape((64, 1024), F32), shape((2, 1, 1024), F32)],
        cost_estimate=pl.CostEstimate(flops=350_000_000, bytes_accessed=6_000_000, transcendentals=0),
        compiler_params=MEDIUM,
        name="combine_grad",
    )(grad_out, sum_a, sum_b, comb)


def dispatch_grad_kernel(tok, gslot, slot_in, logits, lse, comb, gcomb, full, c0, c1, c2, c3, all_weight):
    for i in range(2):
        half = slice(32 * i, 32 * i + 32)
        rows = gslot[half, :]
        col_dot = jnp.sum(slot_in[half, :].astype(F32) * rows.astype(F32), axis=1, keepdims=True)
        grad = lax.dot_general(tok[i], rows, NT, preferred_element_type=F32).T
        weight = jnp.exp(logits[half, :] - lse[half, :1])
        full[half, :] = weight * (grad - col_dot) + comb[half, :].astype(F32) * gcomb[half, :]
        all_weight[half, :] = weight
        for k, out in enumerate((c0, c1, c2, c3)):
            piece = pl.ds(chunk("y", k, 256), 256)
            out[half, :1280] = rows
            out[half, 1280:1536] = full[half, piece].astype(BF16)
            out[half, 1536:] = all_weight[half, piece].astype(BF16)


def dispatch_grad(tokens, gslot, slot_in, logits, lse, comb, gcomb):
    return pl.pallas_call(
        dispatch_grad_kernel,
        out_shape=[shape((64, 1024), F32)] + [shape((64, 1792), BF16)] * 4,
        scratch_shapes=[pltpu.VMEM((64, 1024), F32)],
        cost_estimate=pl.CostEstimate(flops=350_000_000, bytes_accessed=7_000_000, transcendentals=65536),
        compiler_params=MEDIUM,
        name="dispatch_grad",
    )(tokens, gslot, slot_in, logits, lse, comb, gcomb)


def inputs_kernel(comb, embed, o0, o1, o2, o3):
    for k, out in enumerate((o0, o1, o2, o3)):
        out[:64, :] = comb[:, pl.ds(chunk("y", k, 256), 256)]
        for n in range(5):
            out[64 + 32 * n : 96 + 32 * n, :] = embed[:, 256 * n : 256 * n + 256]


def input_blocks(comb, embed):
    return pl.pallas_call(
        inputs_kernel,
        out_shape=[shape((224, 256), BF16)] * 4,
        cost_estimate=pl.CostEstimate(flops=0, bytes_accessed=700_000, transcendentals=0),
        compiler_params=SMALL,
        name="input_blocks",
    )(comb, embed)


def embed_grad_kernel(tok, partial_logits, comb, row_dot, out, patches, sems):
    wait = start_patches(tok, patches, sems)
    value = 0.0
    for i in range(2):
        half = slice(32 * i, 32 * i + 32)
        grad = partial_logits[half, :] - comb[half, :].astype(F32) * row_dot[i]
        grad = grad.astype(BF16)
        for n in range(4):
            wait(i, n)
            span = slice(256 * n, 256 * n + 256)
            value = value + jnp.dot(
                grad[:, span], patches[i, span, :], preferred_element_type=F32
            )
    out[...] = value.astype(BF16)


def embed_grad(tokens, partial_logits, comb, row_dot):
    return pl.pallas_call(
        embed_grad_kernel,
        in_specs=[pl.BlockSpec(memory_space=pl.ANY)]
        + [pl.BlockSpec(memory_space=pltpu.VMEM)] * 3,
        out_shape=shape((32, 1280), BF16),
        scratch_shapes=[pltpu.VMEM((2, 1024, 1280), BF16), pltpu.SemaphoreType.DMA((8,))],
        cost_estimate=pl.CostEstimate(flops=170_000_000, bytes_accessed=6_000_000, transcendentals=0),
        compiler_params=MEDIUM,
        name="embed_grad",
    )(in_hbm(tokens), partial_logits, comb, row_dot)


def rows_kernel(*refs):
    parts, inputs = refs[:4], refs[4:8]
    row_dot, mine, other, scratch = refs[8:]
    core = lax.axis_index("core")
    embeds = [
        jnp.concatenate([one[64 + 32 * n : 96 + 32 * n, :] for n in range(5)], axis=1)
        for one in inputs
    ]
    for i in range(2):
        half = slice(32 * i, 32 * i + 32)
        dots = row_dot[i, :, pl.ds(chunk("y", 0, 256), 256)]
        weights = [one[half, 1536:] for one in parts] + [
            (p[half, 1280:1536].astype(F32) - c[half, :].astype(F32) * dots).astype(BF16)
            for p, c in zip(parts, inputs)
        ]
        rows = [one[half, :1280] for one in parts] + embeds
        scratch[i] = lax.dot_general(
            jnp.concatenate(weights), jnp.concatenate(rows), TN, preferred_element_type=F32
        )
        for k in range(4):
            base = ((lax.axis_index("x") + k) & 3) * 64
            here = pl.multiple_of(base + core * 32, 32)
            there = pl.multiple_of(base + (1 - core) * 32, 32)
            mine[k, i] = scratch[i, pl.ds(here, 32), :].astype(BF16)
            other[k, i] = scratch[i, pl.ds(there, 32), :].astype(BF16)


def patch_rows(parts, inputs, row_dot):
    return pl.pallas_call(
        rows_kernel,
        out_shape=[shape((4, 2, 32, 1280), BF16)] * 2,
        scratch_shapes=[pltpu.VMEM((2, 256, 1280), F32)],
        cost_estimate=pl.CostEstimate(flops=335_000_000, bytes_accessed=3_000_000, transcendentals=0),
        compiler_params=MEDIUM,
        name="patch_rows",
    )(*parts, *inputs, row_dot)


def add_kernel(mine, other, o0, o1, o2, o3):
    for k, out in enumerate((o0, o1, o2, o3)):
        out[...] = add(mine[k], other[k])


def add_cores(mine, other):
    return pl.pallas_call(
        add_kernel,
        out_shape=[pltpu.HBM((2, 32, 1280), BF16)] * 4,
        cost_estimate=pl.CostEstimate(flops=327_680, bytes_accessed=2_000_000, transcendentals=0),
        compiler_params=SMALL,
        name="add_cores",
    )(mine, other)


def after(value, *others):
    return lax.optimization_barrier((value, *others))[0]


def sources(terms):
    return [terms[0], terms[3], terms[2], terms[1]]


def local(tokens, slot_embed, combine, w_in, w_out, grad_out):
    w_in, w_out = w_in[0], w_out[0]
    embed = slot_embed.T
    comb = jnp.transpose(combine, (0, 2, 1)).reshape(64, 1024)

    logits, part = local_softmax(tokens, embed)
    comb_late = after(comb, part)
    out_part = jnp.einsum(
        "ijt,itd->ijd", comb_late.reshape(2, 32, 1024), grad_out, preferred_element_type=F32
    )
    out_part = out_part.astype(BF16).reshape(64, 1280)
    part_other = near(part)
    part, out_part = lax.optimization_barrier((part, out_part))
    out_other = far(out_part)
    part = merge_pair(part, part_other)
    out_part = add(after(out_part, part), out_other)
    out_other = near(out_part)
    slot_in, lse = merge_last(part, far(part))
    inputs = list(input_blocks(after(comb_late, out_part), embed))

    pre_act = jnp.dot(slot_in, w_in, preferred_element_type=F32)
    act, slope = gelu_parts(pre_act)
    act = act.astype(BF16)
    out_sum = jnp.dot(act, w_out, preferred_element_type=F32).astype(BF16)
    grad_slot_out = add(after(out_part, out_sum), out_other)
    inputs[3] = after(inputs[3], out_sum)
    inputs = sources(scatter_terms(inputs, "y"))
    out_sum = add(out_sum, near(out_sum))
    out_sum = after(out_sum, *inputs)
    sum_other = far(out_sum)
    grad_act = jnp.einsum("sd,hd->sh", grad_slot_out, w_out, preferred_element_type=F32)
    grad_pre = (grad_act * slope).astype(BF16)
    in_sum = jnp.einsum("sh,dh->sd", grad_pre, w_in, preferred_element_type=F32).astype(BF16)
    in_sum, act_late, slots_late = lax.optimization_barrier(
        (in_sum, act, grad_slot_out, out_sum)
    )[:3]
    in_other = near(in_sum)
    grad_w_out = jnp.einsum("sh,sd->hd", act_late, slots_late, preferred_element_type=F32)
    grad_w_out = grad_w_out.astype(BF16)
    in_sum = add(after(in_sum, grad_w_out), in_other)
    in_other = far(in_sum)

    grad_combine, row_dot = combine_grad(grad_out, out_sum, sum_other, comb)
    grad_slot_in = add(after(in_sum, row_dot), in_other)
    row_dot = row_dot + swap_cores(row_dot)
    late, row_dot = lax.optimization_barrier((grad_slot_in, row_dot))
    row_dot = row_dot + near(row_dot, "x")
    row_dot = row_dot + far(row_dot, "x")
    row_dot = row_dot + near(row_dot, "y")
    row_dot = row_dot + far(row_dot, "y")

    partial_logits, *parts = dispatch_grad(
        tokens, late, slot_in, logits, lse, comb, grad_combine
    )
    parts = sources(scatter_terms(parts, "y"))

    mine, other = patch_rows(parts, inputs, row_dot)
    other_core = swap_cores(other)

    partial_logits, mine = lax.optimization_barrier((partial_logits, mine))
    embed_part = embed_grad(tokens, partial_logits, comb, row_dot)
    sums = add_cores(after(mine, embed_part), other_core)
    embed_part = after(embed_part, sums[0])
    embed_other = near(embed_part)
    terms = scatter_terms(sums, "x")
    grad_tokens = sum(term.astype(F32) for term in terms).astype(BF16)
    embed_part = add(embed_part, embed_other)
    embed_sum = add(embed_part, far(embed_part))
    z = lax.axis_index("seq")
    grad_embed = lax.dynamic_slice_in_dim(embed_sum, z * 320, 320, axis=1).T
    slot_late = after(slot_in, embed_part)
    grad_w_in = jnp.einsum("sd,sh->dh", slot_late, grad_pre, preferred_element_type=F32)
    grad_w_in = grad_w_in.astype(BF16)

    return (
        grad_tokens,
        grad_embed,
        grad_w_in[None],
        grad_w_out[None],
    )


def solution(mesh):
    fine = Mesh(mesh.devices.reshape(4, 4, 4, 2), ("seq", "y", "x", "core"))
    expert = ("y", "x", "core")
    return jax.shard_map(
        local,
        mesh=fine,
        in_specs=(
            P(None, "seq", None),
            P(None, expert),
            P(None, "seq", expert),
            P(expert, None, "seq"),
            P(expert, "seq", None),
            P(None, "seq", None),
        ),
        out_specs=(
            P(None, ("seq", *expert), None),
            P("seq", expert),
            P(expert, None, "seq"),
            P(expert, "seq", None),
        ),
        check_vma=False,
    )
```

```python
import math

import jax
import jax.numpy as jnp
from jax import lax
from jax.experimental import pallas as pl
from jax.experimental.pallas import tpu as pltpu
from jax.sharding import Mesh, PartitionSpec as P

F32 = jnp.float32
BF16 = jnp.bfloat16
NT = (((1,), (1,)), ((), ()))
TN = (((0,), (0,)), ((), ()))
LARGE = pltpu.CompilerParams(vmem_limit_bytes=16 * 1024 * 1024)
MEDIUM = pltpu.CompilerParams(vmem_limit_bytes=10 * 1024 * 1024)
SMALL = pltpu.CompilerParams(vmem_limit_bytes=4 * 1024 * 1024)


def shape(dims, dtype):
    return jax.ShapeDtypeStruct(dims, dtype)


def gelu_parts(values):
    cdf = 0.5 * (1.0 + jax.scipy.special.erf(values / math.sqrt(2.0)))
    slope = cdf + values * jnp.exp(-0.5 * values * values) / math.sqrt(2.0 * math.pi)
    return values * cdf, slope


def shift(value, axis, by):
    return lax.ppermute(value, axis, [(i, (i + by) % 4) for i in range(4)])


def swap_cores(value):
    return lax.ppermute(value, "core", [(0, 1), (1, 0)])


def near(value, axis="seq"):
    return lax.ppermute(value, axis, [(0, 1), (1, 0), (2, 3), (3, 2)])


def far(value, axis="seq"):
    return lax.ppermute(value, axis, [(0, 3), (3, 0), (1, 2), (2, 1)])


def add(one, two):
    return (one.astype(F32) + two.astype(F32)).astype(BF16)


def scatter_terms(blocks, axis):
    return [blocks[0]] + [shift(blocks[k], axis, k) for k in (1, 2, 3)]


def gather_blocks(block, axis):
    return [block] + [shift(block, axis, -k) for k in (1, 2, 3)]


def chunk(axis, k, size):
    return pl.multiple_of(((lax.axis_index(axis) + k) & 3) * size, size)


def lse_lanes(lse):
    high = lse.astype(BF16).astype(F32)
    middle = (lse - high).astype(BF16).astype(F32)
    low = lse - high - middle
    lane = lax.broadcasted_iota(jnp.int32, (lse.shape[0], 128), 1)
    lanes = jnp.where(lane == 0, high, jnp.where(lane == 1, middle, low))
    return jnp.where(lane < 3, lanes, 0.0).astype(BF16)


def lse_column(lanes):
    lanes = lanes.astype(F32)
    return lanes[:, 0:1] + lanes[:, 1:2] + lanes[:, 2:3]


def start_patches(source, target, sems):
    copies = [
        [
            pltpu.make_async_copy(
                source.at[i, pl.ds(256 * n, 256)],
                target.at[i, pl.ds(256 * n, 256)],
                sems.at[4 * i + n],
            )
            for n in range(4)
        ]
        for i in range(2)
    ]
    for i in range(2):
        for n in range(4):
            copies[i][n].start()
    return lambda i, n: copies[i][n].wait()


def softmax_kernel(*refs):
    embed, logits, part = refs[8:]
    columns = embed[...]
    blocks = [[one[0] for one in refs[4 * i : 4 * i + 4]] for i in range(2)]
    scores = [
        jnp.concatenate(
            [lax.dot_general(one, columns, NT, preferred_element_type=F32).T for one in four],
            axis=1,
        )
        for four in blocks
    ]
    for i in range(2):
        half = slice(32 * i, 32 * i + 32)
        logits[half, :] = scores[i]
        peak = jnp.max(scores[i], axis=1, keepdims=True)
        weight = jnp.exp(scores[i] - peak)
        total = jnp.sum(weight, axis=1, keepdims=True)
        weight = weight.astype(BF16)
        sums = 0.0
        for n in range(4):
            sums = sums + jnp.dot(
                weight[:, 256 * n : 256 * n + 256], blocks[i][n], preferred_element_type=F32
            )
        part[half, :1280] = (sums / total).astype(BF16)
        part[half, 1280:] = lse_lanes(peak + jnp.log(total))


def in_hbm(value):
    return pltpu.with_memory_space_constraint(value, pltpu.HBM)


def local_softmax(tokens, embed):
    return pl.pallas_call(
        softmax_kernel,
        grid=(1,),
        in_specs=[
            pl.BlockSpec((1, 256, 1280), lambda t, i=i, n=n: (i, n, 0))
            for i in range(2)
            for n in range(4)
        ]
        + [pl.BlockSpec((32, 1280), lambda t: (0, 0))],
        out_specs=[
            pl.BlockSpec((64, 1024), lambda t: (0, 0)),
            pl.BlockSpec((64, 1408), lambda t: (0, 0)),
        ],
        out_shape=[shape((64, 1024), F32), shape((64, 1408), BF16)],
        cost_estimate=pl.CostEstimate(flops=700_000_000, bytes_accessed=6_000_000, transcendentals=65536),
        compiler_params=LARGE,
        name="local_softmax",
    )(*[in_hbm(tokens)] * 8, in_hbm(embed))


def merge_kernel(one, two, sums, lse):
    lse_a, lse_b = lse_column(one[:, 1280:]), lse_column(two[:, 1280:])
    top = jnp.maximum(lse_a, lse_b)
    weight_a, weight_b = jnp.exp(lse_a - top), jnp.exp(lse_b - top)
    total = weight_a + weight_b
    part = (weight_a / total) * one[:, :1280].astype(F32)
    part = part + (weight_b / total) * two[:, :1280].astype(F32)
    lse_all = top + jnp.log(total)
    sums[:, :1280] = part.astype(BF16)
    if lse is None:
        sums[:, 1280:] = lse_lanes(lse_all)
    else:
        lse[...] = jnp.broadcast_to(lse_all, lse.shape)


def merge_pair(one, two):
    return pl.pallas_call(
        lambda a, b, out: merge_kernel(a, b, out, None),
        out_shape=shape((64, 1408), BF16),
        cost_estimate=pl.CostEstimate(flops=300_000, bytes_accessed=540_000, transcendentals=256),
        compiler_params=SMALL,
        name="merge_pair",
    )(one, two)


def merge_last(one, two):
    return pl.pallas_call(
        merge_kernel,
        out_shape=[shape((64, 1280), BF16), shape((64, 128), F32)],
        cost_estimate=pl.CostEstimate(flops=300_000, bytes_accessed=540_000, transcendentals=256),
        compiler_params=SMALL,
        name="merge_last",
    )(one, two)


def combine_grad_kernel(gout, sum_a, sum_b, comb, grad, row):
    slot_out = add(sum_a[...], sum_b[...])
    for i in range(2):
        half = slice(32 * i, 32 * i + 32)
        value = lax.dot_general(gout[i], slot_out[half, :], NT, preferred_element_type=F32).T
        grad[half, :] = value
        row[i] = jnp.sum(comb[half, :].astype(F32) * value, axis=0, keepdims=True)


def combine_grad(grad_out, sum_a, sum_b, comb):
    return pl.pallas_call(
        combine_grad_kernel,
        out_shape=[shape((64, 1024), F32), shape((2, 1, 1024), F32)],
        cost_estimate=pl.CostEstimate(flops=350_000_000, bytes_accessed=6_000_000, transcendentals=0),
        compiler_params=MEDIUM,
        name="combine_grad",
    )(grad_out, sum_a, sum_b, comb)


def dispatch_grad_kernel(tok, gslot, slot_in, logits, lse, comb, gcomb, full, c0, c1, c2, c3, all_weight):
    for i in range(2):
        half = slice(32 * i, 32 * i + 32)
        rows = gslot[half, :]
        col_dot = jnp.sum(slot_in[half, :].astype(F32) * rows.astype(F32), axis=1, keepdims=True)
        grad = lax.dot_general(tok[i], rows, NT, preferred_element_type=F32).T
        weight = jnp.exp(logits[half, :] - lse[half, :1])
        full[half, :] = weight * (grad - col_dot) + comb[half, :].astype(F32) * gcomb[half, :]
        all_weight[half, :] = weight
        for k, out in enumerate((c0, c1, c2, c3)):
            piece = pl.ds(chunk("y", k, 256), 256)
            out[half, :1280] = rows
            out[half, 1280:1536] = full[half, piece].astype(BF16)
            out[half, 1536:] = all_weight[half, piece].astype(BF16)


def dispatch_grad(tokens, gslot, slot_in, logits, lse, comb, gcomb):
    return pl.pallas_call(
        dispatch_grad_kernel,
        out_shape=[shape((64, 1024), F32)] + [shape((64, 1792), BF16)] * 4,
        scratch_shapes=[pltpu.VMEM((64, 1024), F32)],
        cost_estimate=pl.CostEstimate(flops=350_000_000, bytes_accessed=7_000_000, transcendentals=65536),
        compiler_params=MEDIUM,
        name="dispatch_grad",
    )(tokens, gslot, slot_in, logits, lse, comb, gcomb)


def inputs_kernel(comb, embed, o0, o1, o2, o3):
    for k, out in enumerate((o0, o1, o2, o3)):
        out[:64, :] = comb[:, pl.ds(chunk("y", k, 256), 256)]
        for n in range(5):
            out[64 + 32 * n : 96 + 32 * n, :] = embed[:, 256 * n : 256 * n + 256]


def input_blocks(comb, embed):
    return pl.pallas_call(
        inputs_kernel,
        out_shape=[shape((224, 256), BF16)] * 4,
        cost_estimate=pl.CostEstimate(flops=0, bytes_accessed=700_000, transcendentals=0),
        compiler_params=SMALL,
        name="input_blocks",
    )(comb, embed)


def embed_grad_kernel(tok, partial_logits, comb, row_dot, out, patches, sems):
    wait = start_patches(tok, patches, sems)
    value = 0.0
    for i in range(2):
        half = slice(32 * i, 32 * i + 32)
        grad = partial_logits[half, :] - comb[half, :].astype(F32) * row_dot[i]
        grad = grad.astype(BF16)
        for n in range(4):
            wait(i, n)
            span = slice(256 * n, 256 * n + 256)
            value = value + jnp.dot(
                grad[:, span], patches[i, span, :], preferred_element_type=F32
            )
    out[...] = value.astype(BF16)


def embed_grad(tokens, partial_logits, comb, row_dot):
    return pl.pallas_call(
        embed_grad_kernel,
        in_specs=[pl.BlockSpec(memory_space=pl.ANY)]
        + [pl.BlockSpec(memory_space=pltpu.VMEM)] * 3,
        out_shape=shape((32, 1280), BF16),
        scratch_shapes=[pltpu.VMEM((2, 1024, 1280), BF16), pltpu.SemaphoreType.DMA((8,))],
        cost_estimate=pl.CostEstimate(flops=170_000_000, bytes_accessed=6_000_000, transcendentals=0),
        compiler_params=MEDIUM,
        name="embed_grad",
    )(in_hbm(tokens), partial_logits, comb, row_dot)


def rows_kernel(*refs):
    parts, inputs = refs[:4], refs[4:8]
    row_dot, mine, other, scratch = refs[8:]
    core = lax.axis_index("core")
    embeds = [
        jnp.concatenate([one[64 + 32 * n : 96 + 32 * n, :] for n in range(5)], axis=1)
        for one in inputs
    ]
    for i in range(2):
        half = slice(32 * i, 32 * i + 32)
        dots = row_dot[i, :, pl.ds(chunk("y", 0, 256), 256)]
        weights = [one[half, 1536:] for one in parts] + [
            (p[half, 1280:1536].astype(F32) - c[half, :].astype(F32) * dots).astype(BF16)
            for p, c in zip(parts, inputs)
        ]
        rows = [one[half, :1280] for one in parts] + embeds
        scratch[i] = lax.dot_general(
            jnp.concatenate(weights), jnp.concatenate(rows), TN, preferred_element_type=F32
        )
        for k in range(4):
            base = ((lax.axis_index("x") + k) & 3) * 64
            here = pl.multiple_of(base + core * 32, 32)
            there = pl.multiple_of(base + (1 - core) * 32, 32)
            mine[k, i] = scratch[i, pl.ds(here, 32), :].astype(BF16)
            other[k, i] = scratch[i, pl.ds(there, 32), :].astype(BF16)


def patch_rows(parts, inputs, row_dot):
    return pl.pallas_call(
        rows_kernel,
        out_shape=[shape((4, 2, 32, 1280), BF16)] * 2,
        scratch_shapes=[pltpu.VMEM((2, 256, 1280), F32)],
        cost_estimate=pl.CostEstimate(flops=335_000_000, bytes_accessed=3_000_000, transcendentals=0),
        compiler_params=MEDIUM,
        name="patch_rows",
    )(*parts, *inputs, row_dot)


def add_kernel(mine, other, o0, o1, o2, o3):
    for k, out in enumerate((o0, o1, o2, o3)):
        out[...] = add(mine[k], other[k])


def add_cores(mine, other):
    return pl.pallas_call(
        add_kernel,
        out_shape=[pltpu.VMEM((2, 32, 1280), BF16)] + [pltpu.HBM((2, 32, 1280), BF16)] * 3,
        cost_estimate=pl.CostEstimate(flops=327_680, bytes_accessed=2_000_000, transcendentals=0),
        compiler_params=SMALL,
        name="add_cores",
    )(mine, other)


def after(value, *others):
    return lax.optimization_barrier((value, *others))[0]


def sources(terms):
    return [terms[0], terms[3], terms[2], terms[1]]


def local(tokens, slot_embed, combine, w_in, w_out, grad_out):
    w_in, w_out = w_in[0], w_out[0]
    embed = slot_embed.T
    comb = jnp.transpose(combine, (0, 2, 1)).reshape(64, 1024)

    logits, part = local_softmax(tokens, embed)
    comb_late = after(comb, part)
    out_part = jnp.einsum(
        "ijt,itd->ijd", comb_late.reshape(2, 32, 1024), grad_out, preferred_element_type=F32
    )
    out_part = out_part.astype(BF16).reshape(64, 1280)
    part_other = near(part)
    part, out_part = lax.optimization_barrier((part, out_part))
    out_other = far(out_part)
    part = merge_pair(part, part_other)
    out_part = add(after(out_part, part), out_other)
    out_other = near(out_part)
    slot_in, lse = merge_last(part, far(part))
    inputs = list(input_blocks(after(comb_late, out_part), embed))

    pre_act = jnp.dot(slot_in, w_in, preferred_element_type=F32)
    act, slope = gelu_parts(pre_act)
    act = act.astype(BF16)
    out_sum = jnp.dot(act, w_out, preferred_element_type=F32).astype(BF16)
    grad_slot_out = add(after(out_part, out_sum), out_other)
    inputs[3] = after(inputs[3], out_sum)
    inputs = sources(scatter_terms(inputs, "y"))
    out_sum = add(out_sum, near(out_sum))
    out_sum = after(out_sum, *inputs)
    sum_other = far(out_sum)
    grad_act = jnp.einsum("sd,hd->sh", grad_slot_out, w_out, preferred_element_type=F32)
    grad_pre = (grad_act * slope).astype(BF16)
    in_sum = jnp.einsum("sh,dh->sd", grad_pre, w_in, preferred_element_type=F32).astype(BF16)
    in_sum, act_late, slots_late = lax.optimization_barrier(
        (in_sum, act, grad_slot_out, out_sum)
    )[:3]
    in_other = near(in_sum)
    grad_w_out = jnp.einsum("sh,sd->hd", act_late, slots_late, preferred_element_type=F32)
    grad_w_out = grad_w_out.astype(BF16)
    in_sum = add(after(in_sum, grad_w_out), in_other)
    in_other = far(in_sum)

    grad_combine, row_dot = combine_grad(grad_out, out_sum, sum_other, comb)
    grad_slot_in = add(after(in_sum, row_dot), in_other)
    row_dot = row_dot + swap_cores(row_dot)
    late, row_dot = lax.optimization_barrier((grad_slot_in, row_dot))
    row_dot = row_dot + near(row_dot, "x")
    row_dot = row_dot + far(row_dot, "x")
    row_dot = row_dot + near(row_dot, "y")
    row_dot = row_dot + far(row_dot, "y")

    partial_logits, *parts = dispatch_grad(
        tokens, late, slot_in, logits, lse, comb, grad_combine
    )
    parts = sources(scatter_terms(parts, "y"))

    mine, other = patch_rows(parts, inputs, row_dot)
    other_core = swap_cores(other)

    partial_logits, mine = lax.optimization_barrier((partial_logits, mine))
    embed_part = embed_grad(tokens, partial_logits, comb, row_dot)
    sums = add_cores(after(mine, embed_part), other_core)
    embed_part = after(embed_part, sums[0])
    embed_other = near(embed_part)
    terms = scatter_terms(sums, "x")
    grad_tokens = sum(term.astype(F32) for term in terms).astype(BF16)
    embed_part = add(embed_part, embed_other)
    embed_sum = add(embed_part, far(embed_part))
    z = lax.axis_index("seq")
    grad_embed = lax.dynamic_slice_in_dim(embed_sum, z * 320, 320, axis=1).T
    slot_late = after(slot_in, embed_part)
    grad_w_in = jnp.einsum("sd,sh->dh", slot_late, grad_pre, preferred_element_type=F32)
    grad_w_in = grad_w_in.astype(BF16)

    return (
        grad_tokens,
        grad_embed,
        grad_w_in[None],
        grad_w_out[None],
    )


def solution(mesh):
    fine = Mesh(mesh.devices.reshape(4, 4, 4, 2), ("seq", "y", "x", "core"))
    expert = ("y", "x", "core")
    return jax.shard_map(
        local,
        mesh=fine,
        in_specs=(
            P(None, "seq", None),
            P(None, expert),
            P(None, "seq", expert),
            P(expert, None, "seq"),
            P(expert, "seq", None),
            P(None, "seq", None),
        ),
        out_specs=(
            P(None, ("seq", *expert), None),
            P("seq", expert),
            P(expert, None, "seq"),
            P(expert, "seq", None),
        ),
        check_vma=False,
    )
```
